256 devices in a mesh: batch: 2 (over y_lo), tm: 64 (over z, x, y_hi), mp: 2 (over core).
Axes of the slice: x: 4, y: 4 (y_hi: 2, y_lo: 2; y = y_hi * 2 + y_lo), z: 8, core: 2. Of those that a mesh axis runs over, the one named last changes fastest.
Arguments:
- input_signal: bfloat16 [2, 8192, 1536], P('batch', 'tm'), may hold values from -6 to 6
- standardize_factor: float32 [1536], replicated, may hold values from 0.1 to 1.9
- triple_projection: bfloat16 [3, 1536, 768], P(None, None, 'mp'), may hold values from -0.15625 to 0.15625
- score_sharpening: float32 [8], P('mp'), may hold values from 1 to 3.5
- final_projection: bfloat16 [768, 1536], P('mp'), may hold values from -0.21875 to 0.21875
- filter_taps: float32 [31, 1536], replicated, may hold values from -1.2 to 1.2
- mixture_adjoint: bfloat16 [2, 8192, 1536], P('batch', 'tm'), may hold values from -16 to 16
Outputs:
- sublayer_result: bfloat16 [2, 8192, 1536], P('batch', 'tm')
- signal_adjoint: bfloat16 [2, 8192, 1536], P('batch', 'tm')
- filter_adjoint: float32 [31, 1536], P(None, ('batch', 'tm'))
- amplifier_adjoint: float32 [1536], P(('batch', 'tm'))
The draws below stay inside these ranges and needn't reach their ends.
All inputs are finite; a program needn't handle non-finite values.
Results may differ from the reference program's by a relative error of at most 0.015.
Values may be sent and summed in bfloat16 or wider, within the bound.
No kernel may reach another device: no remote copies, remote signals or barrier semaphores. Data moves between devices by JAX's collectives and lax.ppermute only.
A program may use at most 128 MiB of HBM per device.

```python
import math
import jax
import jax.numpy as jnp
from jax import lax

D = 1536
FOCUS_CHANNELS = 8
HEAD_SIZE = 96
KERNEL = 31
SEQ = 8192
UTTERANCES = 2


def with_spikes(entries, stream_key, source, target, parts, factor):
    def block_of(dim):
        return (jnp.arange(entries.shape[dim]) // (entries.shape[dim] // parts)).reshape((-1,) + (1,) * (entries.ndim - 1 - dim))

    first = jax.random.permutation(stream_key, parts)[block_of(target)]
    second = (block_of(target) + parts // 2) % parts
    return jnp.where((block_of(source) == first) | (block_of(source) == second), factor * entries, entries)


def steps_of(stream_key, shape, split, smallest, top_value):
    gain = 1.0
    for axis_at, blocks in split:
        heights = jax.random.uniform(jax.random.fold_in(jax.random.fold_in(stream_key, 6), axis_at), (blocks,), jnp.float32, smallest / len(split), top_value / len(split))
        gain = gain * jnp.repeat(jnp.exp(heights), shape[axis_at] // blocks).reshape((-1,) + (1,) * (len(shape) - 1 - axis_at))
    return gain


def gaussian(key, shape, width, bound, shards=(), kind=jnp.bfloat16):
    entries = jax.random.normal(key, shape, jnp.float32) * width
    if len(shards) > 0:
        entries = steps_of(key, shape, shards, -0.22, 0.18) * entries
    return jnp.clip(entries, min=-bound, max=bound).astype(kind)


def noise_with(stream_key, shape, spread, bound, cuts, heavy, dtype=jnp.bfloat16):
    array = spread * jax.random.normal(stream_key, shape, jnp.float32)
    if cuts:
        array = array * steps_of(stream_key, shape, cuts, -0.22, 0.18)
    return jnp.clip(with_spikes(array, jax.random.fold_in(stream_key, 3), *heavy), -bound, bound).astype(dtype)


def setup_inputs(seed: int = 0) -> dict:
    splits = jax.random.split(jax.random.key(seed), 8)
    return {
        "input_signal": gaussian(splits[0], (UTTERANCES, SEQ, D), 1.0, 6.0, ((0, 2), (1, 64))),
        "standardize_factor": jnp.clip(1.0 + 0.18 * jax.random.normal(splits[1], (D,), jnp.float32), 0.1, 1.9),
        "triple_projection": gaussian(splits[2], (3, D, FOCUS_CHANNELS * HEAD_SIZE), D ** -0.5, 0.15625, ((2, 2),)),
        "score_sharpening": jnp.clip(jnp.exp(math.log(3.5) - 1.25276297 * jax.random.uniform(splits[3], (FOCUS_CHANNELS,), jnp.float32) ** steps_of(splits[3], (FOCUS_CHANNELS,), ((0, 2),), -0.2, 0.2)), 1.0, 3.5),
        "final_projection": gaussian(splits[4], (FOCUS_CHANNELS * HEAD_SIZE, D), (FOCUS_CHANNELS * HEAD_SIZE) ** -0.5, 0.21875, ((0, 2),)),
        "filter_taps": gaussian(splits[5], (KERNEL, D), 0.2, 1.2, (), jnp.float32),
        "mixture_adjoint": noise_with(splits[6], (UTTERANCES, SEQ, D), 1.0, 16.0, ((0, 2), (1, 64)), (1, 2, 64, 4.0)),
    }


def unit_rows(values_in):
    radius = jnp.sqrt(lax.optimization_barrier(jnp.mean(values_in * values_in, axis=-1, keepdims=True)) + 1e-06)
    return (values_in / radius, radius)

def rounded(values_in):
    return lax.optimization_barrier(values_in.astype(jnp.bfloat16)).astype(jnp.float32)

def solo_recording(signal_pieces, standardize_factor, triple_projection, score_sharpening, final_projection, filter_taps, adjoint_slices):
    reach = KERNEL // 2
    inputs = signal_pieces.astype(jnp.float32)
    centred = inputs - lax.optimization_barrier(jnp.mean(inputs, axis=-1, keepdims=True))
    variance = lax.optimization_barrier(jnp.mean(centred * centred, axis=-1, keepdims=True))
    inverse_std = 1.0 / jnp.sqrt(variance + 1e-05)
    incoming_entries = centred * inverse_std
    normed = (incoming_entries * standardize_factor).astype(jnp.bfloat16)
    query = jnp.dot(normed, triple_projection[0], preferred_element_type=jnp.float32).reshape(SEQ, FOCUS_CHANNELS, HEAD_SIZE)
    key_raw = jnp.dot(normed, triple_projection[1], preferred_element_type=jnp.float32).reshape(SEQ, FOCUS_CHANNELS, HEAD_SIZE)
    value_raw = jnp.dot(normed, triple_projection[2], preferred_element_type=jnp.float32).reshape(SEQ, FOCUS_CHANNELS, HEAD_SIZE)
    normalized_probes, q_radius = unit_rows(query)
    khat, k_radius = unit_rows(key_raw)
    head_sharpening = (score_sharpening / math.sqrt(HEAD_SIZE))[None, :, None]
    probe_vectors = (normalized_probes * head_sharpening).astype(jnp.bfloat16)
    keys_f = khat.astype(jnp.bfloat16).astype(jnp.float32)
    values_f = value_raw.astype(jnp.bfloat16).astype(jnp.float32)
    queries_f = probe_vectors.astype(jnp.float32)
    incoming_adjoint = adjoint_slices.astype(jnp.float32)
    grad_pad = jnp.pad(incoming_adjoint, ((reach, reach), (0, 0)))
    grad_res = incoming_adjoint
    for tap_index in range(KERNEL):
        grad_res = grad_res + filter_taps[tap_index] * grad_pad[2 * reach - tap_index:2 * reach - tap_index + SEQ]
    grad_heads = jnp.dot(grad_res.astype(jnp.bfloat16), final_projection.T, preferred_element_type=jnp.float32)
    grad_heads = grad_heads.astype(jnp.bfloat16).reshape(SEQ, FOCUS_CHANNELS, HEAD_SIZE)
    grad_heads_f = grad_heads.astype(jnp.float32)
    block_rows = math.gcd(SEQ, 512)
    block_count = SEQ // block_rows

    def query_block(pieces):
        query_part, grad_part = pieces
        score = jnp.einsum('qhe,khe->qhk', query_part, keys_f)
        weight = jnp.exp(score)
        total = lax.optimization_barrier(jnp.sum(weight, axis=-1))
        weight_low = rounded(weight)
        numer = jnp.einsum('qhk,khe->qhe', weight_low, values_f)
        product = jnp.einsum('qhe,khe->qhk', grad_part, values_f)
        weighted = weight * product
        expect = lax.optimization_barrier(jnp.sum(weighted, axis=-1))
        first = jnp.einsum('qhk,khe->qhe', rounded(weighted), keys_f)
        second = jnp.einsum('qhk,khe->qhe', weight_low, keys_f)
        attended = (numer / total[..., None]).astype(jnp.bfloat16)
        delta = expect / total
        probe_sensitivity = (first - delta[..., None] * second) / total[..., None]
        return (attended, total, delta, probe_sensitivity)
    attended, totals, deltas, probe_sensitivity = lax.map(query_block, (queries_f.reshape(block_count, block_rows, FOCUS_CHANNELS, HEAD_SIZE), grad_heads_f.reshape(block_count, block_rows, FOCUS_CHANNELS, HEAD_SIZE)))
    attended = attended.reshape(SEQ, FOCUS_CHANNELS * HEAD_SIZE)
    totals = totals.reshape(SEQ, FOCUS_CHANNELS)
    deltas = deltas.reshape(SEQ, FOCUS_CHANNELS)
    probe_sensitivity = probe_sensitivity.reshape(SEQ, FOCUS_CHANNELS, HEAD_SIZE)
    residual = (inputs + jnp.dot(attended, final_projection, preferred_element_type=jnp.float32)).astype(jnp.bfloat16)
    res_pad = jnp.pad(residual.astype(jnp.float32), ((reach, reach), (0, 0)))
    sublayer_result = residual.astype(jnp.float32)
    filter_terms = []
    for tap_index in range(KERNEL):
        receptive_span = res_pad[tap_index:tap_index + SEQ]
        sublayer_result = sublayer_result + filter_taps[tap_index] * receptive_span
        filter_terms.append(lax.optimization_barrier(jnp.sum(incoming_adjoint * receptive_span, axis=0)))
    sublayer_result = sublayer_result.astype(jnp.bfloat16)
    filter_terms = jnp.stack(filter_terms)
    totals_t = totals.T[None]
    deltas_t = deltas.T[None]

    def key_block(pieces):
        key_part, value_part = pieces
        score = jnp.einsum('khe,qhe->khq', key_part, queries_f)
        prob = jnp.exp(score) / totals_t
        grad_v = jnp.einsum('khq,qhe->khe', rounded(prob), grad_heads_f)
        product = jnp.einsum('khe,qhe->khq', value_part, grad_heads_f)
        slope = prob * (product - deltas_t)
        grad_k = jnp.einsum('khq,qhe->khe', rounded(slope), queries_f)
        return (grad_k, grad_v)
    grad_keys, grad_values = lax.map(key_block, (keys_f.reshape(block_count, block_rows, FOCUS_CHANNELS, HEAD_SIZE), values_f.reshape(block_count, block_rows, FOCUS_CHANNELS, HEAD_SIZE)))
    grad_keys = grad_keys.reshape(SEQ, FOCUS_CHANNELS, HEAD_SIZE)
    grad_values = grad_values.reshape(SEQ, FOCUS_CHANNELS, HEAD_SIZE)
    sharpened_sensitivity = probe_sensitivity * head_sharpening
    query_grad = (sharpened_sensitivity - normalized_probes * lax.optimization_barrier(jnp.mean(sharpened_sensitivity * normalized_probes, axis=-1, keepdims=True))) / q_radius
    key_grad = (grad_keys - khat * lax.optimization_barrier(jnp.mean(grad_keys * khat, axis=-1, keepdims=True))) / k_radius
    standardized_adjoint = jnp.dot(query_grad.astype(jnp.bfloat16).reshape(SEQ, FOCUS_CHANNELS * HEAD_SIZE), triple_projection[0].T, preferred_element_type=jnp.float32)
    standardized_adjoint = standardized_adjoint + jnp.dot(key_grad.astype(jnp.bfloat16).reshape(SEQ, FOCUS_CHANNELS * HEAD_SIZE), triple_projection[1].T, preferred_element_type=jnp.float32)
    standardized_adjoint = standardized_adjoint + jnp.dot(grad_values.astype(jnp.bfloat16).reshape(SEQ, FOCUS_CHANNELS * HEAD_SIZE), triple_projection[2].T, preferred_element_type=jnp.float32)
    amplifier_terms = lax.optimization_barrier(jnp.sum(standardized_adjoint * incoming_entries, axis=0))
    scaled = standardized_adjoint * standardize_factor
    frame_back = (scaled - lax.optimization_barrier(jnp.mean(scaled, axis=-1, keepdims=True)) - incoming_entries * lax.optimization_barrier(jnp.mean(scaled * incoming_entries, axis=-1, keepdims=True))) * inverse_std
    signal_adjoint = (grad_res + frame_back).astype(jnp.bfloat16)
    return (sublayer_result, signal_adjoint, filter_terms, amplifier_terms)

def reference(input_signal, standardize_factor, triple_projection, score_sharpening, final_projection, filter_taps, mixture_adjoint):
    mixed_list = []
    grad_list = []
    filter_adjoint = jnp.zeros((KERNEL, D), jnp.float32)
    amplifier_adjoint = jnp.zeros((D,), jnp.float32)
    for recording_number in range(UTTERANCES):
        sublayer_result, signal_adjoint, filter_terms, amplifier_terms = solo_recording(input_signal[recording_number], standardize_factor, triple_projection, score_sharpening, final_projection, filter_taps, mixture_adjoint[recording_number])
        mixed_list.append(sublayer_result)
        grad_list.append(signal_adjoint)
        filter_adjoint = filter_adjoint + filter_terms
        amplifier_adjoint = amplifier_adjoint + amplifier_terms
    return (jnp.stack(mixed_list), jnp.stack(grad_list), filter_adjoint, amplifier_adjoint)
```

```python
import functools
import math

import jax
import jax.numpy as jnp
from jax import lax
from jax.experimental import pallas as pl
from jax.experimental.pallas import tpu as pltpu
from jax.sharding import PartitionSpec as P

INTERPRET = False
TM = 64
F32 = jnp.float32
BF16 = jnp.bfloat16


def _split(t):
    return t // 16, (t // 8) % 2, (t // 2) % 4, t % 2


def _join(z4, z2, x, yh):
    return ((z4 % 4) * 2 + z2) * 8 + (x % 4) * 2 + yh


def move_z4(a, s):
    pairs = []
    for t in range(TM):
        z4, z2, x, yh = _split(t)
        pairs.append((t, _join(z4 + s, z2, x, yh)))
    return lax.ppermute(a, "tm", pairs)


def move_x(a, s):
    pairs = []
    for t in range(TM):
        z4, z2, x, yh = _split(t)
        pairs.append((t, _join(z4, z2, x + s, yh)))
    return lax.ppermute(a, "tm", pairs)


def move_zy(a, m):
    pairs = []
    for t in range(TM):
        z4, z2, x, yh = _split(t)
        pairs.append((t, _join(z4, z2 ^ (m & 1), x, yh ^ (m >> 1))))
    return lax.ppermute(a, "tm", pairs)


def vcall(kernel, out_shape, scratch=(), smem=0, n_in=0):
    space = [pl.BlockSpec(memory_space=pltpu.SMEM)] * smem
    space += [pl.BlockSpec(memory_space=pltpu.VMEM)] * n_in
    return pl.pallas_call(
        kernel,
        out_shape=out_shape,
        in_specs=space,
        out_specs=jax.tree.map(lambda _: pl.BlockSpec(memory_space=pltpu.VMEM), out_shape),
        scratch_shapes=list(scratch),
        interpret=INTERPRET,
    )


def dotf(a, b, ca=1, cb=0):
    return lax.dot_general(a, b, (((ca,), (cb,)), ((), ())), preferred_element_type=F32)


def front_kernel(sharp, x, factor, w, pay, qhat_o, khat_o, rad_o, *, heads, hs):
    xf = x[...].astype(F32)
    centred = xf - jnp.mean(xf, axis=-1, keepdims=True)
    var = jnp.mean(centred * centred, axis=-1, keepdims=True)
    unit = centred * (1.0 / jnp.sqrt(var + 1e-05))
    normed = (unit * factor[...]).astype(BF16)
    qt = dotf(normed, w[0]).T
    kt = dotf(normed, w[1]).T
    vt = dotf(normed, w[2]).T
    for h in range(heads):
        q = qt[h * hs : (h + 1) * hs]
        k = kt[h * hs : (h + 1) * hs]
        v = vt[h * hs : (h + 1) * hs]
        qr = jnp.sqrt(jnp.mean(q * q, axis=0, keepdims=True) + 1e-06)
        kr = jnp.sqrt(jnp.mean(k * k, axis=0, keepdims=True) + 1e-06)
        qh = q / qr
        kh = k / kr
        qhat_o[h * hs : (h + 1) * hs] = qh
        khat_o[h * hs : (h + 1) * hs] = kh
        rad_o[h : h + 1] = qr
        rad_o[heads + h : heads + h + 1] = kr
        pay[h, 0:hs] = kh.astype(BF16)
        pay[h, hs : 2 * hs] = v.astype(BF16)
        pay[h, 2 * hs : 3 * hs] = (qh * (sharp[h] / math.sqrt(hs))).astype(BF16)


def send_kernel(idx, pay, gres, wf, o0, o1, o2, o3, g_s, *, hs):
    gt = dotf(wf[...], gres[...], 1, 1).astype(BF16)
    for h in range(4):
        g_s[h] = gt[h * hs : (h + 1) * hs]
    for s, o in enumerate((o0, o1, o2, o3)):
        at = lax.rem(idx[0] + s, 4)
        o[0 : 3 * hs] = pay[at]
        o[3 * hs : 4 * hs] = g_s[at]


KB = 256


def to_rows(a):
    return a.astype(F32).T.astype(BF16)


def totals_kernel(*refs, hs):
    kv = refs[0:4]
    qg = refs[4:8]
    out = refs[8]
    kn, vn, qgs = refs[9:]
    span = kv[0].shape[1]
    for r in range(4):
        kn[r * span : (r + 1) * span] = to_rows(kv[r][0:hs])
        vn[r * span : (r + 1) * span] = to_rows(kv[r][hs : 2 * hs])
        qgs[r] = qg[r][...]
    blocks = 4 * span // KB

    def over_q(j, _):
        qt = qgs[j, 0:hs]
        gt = qgs[j, hs : 2 * hs]

        def over_k(b, state):
            tot, exp = state
            at = pl.multiple_of(b * KB, KB)
            w = jnp.exp(dotf(kn[pl.ds(at, KB)], qt))
            p = dotf(vn[pl.ds(at, KB)], gt)
            tot = tot + jnp.sum(w.reshape(KB // 8, 8, span), axis=0)
            exp = exp + jnp.sum((w * p).reshape(KB // 8, 8, span), axis=0)
            return tot, exp

        zero = jnp.zeros((8, span), F32)
        tot, exp = lax.fori_loop(0, blocks, over_k, (zero, zero))
        out[j, 0:1] = jnp.sum(tot, axis=0, keepdims=True)
        out[j, 1:2] = jnp.sum(exp, axis=0, keepdims=True)
        return 0

    lax.fori_loop(0, 4, over_q, 0)


def grads_kernel(*refs, hs):
    te = refs[0:4]
    kv = refs[4:8]
    qg = refs[8:12]
    rows = refs[12:16]
    cols = refs[16:20]
    kn, vn, kvs, qgs, qn, gn, acc, inv, dlt, colacc = refs[20:]
    span = kv[0].shape[1]
    per = span // KB
    for r in range(4):
        kn[r * span : (r + 1) * span] = to_rows(kv[r][0:hs])
        vn[r * span : (r + 1) * span] = to_rows(kv[r][hs : 2 * hs])
        for c in range(per):
            kvs[r * per + c] = kv[r][:, c * KB : (c + 1) * KB]
        qgs[r] = qg[r][...]
        qn[r] = to_rows(qg[r][0:hs])
        gn[r] = to_rows(qg[r][hs : 2 * hs])
        t = te[0][r] + te[1][r ^ 1] + (te[2][r ^ 2] + te[3][r ^ 3])
        one = 1.0 / t[0:1]
        inv[r] = one
        dlt[r] = t[1:2] * one
    acc[...] = jnp.zeros(acc.shape, F32)

    def over_k(b, _):
        at = pl.multiple_of(b * KB, KB)
        k = kn[pl.ds(at, KB)]
        v = vn[pl.ds(at, KB)]
        kt = kvs[b, 0:hs]
        vt = kvs[b, hs : 2 * hs]

        def over_q(j, state):
            gk, gv = state
            prob = jnp.exp(dotf(k, qgs[j, 0:hs])) * inv[j]
            slope = prob * (dotf(v, qgs[j, hs : 2 * hs]) - dlt[j])
            pb = prob.astype(BF16)
            sb = slope.astype(BF16)
            acc[j, 0:hs] += dotf(vt, pb)
            acc[j, hs : 2 * hs] += dotf(kt, sb)
            return gk + dotf(sb, qn[j]), gv + dotf(pb, gn[j])

        zero = jnp.zeros((KB, hs), F32)
        gk, gv = lax.fori_loop(0, 4, over_q, (zero, zero))
        colacc[b, 0:hs] = gk.T.astype(BF16)
        colacc[b, hs : 2 * hs] = gv.T.astype(BF16)
        return 0

    lax.fori_loop(0, 4 * per, over_k, 0)
    for r in range(4):
        rows[r][...] = acc[r].astype(BF16)
        for c in range(per):
            cols[r][:, c * KB : (c + 1) * KB] = colacc[r * per + c]


def sum_kernel(*refs, hs):
    row = refs[0][...].astype(F32)
    col = refs[4][...].astype(F32)
    for i in range(1, 4):
        row = row + refs[i][...].astype(F32)
        col = col + refs[4 + i][...].astype(F32)
    row = row.astype(BF16)
    col = col.astype(BF16)
    lanes = row.shape[1] // 4
    for s in range(4):
        refs[8 + s][0 : 2 * hs] = row[:, s * lanes : (s + 1) * lanes]
        refs[8 + s][2 * hs : 4 * hs] = col[:, s * lanes : (s + 1) * lanes]


def back_kernel(idx, sharp, b0, b1, b2, b3, qhat, khat, rad, wf, w, out, home, att, qgr, kgr, vgr, *, heads, hs):
    for s, b in enumerate((b0, b1, b2, b3)):
        home[lax.rem(idx[0] + s, 4)] = b[...]
    lanes = b0.shape[1]
    for h in range(heads):
        lo, hi = h * hs, (h + 1) * hs
        att[lo:hi] = home[h, 0:hs].astype(F32)
        gq = home[h, hs : 2 * hs].astype(F32) * (sharp[h] / math.sqrt(hs))
        gk = home[h, 2 * hs : 3 * hs].astype(F32)
        vgr[lo:hi] = home[h, 3 * hs : 4 * hs].astype(F32)
        qh = qhat[lo:hi]
        kh = khat[lo:hi]
        qgr[lo:hi] = (gq - qh * jnp.mean(gq * qh, axis=0, keepdims=True)) / rad[h : h + 1]
        kgr[lo:hi] = (gk - kh * jnp.mean(gk * kh, axis=0, keepdims=True)) / rad[heads + h : heads + h + 1]
    out[0:lanes] = dotf(att[...].T.astype(BF16), wf[...]).astype(BF16)
    normed = dotf(qgr[...].T.astype(BF16), w[0], 1, 1)
    normed = normed + dotf(kgr[...].T.astype(BF16), w[1], 1, 1)
    normed = normed + dotf(vgr[...].T.astype(BF16), w[2], 1, 1)
    out[lanes : 2 * lanes] = normed.astype(BF16)


def rims(cells, width):
    count = TM
    ends = count - 1
    head = cells[:width]
    tail = cells[cells.shape[0] - width :]
    return jnp.concatenate(
        [
            lax.ppermute(tail, "tm", [(i, i + 1) for i in range(ends)]),
            cells,
            lax.ppermute(head, "tm", [(i + 1, i) for i in range(ends)]),
        ],
        axis=0,
    )


def pieces(a, n):
    width = a.shape[1] // n
    return lambda i: lax.dynamic_slice_in_dim(a, i * width, width, axis=1)


def scatter_sum(a, batches):
    t = lax.axis_index("tm")
    z4, z2, x, yh = t // 16, (t // 8) % 2, (t // 2) % 4, t % 2
    if batches > 1:
        b = lax.axis_index("batch")
        at = pieces(a, 2)
        a = at(b) + lax.ppermute(at(1 - b), "batch", [(0, 1), (1, 0)])
    at = pieces(a, 4)
    got = [move_z4(at((z4 + s) % 4), s) for s in (1, 2, 3)]
    a = (at(z4) + got[0]) + (got[1] + got[2])
    at = pieces(a, 2)
    a = at(z2) + move_zy(at(1 - z2), 1)
    at = pieces(a, 4)
    got = [move_x(at((x + s) % 4), s) for s in (1, 2, 3)]
    a = (at(x) + got[0]) + (got[1] + got[2])
    at = pieces(a, 2)
    return at(yh) + move_zy(at(1 - yh), 2)


def local(input_signal, standardize_factor, triple_projection, score_sharpening, final_projection, filter_taps, mixture_adjoint, *, batches, mps):
    rows, width = input_signal.shape[1:]
    heads = score_sharpening.shape[0]
    hs = triple_projection.shape[2] // heads
    flat = heads * hs
    taps = filter_taps.shape[0]
    reach = taps // 2
    t = lax.axis_index("tm")
    z4 = (t // 16).astype(jnp.int32).reshape(1)
    x_in = input_signal[0]
    adj = mixture_adjoint[0]
    shape = jax.ShapeDtypeStruct
    grad_pad = rims(adj, reach).astype(F32)

    pay, qhat, khat, rad = vcall(
        functools.partial(front_kernel, heads=heads, hs=hs),
        (shape((heads, 3 * hs, rows), BF16), shape((flat, rows), F32), shape((flat, rows), F32), shape((2 * heads, rows), F32)),
        smem=1,
        n_in=3,
    )(score_sharpening, x_in, standardize_factor[None], triple_projection)

    incoming_adjoint = adj.astype(F32)
    grad_res = incoming_adjoint
    for j in range(taps):
        grad_res = grad_res + filter_taps[j] * grad_pad[2 * reach - j : 2 * reach - j + rows]

    sent = vcall(
        functools.partial(send_kernel, hs=hs),
        tuple(shape((4 * hs, rows), BF16) for _ in range(4)),
        scratch=[pltpu.VMEM((4, hs, rows), BF16)],
        smem=1,
        n_in=3,
    )(z4, pay, grad_res.astype(BF16), final_projection)
    got = [sent[0]] + [move_z4(sent[s], s) for s in (1, 2, 3)]
    kv0 = jnp.concatenate([g[: 2 * hs] for g in got], axis=1)
    qg0 = jnp.concatenate([g[2 * hs :] for g in got], axis=1)
    kv = [kv0] + [move_x(kv0, s) for s in (1, 2, 3)]
    qg = [qg0] + [move_zy(qg0, m) for m in (1, 2, 3)]
    span = 4 * rows
    te0 = vcall(
        functools.partial(totals_kernel, hs=hs),
        shape((4, 2, span), F32),
        scratch=[pltpu.VMEM((4 * span, hs), BF16), pltpu.VMEM((4 * span, hs), BF16), pltpu.VMEM((4, 2 * hs, span), BF16)],
        n_in=8,
    )(*kv, *qg)
    te = [te0] + [move_zy(te0, m) for m in (1, 2, 3)]
    per = span // KB
    res = vcall(
        functools.partial(grads_kernel, hs=hs),
        tuple(shape((2 * hs, span), BF16) for _ in range(8)),
        scratch=[
            pltpu.VMEM((4 * span, hs), BF16),
            pltpu.VMEM((4 * span, hs), BF16),
            pltpu.VMEM((4 * per, 2 * hs, KB), BF16),
            pltpu.VMEM((4, 2 * hs, span), BF16),
            pltpu.VMEM((4, span, hs), BF16),
            pltpu.VMEM((4, span, hs), BF16),
            pltpu.VMEM((4, 2 * hs, span), F32),
            pltpu.VMEM((4, 1, span), F32),
            pltpu.VMEM((4, 1, span), F32),
            pltpu.VMEM((4 * per, 2 * hs, KB), BF16),
        ],
        n_in=12,
    )(*te, *kv, *qg)
    row = [res[0]] + [move_zy(res[m], m) for m in (1, 2, 3)]
    col = [res[4]] + [move_x(res[4 + s], -s) for s in (1, 2, 3)]
    home = vcall(
        functools.partial(sum_kernel, hs=hs),
        tuple(shape((4 * hs, rows), BF16) for _ in range(4)),
        n_in=8,
    )(*row, *col)
    back = [home[0]] + [move_z4(home[s], -s) for s in (1, 2, 3)]
    part = vcall(
        functools.partial(back_kernel, heads=heads, hs=hs),
        shape((2 * rows, width), BF16),
        scratch=[pltpu.VMEM((4, 4 * hs, rows), BF16)] + [pltpu.VMEM((flat, rows), F32)] * 4,
        smem=2,
        n_in=9,
    )(z4, score_sharpening, *back, qhat, khat, rad, final_projection, triple_projection)
    if mps > 1:
        other = lax.ppermute(part, "mp", [(0, 1), (1, 0)])
        total = part.astype(F32) + other.astype(F32)
    else:
        total = part.astype(F32)

    inputs = x_in.astype(F32)
    residual = (inputs + total[:rows]).astype(BF16)
    res_pad = rims(residual, reach).astype(F32)
    centred = inputs - jnp.mean(inputs, axis=-1, keepdims=True)
    variance = jnp.mean(centred * centred, axis=-1, keepdims=True)
    inverse_std = 1.0 / jnp.sqrt(variance + 1e-05)
    unit = centred * inverse_std
    normed_grad = total[rows:]
    amplifier_terms = jnp.sum(normed_grad * unit, axis=0)
    scaled = normed_grad * standardize_factor
    frame_back = (
        scaled - jnp.mean(scaled, axis=-1, keepdims=True) - unit * jnp.mean(scaled * unit, axis=-1, keepdims=True)
    ) * inverse_std
    signal_adjoint = (grad_res + frame_back).astype(BF16)

    sublayer_result = residual.astype(F32)
    terms = []
    for j in range(taps):
        span_j = res_pad[j : j + rows]
        sublayer_result = sublayer_result + filter_taps[j] * span_j
        terms.append(jnp.sum(incoming_adjoint * span_j, axis=0))
    terms.append(amplifier_terms)
    sums = scatter_sum(jnp.stack(terms), batches)
    return (
        sublayer_result.astype(BF16)[None],
        signal_adjoint[None],
        sums[:taps],
        sums[taps],
    )


def solution(mesh):
    return jax.shard_map(
        functools.partial(local, batches=mesh.shape["batch"], mps=mesh.shape["mp"]),
        mesh=mesh,
        in_specs=(
            P("batch", "tm", None),
            P(),
            P(None, None, "mp"),
            P("mp"),
            P("mp", None),
            P(),
            P("batch", "tm", None),
        ),
        out_specs=(
            P("batch", "tm", None),
            P("batch", "tm", None),
            P(None, ("batch", "tm")),
            P(("batch", "tm")),
        ),
        check_vma=False,
    )
```

```python
import functools
import math

import jax
import jax.numpy as jnp
from jax import lax
from jax.experimental import pallas as pl
from jax.experimental.pallas import tpu as pltpu
from jax.sharding import PartitionSpec as P

INTERPRET = False
TM = 64
F32 = jnp.float32
BF16 = jnp.bfloat16


def _split(t):
    return t // 16, (t // 8) % 2, (t // 2) % 4, t % 2


def _join(z4, z2, x, yh):
    return ((z4 % 4) * 2 + z2) * 8 + (x % 4) * 2 + yh


def move_z4(a, s):
    pairs = []
    for t in range(TM):
        z4, z2, x, yh = _split(t)
        pairs.append((t, _join(z4 + s, z2, x, yh)))
    return lax.ppermute(a, "tm", pairs)


def move_x(a, s):
    pairs = []
    for t in range(TM):
        z4, z2, x, yh = _split(t)
        pairs.append((t, _join(z4, z2, x + s, yh)))
    return lax.ppermute(a, "tm", pairs)


def move_zy(a, m):
    pairs = []
    for t in range(TM):
        z4, z2, x, yh = _split(t)
        pairs.append((t, _join(z4, z2 ^ (m & 1), x, yh ^ (m >> 1))))
    return lax.ppermute(a, "tm", pairs)


def vcall(kernel, out_shape, scratch=(), smem=0, n_in=0):
    space = [pl.BlockSpec(memory_space=pltpu.SMEM)] * smem
    space += [pl.BlockSpec(memory_space=pltpu.VMEM)] * n_in
    return pl.pallas_call(
        kernel,
        out_shape=out_shape,
        in_specs=space,
        out_specs=jax.tree.map(lambda _: pl.BlockSpec(memory_space=pltpu.VMEM), out_shape),
        scratch_shapes=list(scratch),
        interpret=INTERPRET,
    )


def dotf(a, b, ca=1, cb=0):
    if INTERPRET:
        a, b = a.astype(F32), b.astype(F32)
    return lax.dot_general(a, b, (((ca,), (cb,)), ((), ())), preferred_element_type=F32)


def front_kernel(idx, sharp, x, factor, w, o0, o1, o2, o3, qpay, qhat_o, khat_o, rad_o, pay, *, heads, hs):
    xf = x[...].astype(F32)
    centred = xf - jnp.mean(xf, axis=-1, keepdims=True)
    var = jnp.mean(centred * centred, axis=-1, keepdims=True)
    unit = centred * (1.0 / jnp.sqrt(var + 1e-05))
    normed = (unit * factor[...]).astype(BF16)
    kt = dotf(normed, w[1]).T
    vt = dotf(normed, w[2]).T
    qt = dotf(normed, w[0]).T
    for h in range(heads):
        lo, hi = h * hs, (h + 1) * hs
        q = qt[lo:hi]
        k = kt[lo:hi]
        qr = jnp.sqrt(jnp.mean(q * q, axis=0, keepdims=True) + 1e-06)
        kr = jnp.sqrt(jnp.mean(k * k, axis=0, keepdims=True) + 1e-06)
        qh = q / qr
        kh = k / kr
        qhat_o[lo:hi] = qh
        khat_o[lo:hi] = kh
        rad_o[h : h + 1] = qr
        rad_o[heads + h : heads + h + 1] = kr
        pay[h, 0:hs] = kh.astype(BF16)
        pay[h, hs : 2 * hs] = vt[lo:hi].astype(BF16)
        qpay[h] = (qh * (sharp[h] / math.sqrt(hs))).astype(BF16)
    for s, o in enumerate((o0, o1, o2, o3)):
        o[...] = pay[lax.rem(idx[0] + s, 4)]


def fill_pad(pad, left, own, right):
    reach = left.shape[0]
    rows = own.shape[0]
    pad[16 - reach : 16] = left[...].astype(F32)
    pad[16 : 16 + rows] = own[...].astype(F32)
    pad[16 + rows : 16 + rows + reach] = right[...].astype(F32)


def conv_rows(pad, taps, out, rows, flip):
    count = taps.shape[0]
    reach = count // 2

    def chunk(c, _):
        lanes = pl.ds(pl.multiple_of(c * 128, 128), 128)
        acc = pad[16 : 16 + rows, lanes]
        for j in range(count):
            at = 16 + reach - j if flip else 16 - reach + j
            acc = acc + taps[j : j + 1, lanes] * pad[at : at + rows, lanes]
        out[:, lanes] = acc.astype(out.dtype)
        return 0

    lax.fori_loop(0, out.shape[1] // 128, chunk, 0)


def send_kernel(idx, left, own, right, taps, qpay, wf, o0, o1, o2, o3, gres, pad, g_s, *, hs):
    fill_pad(pad, left, own, right)
    conv_rows(pad, taps, gres, own.shape[0], True)
    gt = dotf(wf[...], gres[...].astype(BF16), 1, 1).astype(BF16)
    for h in range(4):
        g_s[h] = gt[h * hs : (h + 1) * hs]
    for s, o in enumerate((o0, o1, o2, o3)):
        at = lax.rem(idx[0] + s, 4)
        o[0:hs] = qpay[at]
        o[hs : 2 * hs] = g_s[at]


def tail_kernel(part, other, x, factor, left, own, right, gres, res_o, sig_o, sums, pad, resf, gain, *, rows, taps):
    fill_pad(pad, left, own, right)
    reach = taps // 2
    total = part[0:rows].astype(F32) + other[0:rows].astype(F32)
    xf = x[...].astype(F32)
    residual = (xf + total).astype(BF16)
    res_o[...] = residual
    resf[...] = residual.astype(F32)
    centred = xf - jnp.mean(xf, axis=-1, keepdims=True)
    var = jnp.mean(centred * centred, axis=-1, keepdims=True)
    inv = 1.0 / jnp.sqrt(var + 1e-05)
    unit = centred * inv
    grad = part[rows : 2 * rows].astype(F32) + other[rows : 2 * rows].astype(F32)
    prod = grad * unit
    gain[...] = jnp.sum(prod, axis=0, keepdims=True)
    f = factor[...]
    scaled = grad * f
    m1 = jnp.mean(scaled, axis=-1, keepdims=True)
    m2 = jnp.mean(prod * f, axis=-1, keepdims=True)
    sig_o[...] = (gres[...] + (scaled - m1 - unit * m2) * inv).astype(BF16)
    half = sums.shape[2] // 128

    for h in range(2):

        def chunk(c, _):
            lanes = pl.ds(pl.multiple_of((h * half + c) * 128, 128), 128)
            to = pl.ds(pl.multiple_of(c * 128, 128), 128)
            r = resf[:, lanes]
            for j in range(taps):
                at = 16 + reach - j
                sums[h, j : j + 1, to] = jnp.sum(r * pad[at : at + rows, lanes], axis=0, keepdims=True)
            sums[h, taps : taps + 1, to] = gain[:, lanes]
            return 0

        lax.fori_loop(0, half, chunk, 0)


def out_kernel(left, own, right, taps, out, pad):
    fill_pad(pad, left, own, right)
    conv_rows(pad, taps, out, own.shape[0], False)


KB = 512
UQ = 4
UK = 4


def to_rows(a):
    return a.astype(F32).T.astype(BF16)


def totals_kernel(*refs, hs):
    kv = refs[0:4]
    qg = refs[4:8]
    out = refs[8]
    kn, vn, qgs = refs[9:]
    span = kv[0].shape[1]
    for r in range(4):
        kn[r * span : (r + 1) * span] = to_rows(kv[r][0:hs])
        vn[r * span : (r + 1) * span] = to_rows(kv[r][hs : 2 * hs])
        qgs[r] = qg[r][...]
    blocks = 4 * span // KB

    def over_q(j, _):
        qt = qgs[j, 0:hs]
        gt = qgs[j, hs : 2 * hs]

        def over_k(b, state):
            tot, exp = state
            at = pl.multiple_of(b * KB, KB)
            w = jnp.exp(dotf(kn[pl.ds(at, KB)], qt))
            p = dotf(vn[pl.ds(at, KB)], gt)
            tot = tot + jnp.sum(w.reshape(KB // 8, 8, span), axis=0)
            exp = exp + jnp.sum((w * p).reshape(KB // 8, 8, span), axis=0)
            return tot, exp

        zero = jnp.zeros((8, span), F32)
        tot, exp = lax.fori_loop(0, blocks, over_k, (zero, zero), unroll=UK)
        out[j, 0:1] = jnp.sum(tot, axis=0, keepdims=True)
        out[j, 1:2] = jnp.sum(exp, axis=0, keepdims=True)
        return 0

    lax.fori_loop(0, 4, over_q, 0)


def grads_kernel(*refs, hs):
    te = refs[0:2]
    kv = refs[2:6]
    qg = refs[6:10]
    rows = refs[10:14]
    cols = refs[14:18]
    kn, vn, kvs, qgs, qn, gn, acc, inv, dlt, colacc = refs[18:]
    span = kv[0].shape[1]
    per = span // KB
    for r in range(4):
        kn[r * span : (r + 1) * span] = to_rows(kv[r][0:hs])
        vn[r * span : (r + 1) * span] = to_rows(kv[r][hs : 2 * hs])
        for c in range(per):
            kvs[r * per + c] = kv[r][:, c * KB : (c + 1) * KB]
        qgs[r] = qg[r][...]
        qn[r] = to_rows(qg[r][0:hs])
        gn[r] = to_rows(qg[r][hs : 2 * hs])
        t = te[0][r] + te[1][r ^ 2]
        one = 1.0 / t[0:1]
        inv[r] = one
        dlt[r] = t[1:2] * one
    acc[...] = jnp.zeros(acc.shape, F32)

    def over_k(b, _):
        at = pl.multiple_of(b * KB, KB)
        k = kn[pl.ds(at, KB)]
        v = vn[pl.ds(at, KB)]
        kt = kvs[b, 0:hs]
        vt = kvs[b, hs : 2 * hs]

        def over_q(j, state):
            gk, gv = state
            prob = jnp.exp(dotf(k, qgs[j, 0:hs])) * inv[j]
            slope = prob * (dotf(v, qgs[j, hs : 2 * hs]) - dlt[j])
            pb = prob.astype(BF16)
            sb = slope.astype(BF16)
            acc[j, 0:hs] += dotf(vt, pb)
            acc[j, hs : 2 * hs] += dotf(kt, sb)
            return gk + dotf(sb, qn[j]), gv + dotf(pb, gn[j])

        zero = jnp.zeros((KB, hs), F32)
        gk, gv = lax.fori_loop(0, 4, over_q, (zero, zero), unroll=UQ)
        colacc[b, 0:hs] = gk.T.astype(BF16)
        colacc[b, hs : 2 * hs] = gv.T.astype(BF16)
        return 0

    lax.fori_loop(0, 4 * per, over_k, 0)
    for r in range(4):
        rows[r][...] = acc[r].astype(BF16)
        for c in range(per):
            cols[r][:, c * KB : (c + 1) * KB] = colacc[r * per + c]


def run_totals(kv, qg, hs, span):
    return vcall(
        functools.partial(totals_kernel, hs=hs),
        jax.ShapeDtypeStruct((4, 2, span), F32),
        scratch=[
            pltpu.VMEM((4 * span, hs), BF16),
            pltpu.VMEM((4 * span, hs), BF16),
            pltpu.VMEM((4, 2 * hs, span), BF16),
        ],
        n_in=8,
    )(*kv, *qg)


def run_grads(te, kv, qg, hs, span):
    per = span // KB
    return vcall(
        functools.partial(grads_kernel, hs=hs),
        tuple(jax.ShapeDtypeStruct((2 * hs, span), BF16) for _ in range(8)),
        scratch=[
            pltpu.VMEM((4 * span, hs), BF16),
            pltpu.VMEM((4 * span, hs), BF16),
            pltpu.VMEM((4 * per, 2 * hs, KB), BF16),
            pltpu.VMEM((4, 2 * hs, span), BF16),
            pltpu.VMEM((4, span, hs), BF16),
            pltpu.VMEM((4, span, hs), BF16),
            pltpu.VMEM((4, 2 * hs, span), F32),
            pltpu.VMEM((4, 1, span), F32),
            pltpu.VMEM((4, 1, span), F32),
            pltpu.VMEM((4 * per, 2 * hs, KB), BF16),
        ],
        n_in=10,
    )(*te, *kv, *qg)


def sum_kernel(*refs, hs):
    row = refs[0][...].astype(F32)
    col = refs[4][...].astype(F32)
    for i in range(1, 4):
        row = row + refs[i][...].astype(F32)
        col = col + refs[4 + i][...].astype(F32)
    row = row.astype(BF16)
    col = col.astype(BF16)
    lanes = row.shape[1] // 4
    for s in range(4):
        refs[8 + s][0 : 2 * hs] = row[:, s * lanes : (s + 1) * lanes]
        refs[8 + s][2 * hs : 4 * hs] = col[:, s * lanes : (s + 1) * lanes]


def back_kernel(idx, sharp, b0, b1, b2, b3, qhat, khat, rad, wf, w, out, home, att, qgr, kgr, vgr, *, heads, hs):
    for s, b in enumerate((b0, b1, b2, b3)):
        home[lax.rem(idx[0] + s, 4)] = b[...]
    lanes = b0.shape[1]
    for h in range(heads):
        lo, hi = h * hs, (h + 1) * hs
        att[lo:hi] = home[h, 0:hs].astype(F32)
        gq = home[h, hs : 2 * hs].astype(F32) * (sharp[h] / math.sqrt(hs))
        gk = home[h, 2 * hs : 3 * hs].astype(F32)
        vgr[lo:hi] = home[h, 3 * hs : 4 * hs].astype(F32)
        qh = qhat[lo:hi]
        kh = khat[lo:hi]
        qgr[lo:hi] = (gq - qh * jnp.mean(gq * qh, axis=0, keepdims=True)) / rad[h : h + 1]
        kgr[lo:hi] = (gk - kh * jnp.mean(gk * kh, axis=0, keepdims=True)) / rad[heads + h : heads + h + 1]
    out[0:lanes] = dotf(att[...].T.astype(BF16), wf[...]).astype(BF16)
    normed = dotf(qgr[...].T.astype(BF16), w[0], 1, 1)
    normed = normed + dotf(kgr[...].T.astype(BF16), w[1], 1, 1)
    normed = normed + dotf(vgr[...].T.astype(BF16), w[2], 1, 1)
    out[lanes : 2 * lanes] = normed.astype(BF16)


def rims(cells, width):
    ends = TM - 1
    head = cells[:width]
    tail = cells[cells.shape[0] - width :]
    return (
        lax.ppermute(tail, "tm", [(i, i + 1) for i in range(ends)]),
        cells,
        lax.ppermute(head, "tm", [(i + 1, i) for i in range(ends)]),
    )


def pieces(a, n):
    width = a.shape[1] // n
    return lambda i: lax.dynamic_slice_in_dim(a, i * width, width, axis=1)


def scatter_sum(a, batches):
    t = lax.axis_index("tm")
    z4, z2, x, yh = t // 16, (t // 8) % 2, (t // 2) % 4, t % 2
    if batches > 1:
        b = lax.axis_index("batch")
        away = lax.dynamic_index_in_dim(a, 1 - b, 0, keepdims=False)
        a = lax.dynamic_index_in_dim(a, b, 0, keepdims=False) + lax.ppermute(away, "batch", [(0, 1), (1, 0)])
    else:
        a = jnp.concatenate([a[0], a[1]], axis=1)
    at = pieces(a, 4)
    got = [move_z4(at((z4 + s) % 4), s) for s in (1, 2, 3)]
    a = (at(z4) + got[0]) + (got[1] + got[2])
    at = pieces(a, 2)
    a = at(z2) + move_zy(at(1 - z2), 1)
    at = pieces(a, 4)
    got = [move_x(at((x + s) % 4), s) for s in (1, 2, 3)]
    a = (at(x) + got[0]) + (got[1] + got[2])
    at = pieces(a, 2)
    return at(yh) + move_zy(at(1 - yh), 2)


def local(input_signal, standardize_factor, triple_projection, score_sharpening, final_projection, filter_taps, mixture_adjoint, *, batches, mps):
    rows, width = input_signal.shape[1:]
    heads = score_sharpening.shape[0]
    hs = triple_projection.shape[2] // heads
    flat = heads * hs
    taps = filter_taps.shape[0]
    reach = taps // 2
    t = lax.axis_index("tm")
    z4 = (t // 16).astype(jnp.int32).reshape(1)
    x_in = input_signal[0]
    adj = mixture_adjoint[0]
    factor = standardize_factor[None]
    shape = jax.ShapeDtypeStruct
    adj_rims = rims(adj, reach)
    piece = shape((2 * hs, rows), BF16)
    *sent_kv, qpay, qhat, khat, rad = vcall(
        functools.partial(front_kernel, heads=heads, hs=hs),
        (piece,) * 4 + (shape((heads, hs, rows), BF16), shape((flat, rows), F32), shape((flat, rows), F32), shape((2 * heads, rows), F32)),
        scratch=[pltpu.VMEM((heads, 2 * hs, rows), BF16)],
        smem=2,
        n_in=3,
    )(z4, score_sharpening, x_in, factor, triple_projection)
    got_kv = [sent_kv[0]] + [move_z4(sent_kv[s], s) for s in (1, 2, 3)]
    pad = pltpu.VMEM((rows + 32, width), F32)
    *sent_qg, grad_res = vcall(
        functools.partial(send_kernel, hs=hs),
        (piece,) * 4 + (shape((rows, width), F32),),
        scratch=[pad, pltpu.VMEM((4, hs, rows), BF16)],
        smem=1,
        n_in=6,
    )(z4, *adj_rims, filter_taps, qpay, final_projection)
    got_qg = [sent_qg[0]] + [move_z4(sent_qg[s], s) for s in (1, 2, 3)]
    kv0 = jnp.concatenate(got_kv, axis=1)
    qg0 = jnp.concatenate(got_qg, axis=1)
    kv = [kv0] + [move_x(kv0, s) for s in (1, 2, 3)]
    qg = [qg0] + [move_zy(qg0, m) for m in (1, 2, 3)]
    span = 4 * rows
    te0 = run_totals(kv, qg, hs, span)
    te1 = move_zy(te0, 1)
    te1 = te0 + jnp.stack([te1[r ^ 1] for r in range(4)])
    te = [te1, move_zy(te1, 2)]
    res = run_grads(te, kv, qg, hs, span)
    row = [res[0]] + [move_zy(res[m], m) for m in (1, 2, 3)]
    col = [res[4]] + [move_x(res[4 + s], -s) for s in (1, 2, 3)]
    home = vcall(
        functools.partial(sum_kernel, hs=hs),
        tuple(shape((4 * hs, rows), BF16) for _ in range(4)),
        n_in=8,
    )(*row, *col)
    back = [home[0]] + [move_z4(home[s], -s) for s in (1, 2, 3)]
    part = vcall(
        functools.partial(back_kernel, heads=heads, hs=hs),
        shape((2 * rows, width), BF16),
        scratch=[pltpu.VMEM((4, 4 * hs, rows), BF16)] + [pltpu.VMEM((flat, rows), F32)] * 4,
        smem=2,
        n_in=9,
    )(z4, score_sharpening, *back, qhat, khat, rad, final_projection, triple_projection)
    other = lax.ppermute(part, "mp", [(0, 1), (1, 0)]) if mps > 1 else jnp.zeros_like(part)
    residual, signal_adjoint, sums = vcall(
        functools.partial(tail_kernel, rows=rows, taps=taps),
        (shape((rows, width), BF16), shape((rows, width), BF16), shape((2, taps + 1, width // 2), F32)),
        scratch=[pad, pltpu.VMEM((rows, width), F32), pltpu.VMEM((1, width), F32)],
        n_in=8,
    )(part, other, x_in, factor, *adj_rims, grad_res)
    res_rims = rims(residual, reach)
    sublayer_result = vcall(out_kernel, shape((rows, width), BF16), scratch=[pad], n_in=4)(*res_rims, filter_taps)
    sums = scatter_sum(sums, batches)
    return (sublayer_result[None], signal_adjoint[None], sums[:taps], sums[taps])


def solution(mesh):
    return jax.shard_map(
        functools.partial(local, batches=mesh.shape["batch"], mps=mesh.shape["mp"]),
        mesh=mesh,
        in_specs=(
            P("batch", "tm", None),
            P(),
            P(None, None, "mp"),
            P("mp"),
            P("mp", None),
            P(),
            P("batch", "tm", None),
        ),
        out_specs=(
            P("batch", "tm", None),
            P("batch", "tm", None),
            P(None, ("batch", "tm")),
            P(("batch", "tm")),
        ),
        check_vma=False,
    )
```

```python
import functools
import math

import jax
import jax.numpy as jnp
from jax import lax
from jax.experimental import pallas as pl
from jax.experimental.pallas import tpu as pltpu
from jax.sharding import PartitionSpec as P


INTERPRET = False
LIMIT = 24 * 1024 * 1024
TM = 64
F32 = jnp.float32
BF16 = jnp.bfloat16


def _split(t):
    return t // 16, (t // 8) % 2, (t // 2) % 4, t % 2


def _join(z4, z2, x, yh):
    return ((z4 % 4) * 2 + z2) * 8 + (x % 4) * 2 + yh


def move_z4(a, s):
    pairs = []
    for t in range(TM):
        z4, z2, x, yh = _split(t)
        pairs.append((t, _join(z4 + s, z2, x, yh)))
    return lax.ppermute(a, "tm", pairs)


def move_x(a, s):
    pairs = []
    for t in range(TM):
        z4, z2, x, yh = _split(t)
        pairs.append((t, _join(z4, z2, x + s, yh)))
    return lax.ppermute(a, "tm", pairs)


def move_zy(a, m):
    pairs = []
    for t in range(TM):
        z4, z2, x, yh = _split(t)
        pairs.append((t, _join(z4, z2 ^ (m & 1), x, yh ^ (m >> 1))))
    return lax.ppermute(a, "tm", pairs)


def vcall(kernel, out_shape, scratch=(), smem=0, n_in=0, out_hbm=(), in_hbm=()):
    space = [pl.BlockSpec(memory_space=pltpu.SMEM)] * smem
    space += [pl.BlockSpec(memory_space=pltpu.VMEM)] * n_in
    flat, tree = jax.tree.flatten(out_shape)
    held = flat
    if not INTERPRET:
        held = [o if i in out_hbm else pltpu.VMEM(o.shape, o.dtype) for i, o in enumerate(flat)]
    call = pl.pallas_call(
        kernel,
        out_shape=jax.tree.unflatten(tree, held),
        in_specs=space,
        out_specs=jax.tree.unflatten(tree, [pl.BlockSpec(memory_space=pltpu.VMEM)] * len(flat)),
        scratch_shapes=list(scratch),
        compiler_params=pltpu.CompilerParams(vmem_limit_bytes=LIMIT),
        interpret=INTERPRET,
    )

    def run(*args):
        if not INTERPRET:
            args = [
                a if i < smem or i - smem in in_hbm else pltpu.with_memory_space_constraint(a, pltpu.VMEM)
                for i, a in enumerate(args)
            ]
        return call(*args)

    return run


def dotf(a, b, ca=1, cb=0):
    if INTERPRET:
        a, b = a.astype(F32), b.astype(F32)
    return lax.dot_general(a, b, (((ca,), (cb,)), ((), ())), preferred_element_type=F32)


def front_kernel(idx, sharp, x, factor, w, o0, o1, o2, o3, qpay, qhat_o, khat_o, rad_o, pay, *, heads, hs):
    xf = x[...].astype(F32)
    centred = xf - jnp.mean(xf, axis=-1, keepdims=True)
    var = jnp.mean(centred * centred, axis=-1, keepdims=True)
    unit = centred * (1.0 / jnp.sqrt(var + 1e-05))
    normed = (unit * factor[...]).astype(BF16)
    kt = dotf(normed, w[1]).T
    vt = dotf(normed, w[2]).T
    qt = dotf(normed, w[0]).T
    for h in range(heads):
        lo, hi = h * hs, (h + 1) * hs
        q = qt[lo:hi]
        k = kt[lo:hi]
        qr = jnp.sqrt(jnp.mean(q * q, axis=0, keepdims=True) + 1e-06)
        kr = jnp.sqrt(jnp.mean(k * k, axis=0, keepdims=True) + 1e-06)
        qh = q / qr
        kh = k / kr
        qhat_o[lo:hi] = qh
        khat_o[lo:hi] = kh
        rad_o[h : h + 1] = qr
        rad_o[heads + h : heads + h + 1] = kr
        pay[h, 0:hs] = kh.astype(BF16)
        pay[h, hs : 2 * hs] = vt[lo:hi].astype(BF16)
        qpay[h] = (qh * (sharp[h] / math.sqrt(hs))).astype(BF16)
    for s, o in enumerate((o0, o1, o2, o3)):
        o[...] = pay[lax.rem(idx[0] + s, 4)]


def fill_pad(pad, left, own, right):
    reach = left.shape[0]
    rows = own.shape[0]
    pad[16 - reach : 16] = left[...].astype(F32)
    pad[16 : 16 + rows] = own[...].astype(F32)
    pad[16 + rows : 16 + rows + reach] = right[...].astype(F32)


def conv_rows(pad, taps, out, rows, flip):
    count = taps.shape[0]
    reach = count // 2

    def chunk(c, _):
        lanes = pl.ds(pl.multiple_of(c * 128, 128), 128)
        acc = pad[16 : 16 + rows, lanes]
        for phase in range(8):
            shifted = pad[phase : phase + rows + 24, lanes]
            for j in range(count):
                at = 16 + reach - j if flip else 16 - reach + j
                if at % 8 == phase:
                    acc = acc + taps[j : j + 1, lanes] * shifted[at - phase : at - phase + rows]
        out[:, lanes] = acc.astype(out.dtype)
        return 0

    lax.fori_loop(0, out.shape[1] // 128, chunk, 0)


def send_kernel(idx, left, own, right, taps, qpay, wf, o0, o1, o2, o3, gres, pad, g_s, *, hs):
    fill_pad(pad, left, own, right)
    conv_rows(pad, taps, gres, own.shape[0], True)
    gt = dotf(wf[...], gres[...].astype(BF16), 1, 1).astype(BF16)
    for h in range(4):
        g_s[h] = gt[h * hs : (h + 1) * hs]
    for s, o in enumerate((o0, o1, o2, o3)):
        at = lax.rem(idx[0] + s, 4)
        o[0:hs] = qpay[at]
        o[hs : 2 * hs] = g_s[at]


def tail_kernel(part, other, x, factor, left, own, right, gres, res_o, sig_o, sums, pad, resf, gain, *, rows, taps):
    fill_pad(pad, left, own, right)
    reach = taps // 2
    total = part[0:rows].astype(F32) + other[0:rows].astype(F32)
    xf = x[...].astype(F32)
    residual = (xf + total).astype(BF16)
    res_o[...] = residual
    resf[...] = residual.astype(F32)
    centred = xf - jnp.mean(xf, axis=-1, keepdims=True)
    var = jnp.mean(centred * centred, axis=-1, keepdims=True)
    inv = 1.0 / jnp.sqrt(var + 1e-05)
    unit = centred * inv
    grad = part[rows : 2 * rows].astype(F32) + other[rows : 2 * rows].astype(F32)
    prod = grad * unit
    gain[...] = jnp.sum(prod, axis=0, keepdims=True)
    f = factor[...]
    scaled = grad * f
    m1 = jnp.mean(scaled, axis=-1, keepdims=True)
    m2 = jnp.mean(prod * f, axis=-1, keepdims=True)
    sig_o[...] = (gres[...] + (scaled - m1 - unit * m2) * inv).astype(BF16)
    half = sums.shape[2] // 128

    for h in range(2):

        def chunk(c, _):
            lanes = pl.ds(pl.multiple_of((h * half + c) * 128, 128), 128)
            to = pl.ds(pl.multiple_of(c * 128, 128), 128)
            r = resf[:, lanes]
            for phase in range(8):
                shifted = pad[phase : phase + rows + 24, lanes]
                for j in range(taps):
                    at = 16 + reach - j
                    if at % 8 == phase:
                        moved = shifted[at - phase : at - phase + rows]
                        sums[h, j : j + 1, to] = jnp.sum(r * moved, axis=0, keepdims=True)
            sums[h, taps : taps + 1, to] = gain[:, lanes]
            return 0

        lax.fori_loop(0, half, chunk, 0)


def out_kernel(left, own, right, taps, out, pad):
    fill_pad(pad, left, own, right)
    conv_rows(pad, taps, out, own.shape[0], False)


KB = 512
UQ = 4
UK = 4


def to_rows(a):
    return a.astype(F32).T.astype(BF16)


def totals_kernel(*refs, hs):
    kv = refs[0:4]
    qg = refs[4:8]
    out = refs[8]
    kn, vn, qgs = refs[9:]
    span = kv[0].shape[1]
    for r in range(4):
        kn[r * span : (r + 1) * span] = to_rows(kv[r][0:hs])
        vn[r * span : (r + 1) * span] = to_rows(kv[r][hs : 2 * hs])
        qgs[r] = qg[r][...]
    blocks = 4 * span // KB

    def over_q(j, _):
        qt = qgs[j, 0:hs]
        gt = qgs[j, hs : 2 * hs]

        def over_k(b, state):
            tot, exp = state
            at = pl.multiple_of(b * KB, KB)
            w = jnp.exp(dotf(kn[pl.ds(at, KB)], qt))
            p = dotf(vn[pl.ds(at, KB)], gt)
            tot = tot + jnp.sum(w.reshape(KB // 8, 8, span), axis=0)
            exp = exp + jnp.sum((w * p).reshape(KB // 8, 8, span), axis=0)
            return tot, exp

        zero = jnp.zeros((8, span), F32)
        tot, exp = lax.fori_loop(0, blocks, over_k, (zero, zero), unroll=UK)
        out[j, 0:1] = jnp.sum(tot, axis=0, keepdims=True)
        out[j, 1:2] = jnp.sum(exp, axis=0, keepdims=True)
        return 0

    lax.fori_loop(0, 4, over_q, 0)


def grads_kernel(*refs, hs):
    te = refs[0:2]
    kv = refs[2:6]
    qg = refs[6:10]
    rows = refs[10:14]
    cols = refs[14:18]
    kn, vn, kvs, qgs, qn, gn, acc, inv, dlt, colacc = refs[18:]
    span = kv[0].shape[1]
    per = span // KB
    for r in range(4):
        kn[r * span : (r + 1) * span] = to_rows(kv[r][0:hs])
        vn[r * span : (r + 1) * span] = to_rows(kv[r][hs : 2 * hs])
        for c in range(per):
            kvs[r * per + c] = kv[r][:, c * KB : (c + 1) * KB]
        qgs[r] = qg[r][...]
        qn[r] = to_rows(qg[r][0:hs])
        gn[r] = to_rows(qg[r][hs : 2 * hs])
        t = te[0][r] + te[1][r ^ 2]
        one = 1.0 / t[0:1]
        inv[r] = one
        dlt[r] = t[1:2] * one
    acc[...] = jnp.zeros(acc.shape, F32)

    def over_k(b, _):
        at = pl.multiple_of(b * KB, KB)
        k = kn[pl.ds(at, KB)]
        v = vn[pl.ds(at, KB)]
        kt = kvs[b, 0:hs]
        vt = kvs[b, hs : 2 * hs]

        def over_q(j, state):
            gk, gv = state
            prob = jnp.exp(dotf(k, qgs[j, 0:hs])) * inv[j]
            slope = prob * (dotf(v, qgs[j, hs : 2 * hs]) - dlt[j])
            pb = prob.astype(BF16)
            sb = slope.astype(BF16)
            acc[j, 0:hs] += dotf(vt, pb)
            acc[j, hs : 2 * hs] += dotf(kt, sb)
            return gk + dotf(sb, qn[j]), gv + dotf(pb, gn[j])

        zero = jnp.zeros((KB, hs), F32)
        gk, gv = lax.fori_loop(0, 4, over_q, (zero, zero), unroll=UQ)
        colacc[b, 0:hs] = gk.T.astype(BF16)
        colacc[b, hs : 2 * hs] = gv.T.astype(BF16)
        return 0

    lax.fori_loop(0, 4 * per, over_k, 0)
    for r in range(4):
        rows[r][...] = acc[r].astype(BF16)
        for c in range(per):
            cols[r][:, c * KB : (c + 1) * KB] = colacc[r * per + c]


def run_totals(kv, qg, hs, span):
    return vcall(
        functools.partial(totals_kernel, hs=hs),
        jax.ShapeDtypeStruct((4, 2, span), F32),
        scratch=[
            pltpu.VMEM((4 * span, hs), BF16),
            pltpu.VMEM((4 * span, hs), BF16),
            pltpu.VMEM((4, 2 * hs, span), BF16),
        ],
        n_in=8,
    )(*kv, *qg)


def run_grads(te, kv, qg, hs, span):
    per = span // KB
    return vcall(
        functools.partial(grads_kernel, hs=hs),
        tuple(jax.ShapeDtypeStruct((2 * hs, span), BF16) for _ in range(8)),
        scratch=[
            pltpu.VMEM((4 * span, hs), BF16),
            pltpu.VMEM((4 * span, hs), BF16),
            pltpu.VMEM((4 * per, 2 * hs, KB), BF16),
            pltpu.VMEM((4, 2 * hs, span), BF16),
            pltpu.VMEM((4, span, hs), BF16),
            pltpu.VMEM((4, span, hs), BF16),
            pltpu.VMEM((4, 2 * hs, span), F32),
            pltpu.VMEM((4, 1, span), F32),
            pltpu.VMEM((4, 1, span), F32),
            pltpu.VMEM((4 * per, 2 * hs, KB), BF16),
        ],
        n_in=10,
    )(*te, *kv, *qg)


def sum_kernel(*refs, hs):
    row = refs[0][...].astype(F32)
    col = refs[4][...].astype(F32)
    for i in range(1, 4):
        row = row + refs[i][...].astype(F32)
        col = col + refs[4 + i][...].astype(F32)
    row = row.astype(BF16)
    col = col.astype(BF16)
    lanes = row.shape[1] // 4
    for s in range(4):
        refs[8 + s][0 : 2 * hs] = row[:, s * lanes : (s + 1) * lanes]
        refs[8 + s][2 * hs : 4 * hs] = col[:, s * lanes : (s + 1) * lanes]


def back_kernel(idx, sharp, b0, b1, b2, b3, qhat, khat, rad, wf, w, out, home, att, qgr, kgr, vgr, *, heads, hs):
    for s, b in enumerate((b0, b1, b2, b3)):
        home[lax.rem(idx[0] + s, 4)] = b[...]
    lanes = b0.shape[1]
    for h in range(heads):
        lo, hi = h * hs, (h + 1) * hs
        att[lo:hi] = home[h, 0:hs].astype(F32)
        gq = home[h, hs : 2 * hs].astype(F32) * (sharp[h] / math.sqrt(hs))
        gk = home[h, 2 * hs : 3 * hs].astype(F32)
        vgr[lo:hi] = home[h, 3 * hs : 4 * hs].astype(F32)
        qh = qhat[lo:hi]
        kh = khat[lo:hi]
        qgr[lo:hi] = (gq - qh * jnp.mean(gq * qh, axis=0, keepdims=True)) / rad[h : h + 1]
        kgr[lo:hi] = (gk - kh * jnp.mean(gk * kh, axis=0, keepdims=True)) / rad[heads + h : heads + h + 1]
    out[0:lanes] = dotf(att[...].T.astype(BF16), wf[...]).astype(BF16)
    normed = dotf(qgr[...].T.astype(BF16), w[0], 1, 1)
    normed = normed + dotf(kgr[...].T.astype(BF16), w[1], 1, 1)
    normed = normed + dotf(vgr[...].T.astype(BF16), w[2], 1, 1)
    out[lanes : 2 * lanes] = normed.astype(BF16)


def rims(cells, width):
    ends = TM - 1
    head = cells[:width]
    tail = cells[cells.shape[0] - width :]
    left = lax.ppermute(tail, "tm", [(i, i + 1) for i in range(ends)])
    right = lax.ppermute(head, "tm", [(i + 1, i) for i in range(ends)])
    return left, cells, right


def pieces(a, n):
    width = a.shape[1] // n
    return lambda i: lax.dynamic_slice_in_dim(a, i * width, width, axis=1)


def scatter_sum(a, batches):
    t = lax.axis_index("tm")
    z4, z2, x, yh = t // 16, (t // 8) % 2, (t // 2) % 4, t % 2
    if batches > 1:
        b = lax.axis_index("batch")
        away = lax.dynamic_index_in_dim(a, 1 - b, 0, keepdims=False)
        got = lax.ppermute(away, "batch", [(0, 1), (1, 0)])
        a = lax.dynamic_index_in_dim(a, b, 0, keepdims=False) + got
    else:
        a = jnp.concatenate([a[0], a[1]], axis=1)
    at = pieces(a, 4)
    got = [move_z4(at((z4 + s) % 4), s) for s in (1, 2, 3)]
    a = (at(z4) + got[0]) + (got[1] + got[2])
    at = pieces(a, 2)
    a = at(z2) + move_zy(at(1 - z2), 1)
    at = pieces(a, 4)
    got = [move_x(at((x + s) % 4), s) for s in (1, 2, 3)]
    a = (at(x) + got[0]) + (got[1] + got[2])
    at = pieces(a, 2)
    return at(yh) + move_zy(at(1 - yh), 2)


def step(input_signal, standardize_factor, triple_projection, score_sharpening, final_projection, filter_taps, mixture_adjoint, *, batches, mps):
    rows, width = input_signal.shape[1:]
    heads = score_sharpening.shape[0]
    hs = triple_projection.shape[2] // heads
    flat = heads * hs
    taps = filter_taps.shape[0]
    reach = taps // 2
    t = lax.axis_index("tm")
    z4 = (t // 16).astype(jnp.int32).reshape(1)
    x_in = input_signal[0]
    adj = mixture_adjoint[0]
    factor = standardize_factor[None]
    shape = jax.ShapeDtypeStruct
    adj_rims = rims(adj, reach)
    piece = shape((2 * hs, rows), BF16)
    *sent_kv, qpay, qhat, khat, rad = vcall(
        functools.partial(front_kernel, heads=heads, hs=hs),
        (piece,) * 4 + (shape((heads, hs, rows), BF16), shape((flat, rows), F32), shape((flat, rows), F32), shape((2 * heads, rows), F32)),
        scratch=[pltpu.VMEM((heads, 2 * hs, rows), BF16)],
        smem=2,
        n_in=3,
        in_hbm=(0, 1, 2),
    )(z4, score_sharpening, x_in, factor, triple_projection)
    got_kv = [sent_kv[0]] + [move_z4(sent_kv[s], s) for s in (1, 2, 3)]
    pad = pltpu.VMEM((rows + 32, width), F32)
    *sent_qg, grad_res = vcall(
        functools.partial(send_kernel, hs=hs),
        (piece,) * 4 + (shape((rows, width), F32),),
        scratch=[pad, pltpu.VMEM((4, hs, rows), BF16)],
        smem=1,
        n_in=6,
    )(z4, *adj_rims, filter_taps, qpay, final_projection)
    got_qg = [sent_qg[0]] + [move_z4(sent_qg[s], s) for s in (1, 2, 3)]
    kv0 = jnp.concatenate(got_kv, axis=1)
    qg0 = jnp.concatenate(got_qg, axis=1)
    kv = [kv0] + [move_x(kv0, s) for s in (1, 2, 3)]
    qg = [qg0] + [move_zy(qg0, m) for m in (1, 2, 3)]
    span = 4 * rows
    te0 = run_totals(kv, qg, hs, span)
    te1 = move_zy(te0, 1)
    te1 = te0 + jnp.stack([te1[r ^ 1] for r in range(4)])
    te = [te1, move_zy(te1, 2)]
    res = run_grads(te, kv, qg, hs, span)
    row = [res[0]] + [move_zy(res[m], m) for m in (1, 2, 3)]
    col = [res[4]] + [move_x(res[4 + s], -s) for s in (1, 2, 3)]
    home = vcall(
        functools.partial(sum_kernel, hs=hs),
        tuple(shape((4 * hs, rows), BF16) for _ in range(4)),
        n_in=8,
    )(*row, *col)
    back = [home[0]] + [move_z4(home[s], -s) for s in (1, 2, 3)]
    part = vcall(
        functools.partial(back_kernel, heads=heads, hs=hs),
        shape((2 * rows, width), BF16),
        scratch=[pltpu.VMEM((4, 4 * hs, rows), BF16)] + [pltpu.VMEM((flat, rows), F32)] * 4,
        smem=2,
        n_in=9,
    )(z4, score_sharpening, *back, qhat, khat, rad, final_projection, triple_projection)
    other = lax.ppermute(part, "mp", [(0, 1), (1, 0)]) if mps > 1 else jnp.zeros_like(part)
    residual, signal_adjoint, sums = vcall(
        functools.partial(tail_kernel, rows=rows, taps=taps),
        (shape((rows, width), BF16), shape((rows, width), BF16), shape((2, taps + 1, width // 2), F32)),
        scratch=[pad, pltpu.VMEM((rows, width), F32), pltpu.VMEM((1, width), F32)],
        n_in=8,
        out_hbm=(1,),
    )(part, other, x_in, factor, *adj_rims, grad_res)
    res_rims = rims(residual, reach)
    sublayer_result = vcall(out_kernel, shape((rows, width), BF16), scratch=[pad], n_in=4, out_hbm=(0,))(*res_rims, filter_taps)
    sums = scatter_sum(sums, batches)
    return (sublayer_result[None], signal_adjoint[None], sums[:taps], sums[taps])


def solution(mesh):
    call = mapped(mesh)
    return call


def mapped(mesh):
    return jax.shard_map(
        functools.partial(step, batches=mesh.shape["batch"], mps=mesh.shape["mp"]),
        mesh=mesh,
        in_specs=(
            P("batch", "tm", None),
            P(),
            P(None, None, "mp"),
            P("mp"),
            P("mp", None),
            P(),
            P("batch", "tm", None),
        ),
        out_specs=(
            P("batch", "tm", None),
            P("batch", "tm", None),
            P(None, ("batch", "tm")),
            P(("batch", "tm")),
        ),
        check_vma=False,
    )
```

```python
import functools
import math

import jax
import jax.numpy as jnp
from jax import lax
from jax.experimental import pallas as pl
from jax.experimental.pallas import tpu as pltpu
from jax.sharding import PartitionSpec as P


INTERPRET = False
LIMIT = 24 * 1024 * 1024
TM = 64
F32 = jnp.float32
BF16 = jnp.bfloat16


def _split(t):
    return t // 16, (t // 8) % 2, (t // 2) % 4, t % 2


def _join(z4, z2, x, yh):
    return ((z4 % 4) * 2 + z2) * 8 + (x % 4) * 2 + yh


def move_z4(a, s):
    pairs = []
    for t in range(TM):
        z4, z2, x, yh = _split(t)
        pairs.append((t, _join(z4 + s, z2, x, yh)))
    return lax.ppermute(a, "tm", pairs)


def move_x(a, s):
    pairs = []
    for t in range(TM):
        z4, z2, x, yh = _split(t)
        pairs.append((t, _join(z4, z2, x + s, yh)))
    return lax.ppermute(a, "tm", pairs)


def move_zy(a, m):
    pairs = []
    for t in range(TM):
        z4, z2, x, yh = _split(t)
        pairs.append((t, _join(z4, z2 ^ (m & 1), x, yh ^ (m >> 1))))
    return lax.ppermute(a, "tm", pairs)


def ordered(move, shifts):
    got = {s: move(s) for s in shifts}
    return [got[s] for s in (1, 2, 3)]


def vcall(kernel, out_shape, scratch=(), smem=0, n_in=0, raw=0, out_hbm=()):
    space = [pl.BlockSpec(memory_space=pltpu.SMEM)] * smem
    space += [pl.BlockSpec(memory_space=pltpu.VMEM)] * n_in
    space += [pl.BlockSpec(memory_space=pltpu.HBM if not INTERPRET else pl.ANY)] * raw
    flat, tree = jax.tree.flatten(out_shape)
    held = flat
    if not INTERPRET:
        held = [o if i in out_hbm else pltpu.VMEM(o.shape, o.dtype) for i, o in enumerate(flat)]
    call = pl.pallas_call(
        kernel,
        out_shape=jax.tree.unflatten(tree, held),
        in_specs=space,
        out_specs=jax.tree.unflatten(tree, [pl.BlockSpec(memory_space=pltpu.VMEM)] * len(flat)),
        scratch_shapes=list(scratch),
        compiler_params=pltpu.CompilerParams(vmem_limit_bytes=LIMIT),
        interpret=INTERPRET,
    )

    def run(*args):
        if not INTERPRET:
            args = [
                a if i < smem else pltpu.with_memory_space_constraint(a, pltpu.VMEM if i < smem + n_in else pltpu.HBM)
                for i, a in enumerate(args)
            ]
        return call(*args)

    return run


def dotf(a, b, ca=1, cb=0):
    if INTERPRET:
        a, b = a.astype(F32), b.astype(F32)
    return lax.dot_general(a, b, (((ca,), (cb,)), ((), ())), preferred_element_type=F32)


def front_kernel(
    idx, sharp, factor, x_hbm, w_hbm, o0, o1, o2, o3, qpay, qhat_o, khat_o, rad_o, pay, x, w, sem, *, heads, hs
):
    x_copy = pltpu.make_async_copy(x_hbm, x, sem.at[0])
    x_copy.start()
    copies = [pltpu.make_async_copy(w_hbm.at[i], w.at[i], sem.at[1 + i]) for i in range(3)]
    for i in (1, 2, 0):
        copies[i].start()
    x_copy.wait()
    xf = x[...].astype(F32)
    centred = xf - jnp.mean(xf, axis=-1, keepdims=True)
    var = jnp.mean(centred * centred, axis=-1, keepdims=True)
    unit = centred * (1.0 / jnp.sqrt(var + 1e-05))
    normed = (unit * factor[...]).astype(BF16)
    copies[1].wait()
    kt = dotf(normed, w[1]).T
    copies[2].wait()
    vt = dotf(normed, w[2]).T
    copies[0].wait()
    qt = dotf(normed, w[0]).T
    for h in range(heads):
        lo, hi = h * hs, (h + 1) * hs
        q = qt[lo:hi]
        k = kt[lo:hi]
        qr = jnp.sqrt(jnp.mean(q * q, axis=0, keepdims=True) + 1e-06)
        kr = jnp.sqrt(jnp.mean(k * k, axis=0, keepdims=True) + 1e-06)
        qh = q / qr
        kh = k / kr
        qhat_o[lo:hi] = qh
        khat_o[lo:hi] = kh
        rad_o[h : h + 1] = qr
        rad_o[heads + h : heads + h + 1] = kr
        pay[h, 0:hs] = kh.astype(BF16)
        pay[h, hs : 2 * hs] = vt[lo:hi].astype(BF16)
        qpay[h] = (qh * (sharp[h] / math.sqrt(hs))).astype(BF16)
    for s, o in enumerate((o0, o1, o2, o3)):
        o[...] = pay[lax.rem(idx[0] + s, 4)]


def fill_pad(pad, left, own, right):
    reach = left.shape[0]
    rows = own.shape[0]
    pad[16 - reach : 16] = left[...].astype(F32)
    pad[16 : 16 + rows] = own[...].astype(F32)
    pad[16 + rows : 16 + rows + reach] = right[...].astype(F32)


def conv_rows(pad, taps, out, rows, flip):
    count = taps.shape[0]
    reach = count // 2

    def chunk(c, _):
        lanes = pl.ds(pl.multiple_of(c * 128, 128), 128)
        acc = pad[16 : 16 + rows, lanes]
        for phase in range(8):
            shifted = pad[phase : phase + rows + 24, lanes]
            for j in range(count):
                at = 16 + reach - j if flip else 16 - reach + j
                if at % 8 == phase:
                    acc = acc + taps[j : j + 1, lanes] * shifted[at - phase : at - phase + rows]
        out[:, lanes] = acc.astype(out.dtype)
        return 0

    lax.fori_loop(0, out.shape[1] // 128, chunk, 0)


def send_kernel(idx, left, own, right, taps, qpay, wf, o0, o1, o2, o3, gres, pad, g_s, *, hs):
    fill_pad(pad, left, own, right)
    conv_rows(pad, taps, gres, own.shape[0], True)
    gt = dotf(wf[...], gres[...].astype(BF16), 1, 1).astype(BF16)
    for h in range(4):
        g_s[h] = gt[h * hs : (h + 1) * hs]
    for s, o in enumerate((o0, o1, o2, o3)):
        at = lax.rem(idx[0] + s, 4)
        o[0:hs] = qpay[at]
        o[hs : 2 * hs] = g_s[at]


def tail_kernel(part, other, x, factor, left, own, right, gres, res_o, sig_o, sums, first, last, pad, resf, gain, *, rows, taps):
    fill_pad(pad, left, own, right)
    reach = taps // 2
    total = part[0:rows].astype(F32) + other[0:rows].astype(F32)
    xf = x[...].astype(F32)
    residual = (xf + total).astype(BF16)
    res_o[...] = residual
    first[...] = residual[:reach]
    last[...] = residual[rows - reach :]
    resf[...] = residual.astype(F32)
    centred = xf - jnp.mean(xf, axis=-1, keepdims=True)
    var = jnp.mean(centred * centred, axis=-1, keepdims=True)
    inv = 1.0 / jnp.sqrt(var + 1e-05)
    unit = centred * inv
    grad = part[rows : 2 * rows].astype(F32) + other[rows : 2 * rows].astype(F32)
    prod = grad * unit
    gain[...] = jnp.sum(prod, axis=0, keepdims=True)
    f = factor[...]
    scaled = grad * f
    m1 = jnp.mean(scaled, axis=-1, keepdims=True)
    m2 = jnp.mean(prod * f, axis=-1, keepdims=True)
    sig_o[...] = (gres[...] + (scaled - m1 - unit * m2) * inv).astype(BF16)
    half = sums.shape[2] // 128

    for h in range(2):

        def chunk(c, _):
            lanes = pl.ds(pl.multiple_of((h * half + c) * 128, 128), 128)
            to = pl.ds(pl.multiple_of(c * 128, 128), 128)
            r = resf[:, lanes]
            for phase in range(8):
                shifted = pad[phase : phase + rows + 24, lanes]
                for j in range(taps):
                    at = 16 + reach - j
                    if at % 8 == phase:
                        moved = shifted[at - phase : at - phase + rows]
                        sums[h, j : j + 1, to] = jnp.sum(r * moved, axis=0, keepdims=True)
            sums[h, taps : taps + 1, to] = gain[:, lanes]
            return 0

        lax.fori_loop(0, half, chunk, 0)


def out_kernel(left, own, right, taps, out, pad):
    fill_pad(pad, left, own, right)
    conv_rows(pad, taps, out, own.shape[0], False)


def to_rows(a):
    return a.astype(F32).T.astype(BF16)


def rows_kernel(*refs, hs):
    kv = refs[0:4]
    qg = refs[4:8]
    te, acc = refs[8:10]
    kn, vn, qgs = refs[10:]
    span = kv[0].shape[1]
    for r in range(4):
        kn[r] = to_rows(kv[r][0:hs])
        vn[r] = to_rows(kv[r][hs : 2 * hs])
        qgs[r] = qg[r][...]

    def over_q(j, _):
        qt = qgs[j, 0:hs]
        gt = qgs[j, hs : 2 * hs]
        tot = jnp.zeros((8, span), F32)
        exp = jnp.zeros((8, span), F32)
        low = jnp.zeros((2 * hs, span), F32)
        high = jnp.zeros((hs, span), F32)
        for r in range(4):
            w = jnp.exp(dotf(kn[r], qt))
            wp = w * dotf(vn[r], gt)
            tot = tot + jnp.sum(w.reshape(span // 8, 8, span), axis=0)
            exp = exp + jnp.sum(wp.reshape(span // 8, 8, span), axis=0)
            low = low + dotf(kv[r][...], w.astype(BF16))
            high = high + dotf(kv[r][0:hs], wp.astype(BF16))
        acc[j, 0 : 2 * hs] = low
        acc[j, 2 * hs : 3 * hs] = high
        te[j, 0:1] = jnp.sum(tot, axis=0, keepdims=True)
        te[j, 1:2] = jnp.sum(exp, axis=0, keepdims=True)
        return 0

    lax.fori_loop(0, 4, over_q, 0)


def norm_kernel(te0, te1, acc, *rows, hs):
    for r in range(4):
        t = te0[r] + te1[r ^ 2]
        inv = 1.0 / t[0:1]
        delta = t[1:2] * inv
        rows[r][0:hs] = (acc[r, hs : 2 * hs] * inv).astype(BF16)
        rows[r][hs : 2 * hs] = ((acc[r, 2 * hs : 3 * hs] - delta * acc[r, 0:hs]) * inv).astype(BF16)


def cols_kernel(*refs, hs):
    te = refs[0:2]
    kv = refs[2:6]
    qg = refs[6:10]
    cols = refs[10:14]
    kn, vn, qn, gn, inv, dlt, colacc = refs[14:]
    span = kv[0].shape[1]
    for r in range(4):
        kn[r] = to_rows(kv[r][0:hs])
        vn[r] = to_rows(kv[r][hs : 2 * hs])
        qn[r] = to_rows(qg[r][0:hs])
        gn[r] = to_rows(qg[r][hs : 2 * hs])
        t = te[0][r] + te[1][r ^ 2]
        one = 1.0 / t[0:1]
        inv[r] = one
        dlt[r] = t[1:2] * one

    def over_k(b, _):
        k = kn[b]
        v = vn[b]
        gk = jnp.zeros((span, hs), F32)
        gv = jnp.zeros((span, hs), F32)
        for j in range(4):
            prob = jnp.exp(dotf(k, qg[j][0:hs])) * inv[j]
            slope = prob * (dotf(v, qg[j][hs : 2 * hs]) - dlt[j])
            gv = gv + dotf(prob.astype(BF16), gn[j])
            gk = gk + dotf(slope.astype(BF16), qn[j])
        colacc[b, 0:hs] = gk.T.astype(BF16)
        colacc[b, hs : 2 * hs] = gv.T.astype(BF16)
        return 0

    lax.fori_loop(0, 4, over_k, 0)
    for r in range(4):
        cols[r][...] = colacc[r]


def run_rows(kv, qg, hs, span):
    nat = pltpu.VMEM((4, span, hs), BF16)
    return vcall(
        functools.partial(rows_kernel, hs=hs),
        (jax.ShapeDtypeStruct((4, 2, span), F32), jax.ShapeDtypeStruct((4, 3 * hs, span), F32)),
        scratch=[nat, nat, pltpu.VMEM((4, 2 * hs, span), BF16)],
        n_in=8,
    )(*kv, *qg)


def run_cols(te, kv, qg, hs, span):
    nat = pltpu.VMEM((4, span, hs), BF16)
    row = pltpu.VMEM((4, 1, span), F32)
    return vcall(
        functools.partial(cols_kernel, hs=hs),
        tuple(jax.ShapeDtypeStruct((2 * hs, span), BF16) for _ in range(4)),
        scratch=[nat, nat, nat, nat, row, row, pltpu.VMEM((4, 2 * hs, span), BF16)],
        n_in=10,
    )(*te, *kv, *qg)


def sum_kernel(*refs, hs):
    row = refs[0][...].astype(F32)
    col = refs[4][...].astype(F32)
    for i in range(1, 4):
        row = row + refs[i][...].astype(F32)
        col = col + refs[4 + i][...].astype(F32)
    row = row.astype(BF16)
    col = col.astype(BF16)
    lanes = row.shape[1] // 4
    for s in range(4):
        refs[8 + s][0 : 2 * hs] = row[:, s * lanes : (s + 1) * lanes]
        refs[8 + s][2 * hs : 4 * hs] = col[:, s * lanes : (s + 1) * lanes]


def back_kernel(idx, sharp, b0, b1, b2, b3, qhat, khat, rad, wf, w, out, home, att, qgr, kgr, vgr, *, heads, hs):
    for s, b in enumerate((b0, b1, b2, b3)):
        home[lax.rem(idx[0] + s, 4)] = b[...]
    lanes = b0.shape[1]
    for h in range(heads):
        lo, hi = h * hs, (h + 1) * hs
        att[lo:hi] = home[h, 0:hs].astype(F32)
        gq = home[h, hs : 2 * hs].astype(F32) * (sharp[h] / math.sqrt(hs))
        gk = home[h, 2 * hs : 3 * hs].astype(F32)
        vgr[lo:hi] = home[h, 3 * hs : 4 * hs].astype(F32)
        qh = qhat[lo:hi]
        kh = khat[lo:hi]
        qgr[lo:hi] = (gq - qh * jnp.mean(gq * qh, axis=0, keepdims=True)) / rad[h : h + 1]
        kgr[lo:hi] = (gk - kh * jnp.mean(gk * kh, axis=0, keepdims=True)) / rad[heads + h : heads + h + 1]
    out[0:lanes] = dotf(att[...].T.astype(BF16), wf[...]).astype(BF16)
    normed = dotf(qgr[...].T.astype(BF16), w[0], 1, 1)
    normed = normed + dotf(kgr[...].T.astype(BF16), w[1], 1, 1)
    normed = normed + dotf(vgr[...].T.astype(BF16), w[2], 1, 1)
    out[lanes : 2 * lanes] = normed.astype(BF16)


def rims(cells, head, tail):
    ends = TM - 1
    left = lax.ppermute(tail, "tm", [(i, i + 1) for i in range(ends)])
    right = lax.ppermute(head, "tm", [(i + 1, i) for i in range(ends)])
    return left, cells, right


def pieces(a, n):
    width = a.shape[1] // n
    return lambda i: lax.dynamic_slice_in_dim(a, i * width, width, axis=1)


def scatter_sum(a, batches):
    t = lax.axis_index("tm")
    z4, z2, x, yh = t // 16, (t // 8) % 2, (t // 2) % 4, t % 2
    if batches > 1:
        b = lax.axis_index("batch")
        away = lax.dynamic_index_in_dim(a, 1 - b, 0, keepdims=False)
        got = lax.ppermute(away, "batch", [(0, 1), (1, 0)])
        a = lax.dynamic_index_in_dim(a, b, 0, keepdims=False) + got
    else:
        a = jnp.concatenate([a[0], a[1]], axis=1)
    at = pieces(a, 4)
    got = ordered(lambda s: move_z4(at((z4 + s) % 4), s), (2, 1, 3))
    a = (at(z4) + got[0]) + (got[1] + got[2])
    at = pieces(a, 2)
    a = at(z2) + move_zy(at(1 - z2), 1)
    at = pieces(a, 4)
    got = ordered(lambda s: move_x(at((x + s) % 4), s), (2, 1, 3))
    a = (at(x) + got[0]) + (got[1] + got[2])
    at = pieces(a, 2)
    return at(yh) + move_zy(at(1 - yh), 2)


def step(input_signal, standardize_factor, triple_projection, score_sharpening, final_projection, filter_taps, mixture_adjoint, *, batches, mps):
    rows, width = input_signal.shape[1:]
    heads = score_sharpening.shape[0]
    hs = triple_projection.shape[2] // heads
    flat = heads * hs
    taps = filter_taps.shape[0]
    reach = taps // 2
    t = lax.axis_index("tm")
    z4 = (t // 16).astype(jnp.int32).reshape(1)
    x_in = input_signal[0]
    adj = mixture_adjoint[0]
    factor = standardize_factor[None]
    shape = jax.ShapeDtypeStruct
    adj_rims = rims(adj, adj[:reach], adj[rows - reach :])
    piece = shape((2 * hs, rows), BF16)
    *sent_kv, qpay, qhat, khat, rad = vcall(
        functools.partial(front_kernel, heads=heads, hs=hs),
        (piece,) * 4 + (shape((heads, hs, rows), BF16), shape((flat, rows), F32), shape((flat, rows), F32), shape((2 * heads, rows), F32)),
        scratch=[
            pltpu.VMEM((heads, 2 * hs, rows), BF16),
            pltpu.VMEM((rows, width), BF16),
            pltpu.VMEM((3, width, flat), BF16),
            pltpu.SemaphoreType.DMA((4,)),
        ],
        smem=2,
        n_in=1,
        raw=2,
    )(z4, score_sharpening, factor, x_in, triple_projection)
    got_kv = [sent_kv[0]] + ordered(lambda s: move_z4(sent_kv[s], s), (2, 1, 3))
    pad = pltpu.VMEM((rows + 32, width), F32)
    *sent_qg, grad_res = vcall(
        functools.partial(send_kernel, hs=hs),
        (piece,) * 4 + (shape((rows, width), F32),),
        scratch=[pad, pltpu.VMEM((4, hs, rows), BF16)],
        smem=1,
        n_in=6,
    )(z4, *adj_rims, filter_taps, qpay, final_projection)
    got_qg = [sent_qg[0]] + ordered(lambda s: move_z4(sent_qg[s], s), (2, 1, 3))
    kv0 = jnp.concatenate(got_kv, axis=1)
    qg0 = jnp.concatenate(got_qg, axis=1)
    kv = [kv0] + ordered(lambda s: move_x(kv0, s), (2, 1, 3))
    qg = [qg0] + ordered(lambda m: move_zy(qg0, m), (3, 2, 1))
    span = 4 * rows
    te0, acc = run_rows(kv, qg, hs, span)
    te1 = move_zy(te0, 1)
    te1 = te0 + jnp.stack([te1[r ^ 1] for r in range(4)])
    te = [te1, move_zy(te1, 2)]
    rowp = vcall(functools.partial(norm_kernel, hs=hs), (shape((2 * hs, span), BF16),) * 4, n_in=3)(*te, acc)
    row = [rowp[0]] + ordered(lambda m: move_zy(rowp[m], m), (3, 2, 1))
    colp = run_cols(te, kv, qg, hs, span)
    col = [colp[0]] + ordered(lambda s: move_x(colp[s], -s), (2, 1, 3))
    home = vcall(
        functools.partial(sum_kernel, hs=hs),
        tuple(shape((4 * hs, rows), BF16) for _ in range(4)),
        n_in=8,
    )(*row, *col)
    back = [home[0]] + ordered(lambda s: move_z4(home[s], -s), (2, 1, 3))
    part = vcall(
        functools.partial(back_kernel, heads=heads, hs=hs),
        shape((2 * rows, width), BF16),
        scratch=[pltpu.VMEM((4, 4 * hs, rows), BF16)] + [pltpu.VMEM((flat, rows), F32)] * 4,
        smem=2,
        n_in=9,
    )(z4, score_sharpening, *back, qhat, khat, rad, final_projection, triple_projection)
    other = lax.ppermute(part, "mp", [(0, 1), (1, 0)]) if mps > 1 else jnp.zeros_like(part)
    edge = shape((reach, width), BF16)
    residual, signal_adjoint, sums, first, last = vcall(
        functools.partial(tail_kernel, rows=rows, taps=taps),
        (shape((rows, width), BF16), shape((rows, width), BF16), shape((2, taps + 1, width // 2), F32), edge, edge),
        scratch=[pad, pltpu.VMEM((rows, width), F32), pltpu.VMEM((1, width), F32)],
        n_in=8,
        out_hbm=(1,),
    )(part, other, x_in, factor, *adj_rims, grad_res)
    res_rims = rims(residual, first, last)
    sublayer_result = vcall(out_kernel, shape((rows, width), BF16), scratch=[pad], n_in=4, out_hbm=(0,))(*res_rims, filter_taps)
    sums = scatter_sum(sums, batches)
    return (sublayer_result[None], signal_adjoint[None], sums[:taps], sums[taps])


def solution(mesh):
    call = mapped(mesh)
    return call


def mapped(mesh):
    return jax.shard_map(
        functools.partial(step, batches=mesh.shape["batch"], mps=mesh.shape["mp"]),
        mesh=mesh,
        in_specs=(
            P("batch", "tm", None),
            P(),
            P(None, None, "mp"),
            P("mp"),
            P("mp", None),
            P(),
            P("batch", "tm", None),
        ),
        out_specs=(
            P("batch", "tm", None),
            P("batch", "tm", None),
            P(None, ("batch", "tm")),
            P(("batch", "tm")),
        ),
        check_vma=False,
    )
```

```python
import functools
import math

import jax
import jax.numpy as jnp
from jax import lax
from jax.experimental import pallas as pl
from jax.experimental.pallas import tpu as pltpu
from jax.sharding import PartitionSpec as P


INTERPRET = False
LIMIT = 24 * 1024 * 1024
TM = 64
F32 = jnp.float32
BF16 = jnp.bfloat16


def _split(t):
    return t // 16, (t // 8) % 2, (t // 2) % 4, t % 2


def _join(z4, z2, x, yh):
    return ((z4 % 4) * 2 + z2) * 8 + (x % 4) * 2 + yh


def send(a, axis, pairs, core=None):
    if core is None:
        return lax.ppermute(a, axis, pairs)
    cores = lax.axis_size("mp")
    return lax.ppermute(a, (axis, "mp"), [(i * cores + core, j * cores + core) for i, j in pairs])


def move_z4(a, s, core=None):
    pairs = []
    for t in range(TM):
        z4, z2, x, yh = _split(t)
        pairs.append((t, _join(z4 + s, z2, x, yh)))
    return send(a, "tm", pairs, core)


def move_x(a, s, core=None):
    pairs = []
    for t in range(TM):
        z4, z2, x, yh = _split(t)
        pairs.append((t, _join(z4, z2, x + s, yh)))
    return send(a, "tm", pairs, core)


def move_zy(a, m, core=None):
    pairs = []
    for t in range(TM):
        z4, z2, x, yh = _split(t)
        pairs.append((t, _join(z4, z2 ^ (m & 1), x, yh ^ (m >> 1))))
    return send(a, "tm", pairs, core)


def ordered(move, shifts):
    got = {s: move(s) for s in shifts}
    return [got[s] for s in (1, 2, 3)]


def vcall(kernel, out_shape, scratch=(), smem=0, n_in=0, raw=0, out_hbm=()):
    space = [pl.BlockSpec(memory_space=pltpu.SMEM)] * smem
    space += [pl.BlockSpec(memory_space=pltpu.VMEM)] * n_in
    space += [pl.BlockSpec(memory_space=pltpu.HBM if not INTERPRET else pl.ANY)] * raw
    flat, tree = jax.tree.flatten(out_shape)
    held = flat
    if not INTERPRET:
        held = [o if i in out_hbm else pltpu.VMEM(o.shape, o.dtype) for i, o in enumerate(flat)]
    call = pl.pallas_call(
        kernel,
        out_shape=jax.tree.unflatten(tree, held),
        in_specs=space,
        out_specs=jax.tree.unflatten(tree, [pl.BlockSpec(memory_space=pltpu.VMEM)] * len(flat)),
        scratch_shapes=list(scratch),
        compiler_params=pltpu.CompilerParams(vmem_limit_bytes=LIMIT),
        interpret=INTERPRET,
    )

    def run(*args):
        if not INTERPRET:
            args = [
                a if i < smem else pltpu.with_memory_space_constraint(a, pltpu.VMEM if i < smem + n_in else pltpu.HBM)
                for i, a in enumerate(args)
            ]
        return call(*args)

    return run


def dotf(a, b, ca=1, cb=0):
    if INTERPRET:
        a, b = a.astype(F32), b.astype(F32)
    return lax.dot_general(a, b, (((ca,), (cb,)), ((), ())), preferred_element_type=F32)


def front_kernel(
    idx, factor, x_hbm, w_hbm, o0, o1, o2, o3, qhat_o, khat_o, rad_o, pay, x, w, sem, *, heads, hs
):
    x_copy = pltpu.make_async_copy(x_hbm, x, sem.at[0])
    x_copy.start()
    copies = [pltpu.make_async_copy(w_hbm.at[i], w.at[i], sem.at[1 + i]) for i in range(3)]
    for i in (1, 2, 0):
        copies[i].start()
    x_copy.wait()
    xf = x[...].astype(F32)
    centred = xf - jnp.mean(xf, axis=-1, keepdims=True)
    var = jnp.mean(centred * centred, axis=-1, keepdims=True)
    unit = centred * (1.0 / jnp.sqrt(var + 1e-05))
    normed = (unit * factor[...]).astype(BF16)
    copies[1].wait()
    kt = dotf(normed, w[1]).T
    copies[2].wait()
    vt = dotf(normed, w[2]).T
    copies[0].wait()
    qt = dotf(normed, w[0]).T
    for h in range(heads):
        lo, hi = h * hs, (h + 1) * hs
        q = qt[lo:hi]
        k = kt[lo:hi]
        qr = jnp.sqrt(jnp.mean(q * q, axis=0, keepdims=True) + 1e-06)
        kr = jnp.sqrt(jnp.mean(k * k, axis=0, keepdims=True) + 1e-06)
        qh = q / qr
        kh = k / kr
        qhat_o[lo:hi] = qh
        khat_o[lo:hi] = kh
        rad_o[h : h + 1] = qr
        rad_o[heads + h : heads + h + 1] = kr
        pay[h, 0:hs] = kh.astype(BF16)
        pay[h, hs : 2 * hs] = vt[lo:hi].astype(BF16)
    for s, o in enumerate((o0, o1, o2, o3)):
        o[...] = pay[lax.rem(idx[0] + s, 4)]


def fill_pad(pad, left, own, right):
    reach = left.shape[0]
    rows = own.shape[0]
    pad[16 - reach : 16] = left[...].astype(F32)
    pad[16 : 16 + rows] = own[...].astype(F32)
    pad[16 + rows : 16 + rows + reach] = right[...].astype(F32)


def conv_rows(pad, taps, out, rows, flip):
    count = taps.shape[0]
    reach = count // 2

    def chunk(c, _):
        lanes = pl.ds(pl.multiple_of(c * 128, 128), 128)
        acc = pad[16 : 16 + rows, lanes]
        for phase in range(8):
            shifted = pad[phase : phase + rows + 24, lanes]
            for j in range(count):
                at = 16 + reach - j if flip else 16 - reach + j
                if at % 8 == phase:
                    acc = acc + taps[j : j + 1, lanes] * shifted[at - phase : at - phase + rows]
        out[:, lanes] = acc.astype(out.dtype)
        return 0

    lax.fori_loop(0, out.shape[1] // 128, chunk, 0)


def send_kernel(idx, sharp, left, own, right, taps, qhat, wf, o0, o1, o2, o3, gres_o, pad, g_s, gres, *, hs):
    fill_pad(pad, left, own, right)
    conv_rows(pad, taps, gres, own.shape[0], True)
    gres_o[...] = gres[...]
    gt = dotf(wf[...], gres[...].astype(BF16), 1, 1).astype(BF16)
    for h in range(4):
        g_s[h, 0:hs] = (qhat[h * hs : (h + 1) * hs] * (sharp[h] / math.sqrt(hs))).astype(BF16)
        g_s[h, hs : 2 * hs] = gt[h * hs : (h + 1) * hs]
    for s, o in enumerate((o0, o1, o2, o3)):
        o[...] = g_s[lax.rem(idx[0] + s, 4)]


def tail_kernel(
    core, part, other, x, factor, left, own, right, gres_hbm, res_o, sig_o, sums, first, last, pad, resf, gain, gres, sem,
    *, rows, taps, red,
):
    fetch = pltpu.make_async_copy(gres_hbm, gres, sem)
    fetch.start()
    fill_pad(pad, left, own, right)
    reach = taps // 2
    total = part[0:rows].astype(F32) + other[0:rows].astype(F32)
    xf = x[...].astype(F32)
    residual = (xf + total).astype(BF16)
    res_o[...] = residual
    first[...] = residual[:reach]
    last[...] = residual[rows - reach :]
    resf[...] = residual.astype(F32)
    centred = xf - jnp.mean(xf, axis=-1, keepdims=True)
    var = jnp.mean(centred * centred, axis=-1, keepdims=True)
    inv = 1.0 / jnp.sqrt(var + 1e-05)
    unit = centred * inv
    grad = part[rows : 2 * rows].astype(F32) + other[rows : 2 * rows].astype(F32)
    prod = grad * unit
    gain[...] = jnp.sum(prod, axis=0, keepdims=True)
    f = factor[...]
    scaled = grad * f
    m1 = jnp.mean(scaled, axis=-1, keepdims=True)
    m2 = jnp.mean(prod * f, axis=-1, keepdims=True)
    fetch.wait()
    sig_o[...] = (gres[...] + (scaled - m1 - unit * m2) * inv).astype(BF16)
    half = sums.shape[2] // 128

    @pl.when(core[0] == red)
    def _():
        for h in range(2):

            def chunk(c, _):
                lanes = pl.ds(pl.multiple_of((h * half + c) * 128, 128), 128)
                to = pl.ds(pl.multiple_of(c * 128, 128), 128)
                r = resf[:, lanes]
                for phase in range(8):
                    shifted = pad[phase : phase + rows + 24, lanes]
                    for j in range(taps):
                        at = 16 + reach - j
                        if at % 8 == phase:
                            moved = shifted[at - phase : at - phase + rows]
                            sums[h, j : j + 1, to] = jnp.sum(r * moved, axis=0, keepdims=True)
                sums[h, taps : taps + 1, to] = gain[:, lanes]
                return 0

            lax.fori_loop(0, half, chunk, 0)

    @pl.when(core[0] != red)
    def _():
        sums[...] = jnp.zeros(sums.shape, F32)


def out_kernel(core, left, own, right, taps, out, pad):
    @pl.when(core[0] == 0)
    def _():
        fill_pad(pad, left, own, right)
        conv_rows(pad, taps, out, own.shape[0], False)

    @pl.when(core[0] != 0)
    def _():
        out[...] = jnp.zeros(out.shape, BF16)


def to_rows(a):
    return a.astype(F32).T.astype(BF16)


def rows_kernel(*refs, hs):
    kv = refs[0:4]
    qg = refs[4:8]
    te, acc = refs[8:10]
    kn, vn, qgs = refs[10:]
    span = kv[0].shape[1]
    for r in range(4):
        kn[r] = to_rows(kv[r][0:hs])
        vn[r] = to_rows(kv[r][hs : 2 * hs])
        qgs[r] = qg[r][...]

    def over_q(j, _):
        qt = qgs[j, 0:hs]
        gt = qgs[j, hs : 2 * hs]
        tot = jnp.zeros((8, span), F32)
        exp = jnp.zeros((8, span), F32)
        low = jnp.zeros((2 * hs, span), F32)
        high = jnp.zeros((hs, span), F32)
        for r in range(4):
            w = jnp.exp(dotf(kn[r], qt))
            wp = w * dotf(vn[r], gt)
            tot = tot + jnp.sum(w.reshape(span // 8, 8, span), axis=0)
            exp = exp + jnp.sum(wp.reshape(span // 8, 8, span), axis=0)
            low = low + dotf(kv[r][...], w.astype(BF16))
            high = high + dotf(kv[r][0:hs], wp.astype(BF16))
        acc[j, 0 : 2 * hs] = low
        acc[j, 2 * hs : 3 * hs] = high
        te[j, 0:1] = jnp.sum(tot, axis=0, keepdims=True)
        te[j, 1:2] = jnp.sum(exp, axis=0, keepdims=True)
        return 0

    lax.fori_loop(0, 4, over_q, 0)


def norm_kernel(te0, te1, acc, *rows, hs):
    for r in range(4):
        t = te0[r] + te1[r ^ 2]
        inv = 1.0 / t[0:1]
        delta = t[1:2] * inv
        rows[r][0:hs] = (acc[r, hs : 2 * hs] * inv).astype(BF16)
        rows[r][hs : 2 * hs] = ((acc[r, 2 * hs : 3 * hs] - delta * acc[r, 0:hs]) * inv).astype(BF16)


def cols_kernel(*refs, hs):
    te = refs[0:2]
    kv = refs[2:6]
    qg = refs[6:10]
    cols = refs[10:14]
    kn, vn, qn, gn, inv, dlt, colacc = refs[14:]
    span = kv[0].shape[1]
    for r in range(4):
        kn[r] = to_rows(kv[r][0:hs])
        vn[r] = to_rows(kv[r][hs : 2 * hs])
        qn[r] = to_rows(qg[r][0:hs])
        gn[r] = to_rows(qg[r][hs : 2 * hs])
        t = te[0][r] + te[1][r ^ 2]
        one = 1.0 / t[0:1]
        inv[r] = one
        dlt[r] = t[1:2] * one

    def over_k(b, _):
        k = kn[b]
        v = vn[b]
        gk = jnp.zeros((span, hs), F32)
        gv = jnp.zeros((span, hs), F32)
        for j in range(4):
            prob = jnp.exp(dotf(k, qg[j][0:hs])) * inv[j]
            slope = prob * (dotf(v, qg[j][hs : 2 * hs]) - dlt[j])
            gv = gv + dotf(prob.astype(BF16), gn[j])
            gk = gk + dotf(slope.astype(BF16), qn[j])
        colacc[b, 0:hs] = gk.T.astype(BF16)
        colacc[b, hs : 2 * hs] = gv.T.astype(BF16)
        return 0

    lax.fori_loop(0, 4, over_k, 0)
    for r in range(4):
        cols[r][...] = colacc[r]


def run_rows(kv, qg, hs, span):
    nat = pltpu.VMEM((4, span, hs), BF16)
    return vcall(
        functools.partial(rows_kernel, hs=hs),
        (jax.ShapeDtypeStruct((4, 2, span), F32), jax.ShapeDtypeStruct((4, 3 * hs, span), F32)),
        scratch=[nat, nat, pltpu.VMEM((4, 2 * hs, span), BF16)],
        n_in=8,
    )(*kv, *qg)


def run_cols(te, kv, qg, hs, span):
    nat = pltpu.VMEM((4, span, hs), BF16)
    row = pltpu.VMEM((4, 1, span), F32)
    return vcall(
        functools.partial(cols_kernel, hs=hs),
        tuple(jax.ShapeDtypeStruct((2 * hs, span), BF16) for _ in range(4)),
        scratch=[nat, nat, nat, nat, row, row, pltpu.VMEM((4, 2 * hs, span), BF16)],
        n_in=10,
    )(*te, *kv, *qg)


def sum_kernel(*refs, hs):
    row = refs[0][...].astype(F32)
    col = refs[4][...].astype(F32)
    for i in range(1, 4):
        row = row + refs[i][...].astype(F32)
        col = col + refs[4 + i][...].astype(F32)
    row = row.astype(BF16)
    col = col.astype(BF16)
    lanes = row.shape[1] // 4
    for s in range(4):
        refs[8 + s][0 : 2 * hs] = row[:, s * lanes : (s + 1) * lanes]
        refs[8 + s][2 * hs : 4 * hs] = col[:, s * lanes : (s + 1) * lanes]


def back_kernel(idx, sharp, b0, b1, b2, b3, qhat, khat, rad, wf, w, out, home, att, qgr, kgr, vgr, *, heads, hs):
    for s, b in enumerate((b0, b1, b2, b3)):
        home[lax.rem(idx[0] + s, 4)] = b[...]
    lanes = b0.shape[1]
    for h in range(heads):
        lo, hi = h * hs, (h + 1) * hs
        att[lo:hi] = home[h, 0:hs].astype(F32)
        gq = home[h, hs : 2 * hs].astype(F32) * (sharp[h] / math.sqrt(hs))
        gk = home[h, 2 * hs : 3 * hs].astype(F32)
        vgr[lo:hi] = home[h, 3 * hs : 4 * hs].astype(F32)
        qh = qhat[lo:hi]
        kh = khat[lo:hi]
        qgr[lo:hi] = (gq - qh * jnp.mean(gq * qh, axis=0, keepdims=True)) / rad[h : h + 1]
        kgr[lo:hi] = (gk - kh * jnp.mean(gk * kh, axis=0, keepdims=True)) / rad[heads + h : heads + h + 1]
    out[0:lanes] = dotf(att[...].T.astype(BF16), wf[...]).astype(BF16)
    normed = dotf(qgr[...].T.astype(BF16), w[0], 1, 1)
    normed = normed + dotf(kgr[...].T.astype(BF16), w[1], 1, 1)
    normed = normed + dotf(vgr[...].T.astype(BF16), w[2], 1, 1)
    out[lanes : 2 * lanes] = normed.astype(BF16)


def rims(cells, head, tail, core=None):
    ends = TM - 1
    left = send(tail, "tm", [(i, i + 1) for i in range(ends)], core)
    right = send(head, "tm", [(i + 1, i) for i in range(ends)], core)
    return left, cells, right


def pieces(a, n):
    width = a.shape[1] // n
    return lambda i: lax.dynamic_slice_in_dim(a, i * width, width, axis=1)


def scatter_sum(a, batches, core):
    t = lax.axis_index("tm")
    z4, z2, x, yh = t // 16, (t // 8) % 2, (t // 2) % 4, t % 2
    if batches > 1:
        b = lax.axis_index("batch")
        away = lax.dynamic_index_in_dim(a, 1 - b, 0, keepdims=False)
        got = send(away, "batch", [(0, 1), (1, 0)], core)
        a = lax.dynamic_index_in_dim(a, b, 0, keepdims=False) + got
    else:
        a = jnp.concatenate([a[0], a[1]], axis=1)
    at = pieces(a, 4)
    got = ordered(lambda s: move_z4(at((z4 + s) % 4), s, core), (2, 1, 3))
    a = (at(z4) + got[0]) + (got[1] + got[2])
    at = pieces(a, 2)
    a = at(z2) + move_zy(at(1 - z2), 1, core)
    at = pieces(a, 4)
    got = ordered(lambda s: move_x(at((x + s) % 4), s, core), (2, 1, 3))
    a = (at(x) + got[0]) + (got[1] + got[2])
    at = pieces(a, 2)
    return at(yh) + move_zy(at(1 - yh), 2, core)


def step(input_signal, standardize_factor, triple_projection, score_sharpening, final_projection, filter_taps, mixture_adjoint, *, batches, mps):
    rows, width = input_signal.shape[1:]
    heads = score_sharpening.shape[0]
    hs = triple_projection.shape[2] // heads
    flat = heads * hs
    taps = filter_taps.shape[0]
    reach = taps // 2
    t = lax.axis_index("tm")
    z4 = (t // 16).astype(jnp.int32).reshape(1)
    x_in = input_signal[0]
    adj = mixture_adjoint[0]
    factor = standardize_factor[None]
    shape = jax.ShapeDtypeStruct
    adj_rims = rims(adj, adj[:reach], adj[rows - reach :])
    piece = shape((2 * hs, rows), BF16)
    *sent_kv, qhat, khat, rad = vcall(
        functools.partial(front_kernel, heads=heads, hs=hs),
        (piece,) * 4 + (shape((flat, rows), F32), shape((flat, rows), F32), shape((2 * heads, rows), F32)),
        scratch=[
            pltpu.VMEM((heads, 2 * hs, rows), BF16),
            pltpu.VMEM((rows, width), BF16),
            pltpu.VMEM((3, width, flat), BF16),
            pltpu.SemaphoreType.DMA((4,)),
        ],
        smem=1,
        n_in=1,
        raw=2,
    )(z4, factor, x_in, triple_projection)
    got_kv = [sent_kv[0]] + ordered(lambda s: move_z4(sent_kv[s], s), (2, 1, 3))
    pad = pltpu.VMEM((rows + 32, width), F32)
    *sent_qg, grad_res = vcall(
        functools.partial(send_kernel, hs=hs),
        (piece,) * 4 + (shape((rows, width), F32),),
        scratch=[pad, pltpu.VMEM((4, 2 * hs, rows), BF16), pltpu.VMEM((rows, width), F32)],
        out_hbm=(4,),
        smem=2,
        n_in=6,
    )(z4, score_sharpening, *adj_rims, filter_taps, qhat, final_projection)
    got_qg = [sent_qg[0]] + ordered(lambda s: move_z4(sent_qg[s], s), (2, 1, 3))
    kv0 = jnp.concatenate(got_kv, axis=1)
    qg0 = jnp.concatenate(got_qg, axis=1)
    kv = [kv0] + ordered(lambda s: move_x(kv0, s), (2, 1, 3))
    qg = [qg0] + ordered(lambda m: move_zy(qg0, m), (3, 2, 1))
    span = 4 * rows
    te0, acc = run_rows(kv, qg, hs, span)
    te1 = move_zy(te0, 1)
    te1 = te0 + jnp.stack([te1[r ^ 1] for r in range(4)])
    te = [te1, move_zy(te1, 2)]
    rowp = vcall(functools.partial(norm_kernel, hs=hs), (shape((2 * hs, span), BF16),) * 4, n_in=3)(*te, acc)
    row = [rowp[0]] + ordered(lambda m: move_zy(rowp[m], m), (3, 2, 1))
    colp = run_cols(te, kv, qg, hs, span)
    col = [colp[0]] + ordered(lambda s: move_x(colp[s], -s), (2, 1, 3))
    home = vcall(
        functools.partial(sum_kernel, hs=hs),
        tuple(shape((4 * hs, rows), BF16) for _ in range(4)),
        n_in=8,
    )(*row, *col)
    back = [home[0]] + ordered(lambda s: move_z4(home[s], -s), (2, 1, 3))
    part = vcall(
        functools.partial(back_kernel, heads=heads, hs=hs),
        shape((2 * rows, width), BF16),
        scratch=[pltpu.VMEM((4, 4 * hs, rows), BF16)] + [pltpu.VMEM((flat, rows), F32)] * 4,
        smem=2,
        n_in=9,
    )(z4, score_sharpening, *back, qhat, khat, rad, final_projection, triple_projection)
    other = lax.ppermute(part, "mp", [(0, 1), (1, 0)]) if mps > 1 else jnp.zeros_like(part)
    edge = shape((reach, width), BF16)
    core = lax.axis_index("mp").astype(jnp.int32)
    red = mps - 1
    residual, signal_adjoint, sums, first, last = vcall(
        functools.partial(tail_kernel, rows=rows, taps=taps, red=red),
        (shape((rows, width), BF16), shape((rows, width), BF16), shape((2, taps + 1, width // 2), F32), edge, edge),
        scratch=[
            pad,
            pltpu.VMEM((rows, width), F32),
            pltpu.VMEM((1, width), F32),
            pltpu.VMEM((rows, width), F32),
            pltpu.SemaphoreType.DMA(()),
        ],
        smem=1,
        n_in=7,
        raw=1,
        out_hbm=(1,),
    )(core.reshape(1), part, other, x_in, factor, *adj_rims, grad_res)
    res_rims = rims(residual, first, last, 0)
    result = vcall(out_kernel, shape((rows, width), BF16), scratch=[pad], smem=1, n_in=4)(
        core.reshape(1), *res_rims, filter_taps
    )
    sums = scatter_sum(sums, batches, red)
    if mps > 1:
        moved = lax.ppermute(result, "mp", [(0, 1)])
        result = jnp.where(core == 0, result, moved)
        moved = lax.ppermute(sums, "mp", [(1, 0)])
        sums = jnp.where(core == 1, sums, moved)
    return (result[None], signal_adjoint[None], sums[:taps], sums[taps])


def solution(mesh):
    call = mapped(mesh)
    return call


def mapped(mesh):
    return jax.shard_map(
        functools.partial(step, batches=mesh.shape["batch"], mps=mesh.shape["mp"]),
        mesh=mesh,
        in_specs=(
            P("batch", "tm", None),
            P(),
            P(None, None, "mp"),
            P("mp"),
            P("mp", None),
            P(),
            P("batch", "tm", None),
        ),
        out_specs=(
            P("batch", "tm", None),
            P("batch", "tm", None),
            P(None, ("batch", "tm")),
            P(("batch", "tm")),
        ),
        check_vma=False,
    )
```

```python
import functools
import math

import jax
import jax.numpy as jnp
from jax import lax
from jax.experimental import pallas as pl
from jax.experimental.pallas import tpu as pltpu
from jax.sharding import PartitionSpec as P


INTERPRET = False
LIMIT = 24 * 1024 * 1024
TM = 64
F32 = jnp.float32
BF16 = jnp.bfloat16


def _split(t):
    return t // 16, (t // 8) % 2, (t // 2) % 4, t % 2


def _join(z4, z2, x, yh):
    return ((z4 % 4) * 2 + z2) * 8 + (x % 4) * 2 + yh


def send(a, axis, pairs, core=None):
    if core is None:
        return lax.ppermute(a, axis, pairs)
    cores = lax.axis_size("mp")
    steps = [(i * cores + c, (j if c == core else i) * cores + c) for i, j in pairs for c in range(cores)]
    return lax.ppermute(a, (axis, "mp"), steps)


def move_z4(a, s, core=None):
    pairs = []
    for t in range(TM):
        z4, z2, x, yh = _split(t)
        pairs.append((t, _join(z4 + s, z2, x, yh)))
    return send(a, "tm", pairs, core)


def move_x(a, s, core=None):
    pairs = []
    for t in range(TM):
        z4, z2, x, yh = _split(t)
        pairs.append((t, _join(z4, z2, x + s, yh)))
    return send(a, "tm", pairs, core)


def move_zy(a, m, core=None):
    pairs = []
    for t in range(TM):
        z4, z2, x, yh = _split(t)
        pairs.append((t, _join(z4, z2 ^ (m & 1), x, yh ^ (m >> 1))))
    return send(a, "tm", pairs, core)


def ordered(move, shifts):
    got = {s: move(s) for s in shifts}
    return [got[s] for s in (1, 2, 3)]


def vcall(kernel, out_shape, scratch=(), smem=0, n_in=0, raw=0, out_hbm=()):
    space = [pl.BlockSpec(memory_space=pltpu.SMEM)] * smem
    space += [pl.BlockSpec(memory_space=pltpu.VMEM)] * n_in
    space += [pl.BlockSpec(memory_space=pltpu.HBM if not INTERPRET else pl.ANY)] * raw
    flat, tree = jax.tree.flatten(out_shape)
    held = flat
    if not INTERPRET:
        held = [o if i in out_hbm else pltpu.VMEM(o.shape, o.dtype) for i, o in enumerate(flat)]
    call = pl.pallas_call(
        kernel,
        out_shape=jax.tree.unflatten(tree, held),
        in_specs=space,
        out_specs=jax.tree.unflatten(tree, [pl.BlockSpec(memory_space=pltpu.VMEM)] * len(flat)),
        scratch_shapes=list(scratch),
        compiler_params=pltpu.CompilerParams(vmem_limit_bytes=LIMIT),
        interpret=INTERPRET,
    )

    def run(*args):
        if not INTERPRET:
            args = [
                a if i < smem else pltpu.with_memory_space_constraint(a, pltpu.VMEM if i < smem + n_in else pltpu.HBM)
                for i, a in enumerate(args)
            ]
        return call(*args)

    return run


def dotf(a, b, ca=1, cb=0):
    if INTERPRET:
        a, b = a.astype(F32), b.astype(F32)
    return lax.dot_general(a, b, (((ca,), (cb,)), ((), ())), preferred_element_type=F32)


def front_kernel(
    idx, factor, x_hbm, w_hbm, o0, o1, o2, o3, qhat_o, khat_o, rad_o, pay, x, w, sem, *, heads, hs
):
    x_copy = pltpu.make_async_copy(x_hbm, x, sem.at[0])
    x_copy.start()
    copies = [pltpu.make_async_copy(w_hbm.at[i], w.at[i], sem.at[1 + i]) for i in range(3)]
    for i in (1, 2, 0):
        copies[i].start()
    x_copy.wait()
    xf = x[...].astype(F32)
    centred = xf - jnp.mean(xf, axis=-1, keepdims=True)
    var = jnp.mean(centred * centred, axis=-1, keepdims=True)
    unit = centred * (1.0 / jnp.sqrt(var + 1e-05))
    normed = (unit * factor[...]).astype(BF16)
    copies[1].wait()
    kt = dotf(normed, w[1]).T
    copies[2].wait()
    vt = dotf(normed, w[2]).T
    copies[0].wait()
    qt = dotf(normed, w[0]).T
    for h in range(heads):
        lo, hi = h * hs, (h + 1) * hs
        q = qt[lo:hi]
        k = kt[lo:hi]
        qr = jnp.sqrt(jnp.mean(q * q, axis=0, keepdims=True) + 1e-06)
        kr = jnp.sqrt(jnp.mean(k * k, axis=0, keepdims=True) + 1e-06)
        qh = q / qr
        kh = k / kr
        qhat_o[lo:hi] = qh
        khat_o[lo:hi] = kh
        rad_o[h : h + 1] = qr
        rad_o[heads + h : heads + h + 1] = kr
        pay[h, 0:hs] = kh.astype(BF16)
        pay[h, hs : 2 * hs] = vt[lo:hi].astype(BF16)
    for s, o in enumerate((o0, o1, o2, o3)):
        o[...] = pay[lax.rem(idx[0] + s, 4)]


def fill_pad(pad, left, own, right, place):
    reach = left.shape[0]
    rows = own.shape[0]
    pad[16 - reach : 16] = jnp.where(place > 0, left[...].astype(F32), 0.0)
    pad[16 : 16 + rows] = own[...].astype(F32)
    pad[16 + rows : 16 + rows + reach] = jnp.where(place < TM - 1, right[...].astype(F32), 0.0)


def conv_rows(pad, taps, out, rows, flip):
    count = taps.shape[0]
    reach = count // 2

    def chunk(c, _):
        lanes = pl.ds(pl.multiple_of(c * 128, 128), 128)
        acc = pad[16 : 16 + rows, lanes]
        for phase in range(8):
            shifted = pad[phase : phase + rows + 24, lanes]
            for j in range(count):
                at = 16 + reach - j if flip else 16 - reach + j
                if at % 8 == phase:
                    acc = acc + taps[j : j + 1, lanes] * shifted[at - phase : at - phase + rows]
        out[:, lanes] = acc.astype(out.dtype)
        return 0

    lax.fori_loop(0, out.shape[1] // 128, chunk, 0)


def send_kernel(idx, place, sharp, left, own, right, taps, qhat, wf, o0, o1, o2, o3, gres_o, pad, g_s, gres, *, hs):
    fill_pad(pad, left, own, right, place[0])
    conv_rows(pad, taps, gres, own.shape[0], True)
    gres_o[...] = gres[...]
    gt = dotf(wf[...], gres[...].astype(BF16), 1, 1).astype(BF16)
    for h in range(4):
        g_s[h, 0:hs] = (qhat[h * hs : (h + 1) * hs] * (sharp[h] / math.sqrt(hs))).astype(BF16)
        g_s[h, hs : 2 * hs] = gt[h * hs : (h + 1) * hs]
    for s, o in enumerate((o0, o1, o2, o3)):
        o[...] = g_s[lax.rem(idx[0] + s, 4)]


def tail_kernel(
    core, place, part, other, x, factor, left, own, right, gres_hbm, res_o, sig_o, sums, first, last, pad, resf, gain, gres, sem,
    *, rows, taps, red,
):
    fetch = pltpu.make_async_copy(gres_hbm, gres, sem)
    fetch.start()
    fill_pad(pad, left, own, right, place[0])
    reach = taps // 2
    total = part[0:rows].astype(F32) + other[0:rows].astype(F32)
    xf = x[...].astype(F32)
    residual = (xf + total).astype(BF16)
    res_o[...] = residual
    first[...] = residual[:reach]
    last[...] = residual[rows - reach :]
    resf[...] = residual.astype(F32)
    centred = xf - jnp.mean(xf, axis=-1, keepdims=True)
    var = jnp.mean(centred * centred, axis=-1, keepdims=True)
    inv = 1.0 / jnp.sqrt(var + 1e-05)
    unit = centred * inv
    grad = part[rows : 2 * rows].astype(F32) + other[rows : 2 * rows].astype(F32)
    prod = grad * unit
    gain[...] = jnp.sum(prod, axis=0, keepdims=True)
    f = factor[...]
    scaled = grad * f
    m1 = jnp.mean(scaled, axis=-1, keepdims=True)
    m2 = jnp.mean(prod * f, axis=-1, keepdims=True)
    fetch.wait()
    sig_o[...] = (gres[...] + (scaled - m1 - unit * m2) * inv).astype(BF16)
    half = sums.shape[2] // 128

    @pl.when(core[0] == red)
    def _():
        for h in range(2):

            def chunk(c, _):
                lanes = pl.ds(pl.multiple_of((h * half + c) * 128, 128), 128)
                to = pl.ds(pl.multiple_of(c * 128, 128), 128)
                r = resf[:, lanes]
                for phase in range(8):
                    shifted = pad[phase : phase + rows + 24, lanes]
                    for j in range(taps):
                        at = 16 + reach - j
                        if at % 8 == phase:
                            moved = shifted[at - phase : at - phase + rows]
                            sums[h, j : j + 1, to] = jnp.sum(r * moved, axis=0, keepdims=True)
                sums[h, taps : taps + 1, to] = gain[:, lanes]
                return 0

            lax.fori_loop(0, half, chunk, 0)

    @pl.when(core[0] != red)
    def _():
        sums[...] = jnp.zeros(sums.shape, F32)


def out_kernel(core, place, left, own, right, taps, out, pad):
    @pl.when(core[0] == 0)
    def _():
        fill_pad(pad, left, own, right, place[0])
        conv_rows(pad, taps, out, own.shape[0], False)

    @pl.when(core[0] != 0)
    def _():
        out[...] = jnp.zeros(out.shape, BF16)


def to_rows(a):
    return a.astype(F32).T.astype(BF16)


def rows_kernel(*refs, hs):
    kv = refs[0:4]
    qg = refs[4:8]
    te, acc = refs[8:10]
    kn, vn, qgs = refs[10:]
    span = kv[0].shape[1]
    for r in range(4):
        kn[r] = to_rows(kv[r][0:hs])
        vn[r] = to_rows(kv[r][hs : 2 * hs])
        qgs[r] = qg[r][...]

    def over_q(j, _):
        qt = qgs[j, 0:hs]
        gt = qgs[j, hs : 2 * hs]
        tot = jnp.zeros((8, span), F32)
        exp = jnp.zeros((8, span), F32)
        low = jnp.zeros((2 * hs, span), F32)
        high = jnp.zeros((hs, span), F32)
        for r in range(4):
            w = jnp.exp(dotf(kn[r], qt))
            wp = w * dotf(vn[r], gt)
            tot = tot + jnp.sum(w.reshape(span // 8, 8, span), axis=0)
            exp = exp + jnp.sum(wp.reshape(span // 8, 8, span), axis=0)
            low = low + dotf(kv[r][...], w.astype(BF16))
            high = high + dotf(kv[r][0:hs], wp.astype(BF16))
        acc[j, 0 : 2 * hs] = low
        acc[j, 2 * hs : 3 * hs] = high
        te[j, 0:1] = jnp.sum(tot, axis=0, keepdims=True)
        te[j, 1:2] = jnp.sum(exp, axis=0, keepdims=True)
        return 0

    lax.fori_loop(0, 4, over_q, 0)


def norm_kernel(te0, te1, acc, *rows, hs):
    for r in range(4):
        t = te0[r] + te1[r ^ 2]
        inv = 1.0 / t[0:1]
        delta = t[1:2] * inv
        rows[r][0:hs] = (acc[r, hs : 2 * hs] * inv).astype(BF16)
        rows[r][hs : 2 * hs] = ((acc[r, 2 * hs : 3 * hs] - delta * acc[r, 0:hs]) * inv).astype(BF16)


def cols_kernel(*refs, hs):
    te = refs[0:2]
    kv = refs[2:6]
    qg = refs[6:10]
    cols = refs[10:14]
    kn, vn, qn, gn, inv, dlt, colacc = refs[14:]
    span = kv[0].shape[1]
    for r in range(4):
        kn[r] = to_rows(kv[r][0:hs])
        vn[r] = to_rows(kv[r][hs : 2 * hs])
        qn[r] = to_rows(qg[r][0:hs])
        gn[r] = to_rows(qg[r][hs : 2 * hs])
        t = te[0][r] + te[1][r ^ 2]
        one = 1.0 / t[0:1]
        inv[r] = one
        dlt[r] = t[1:2] * one

    def over_k(b, _):
        k = kn[b]
        v = vn[b]
        gk = jnp.zeros((span, hs), F32)
        gv = jnp.zeros((span, hs), F32)
        for j in range(4):
            prob = jnp.exp(dotf(k, qg[j][0:hs])) * inv[j]
            slope = prob * (dotf(v, qg[j][hs : 2 * hs]) - dlt[j])
            gv = gv + dotf(prob.astype(BF16), gn[j])
            gk = gk + dotf(slope.astype(BF16), qn[j])
        colacc[b, 0:hs] = gk.T.astype(BF16)
        colacc[b, hs : 2 * hs] = gv.T.astype(BF16)
        return 0

    lax.fori_loop(0, 4, over_k, 0)
    for r in range(4):
        cols[r][...] = colacc[r]


def run_rows(kv, qg, hs, span):
    nat = pltpu.VMEM((4, span, hs), BF16)
    return vcall(
        functools.partial(rows_kernel, hs=hs),
        (jax.ShapeDtypeStruct((4, 2, span), F32), jax.ShapeDtypeStruct((4, 3 * hs, span), F32)),
        scratch=[nat, nat, pltpu.VMEM((4, 2 * hs, span), BF16)],
        n_in=8,
    )(*kv, *qg)


def run_cols(te, kv, qg, hs, span):
    nat = pltpu.VMEM((4, span, hs), BF16)
    row = pltpu.VMEM((4, 1, span), F32)
    return vcall(
        functools.partial(cols_kernel, hs=hs),
        tuple(jax.ShapeDtypeStruct((2 * hs, span), BF16) for _ in range(4)),
        scratch=[nat, nat, nat, nat, row, row, pltpu.VMEM((4, 2 * hs, span), BF16)],
        n_in=10,
    )(*te, *kv, *qg)


def sum_kernel(*refs, hs):
    row = refs[0][...].astype(F32)
    col = refs[4][...].astype(F32)
    for i in range(1, 4):
        row = row + refs[i][...].astype(F32)
        col = col + refs[4 + i][...].astype(F32)
    row = row.astype(BF16)
    col = col.astype(BF16)
    lanes = row.shape[1] // 4
    for s in range(4):
        refs[8 + s][0 : 2 * hs] = row[:, s * lanes : (s + 1) * lanes]
        refs[8 + s][2 * hs : 4 * hs] = col[:, s * lanes : (s + 1) * lanes]


def back_kernel(idx, sharp, b0, b1, b2, b3, qhat, khat, rad, wf, w, out, home, att, qgr, kgr, vgr, *, heads, hs):
    for s, b in enumerate((b0, b1, b2, b3)):
        home[lax.rem(idx[0] + s, 4)] = b[...]
    lanes = b0.shape[1]
    for h in range(heads):
        lo, hi = h * hs, (h + 1) * hs
        att[lo:hi] = home[h, 0:hs].astype(F32)
        gq = home[h, hs : 2 * hs].astype(F32) * (sharp[h] / math.sqrt(hs))
        gk = home[h, 2 * hs : 3 * hs].astype(F32)
        vgr[lo:hi] = home[h, 3 * hs : 4 * hs].astype(F32)
        qh = qhat[lo:hi]
        kh = khat[lo:hi]
        qgr[lo:hi] = (gq - qh * jnp.mean(gq * qh, axis=0, keepdims=True)) / rad[h : h + 1]
        kgr[lo:hi] = (gk - kh * jnp.mean(gk * kh, axis=0, keepdims=True)) / rad[heads + h : heads + h + 1]
    out[0:lanes] = dotf(att[...].T.astype(BF16), wf[...]).astype(BF16)
    normed = dotf(qgr[...].T.astype(BF16), w[0], 1, 1)
    normed = normed + dotf(kgr[...].T.astype(BF16), w[1], 1, 1)
    normed = normed + dotf(vgr[...].T.astype(BF16), w[2], 1, 1)
    out[lanes : 2 * lanes] = normed.astype(BF16)


def rims(cells, head, tail, core=None):
    left = send(tail, "tm", [(i, (i + 1) % TM) for i in range(TM)], core)
    right = send(head, "tm", [((i + 1) % TM, i) for i in range(TM)], core)
    return left, cells, right


def pieces(a, n):
    width = a.shape[1] // n
    return lambda i: lax.dynamic_slice_in_dim(a, i * width, width, axis=1)


def scatter_sum(a, batches, core):
    t = lax.axis_index("tm")
    z4, z2, x, yh = t // 16, (t // 8) % 2, (t // 2) % 4, t % 2
    if batches > 1:
        b = lax.axis_index("batch")
        away = lax.dynamic_index_in_dim(a, 1 - b, 0, keepdims=False)
        got = send(away, "batch", [(0, 1), (1, 0)], core)
        a = lax.dynamic_index_in_dim(a, b, 0, keepdims=False) + got
    else:
        a = jnp.concatenate([a[0], a[1]], axis=1)
    at = pieces(a, 4)
    got = ordered(lambda s: move_z4(at((z4 + s) % 4), s, core), (2, 1, 3))
    a = (at(z4) + got[0]) + (got[1] + got[2])
    at = pieces(a, 2)
    a = at(z2) + move_zy(at(1 - z2), 1, core)
    at = pieces(a, 4)
    got = ordered(lambda s: move_x(at((x + s) % 4), s, core), (2, 1, 3))
    a = (at(x) + got[0]) + (got[1] + got[2])
    at = pieces(a, 2)
    return at(yh) + move_zy(at(1 - yh), 2, core)


def step(input_signal, standardize_factor, triple_projection, score_sharpening, final_projection, filter_taps, mixture_adjoint, *, batches, mps):
    rows, width = input_signal.shape[1:]
    heads = score_sharpening.shape[0]
    hs = triple_projection.shape[2] // heads
    flat = heads * hs
    taps = filter_taps.shape[0]
    reach = taps // 2
    t = lax.axis_index("tm")
    z4 = (t // 16).astype(jnp.int32).reshape(1)
    place = t.astype(jnp.int32).reshape(1)
    x_in = input_signal[0]
    adj = mixture_adjoint[0]
    factor = standardize_factor[None]
    shape = jax.ShapeDtypeStruct
    adj_rims = rims(adj, adj[:reach], adj[rows - reach :])
    piece = shape((2 * hs, rows), BF16)
    *sent_kv, qhat, khat, rad = vcall(
        functools.partial(front_kernel, heads=heads, hs=hs),
        (piece,) * 4 + (shape((flat, rows), F32), shape((flat, rows), F32), shape((2 * heads, rows), F32)),
        scratch=[
            pltpu.VMEM((heads, 2 * hs, rows), BF16),
            pltpu.VMEM((rows, width), BF16),
            pltpu.VMEM((3, width, flat), BF16),
            pltpu.SemaphoreType.DMA((4,)),
        ],
        smem=1,
        n_in=1,
        raw=2,
    )(z4, factor, x_in, triple_projection)
    got_kv = [sent_kv[0]] + ordered(lambda s: move_z4(sent_kv[s], s), (2, 1, 3))
    pad = pltpu.VMEM((rows + 32, width), F32)
    *sent_qg, grad_res = vcall(
        functools.partial(send_kernel, hs=hs),
        (piece,) * 4 + (shape((rows, width), F32),),
        scratch=[pad, pltpu.VMEM((4, 2 * hs, rows), BF16), pltpu.VMEM((rows, width), F32)],
        out_hbm=(4,),
        smem=3,
        n_in=6,
    )(z4, place, score_sharpening, *adj_rims, filter_taps, qhat, final_projection)
    got_qg = [sent_qg[0]] + ordered(lambda s: move_z4(sent_qg[s], s), (2, 1, 3))
    kv0 = jnp.concatenate(got_kv, axis=1)
    qg0 = jnp.concatenate(got_qg, axis=1)
    kv = [kv0] + ordered(lambda s: move_x(kv0, s), (2, 1, 3))
    qg = [qg0] + ordered(lambda m: move_zy(qg0, m), (3, 2, 1))
    span = 4 * rows
    te0, acc = run_rows(kv, qg, hs, span)
    te1 = move_zy(te0, 1)
    te1 = te0 + jnp.stack([te1[r ^ 1] for r in range(4)])
    te = [te1, move_zy(te1, 2)]
    rowp = vcall(functools.partial(norm_kernel, hs=hs), (shape((2 * hs, span), BF16),) * 4, n_in=3)(*te, acc)
    row = [rowp[0]] + ordered(lambda m: move_zy(rowp[m], m), (3, 2, 1))
    colp = run_cols(te, kv, qg, hs, span)
    col = [colp[0]] + ordered(lambda s: move_x(colp[s], -s), (2, 1, 3))
    home = vcall(
        functools.partial(sum_kernel, hs=hs),
        tuple(shape((4 * hs, rows), BF16) for _ in range(4)),
        n_in=8,
    )(*row, *col)
    back = [home[0]] + ordered(lambda s: move_z4(home[s], -s), (2, 1, 3))
    part = vcall(
        functools.partial(back_kernel, heads=heads, hs=hs),
        shape((2 * rows, width), BF16),
        scratch=[pltpu.VMEM((4, 4 * hs, rows), BF16)] + [pltpu.VMEM((flat, rows), F32)] * 4,
        smem=2,
        n_in=9,
    )(z4, score_sharpening, *back, qhat, khat, rad, final_projection, triple_projection)
    other = lax.ppermute(part, "mp", [(0, 1), (1, 0)]) if mps > 1 else jnp.zeros_like(part)
    edge = shape((reach, width), BF16)
    core = lax.axis_index("mp").astype(jnp.int32)
    core_at = core.reshape(1)
    red = mps - 1
    residual, signal_adjoint, sums, first, last = vcall(
        functools.partial(tail_kernel, rows=rows, taps=taps, red=red),
        (shape((rows, width), BF16), shape((rows, width), BF16), shape((2, taps + 1, width // 2), F32), edge, edge),
        scratch=[
            pad,
            pltpu.VMEM((rows, width), F32),
            pltpu.VMEM((1, width), F32),
            pltpu.VMEM((rows, width), F32),
            pltpu.SemaphoreType.DMA(()),
        ],
        smem=2,
        n_in=7,
        raw=1,
        out_hbm=(1,),
    )(core_at, place, part, other, x_in, factor, *adj_rims, grad_res)
    res_rims = rims(residual, first, last, 0)
    result = vcall(out_kernel, shape((rows, width), BF16), scratch=[pad], smem=2, n_in=4)(
        core_at, place, *res_rims, filter_taps
    )
    sums = scatter_sum(sums, batches, red)
    if mps > 1:
        moved = lax.ppermute(result, "mp", [(0, 1), (1, 0)])
        result = jnp.where(core == 0, result, moved)
        moved = lax.ppermute(sums, "mp", [(0, 1), (1, 0)])
        sums = jnp.where(core == 1, sums, moved)
    return (result[None], signal_adjoint[None], sums[:taps], sums[taps])


def solution(mesh):
    call = mapped(mesh)
    return call


def mapped(mesh):
    return jax.shard_map(
        functools.partial(step, batches=mesh.shape["batch"], mps=mesh.shape["mp"]),
        mesh=mesh,
        in_specs=(
            P("batch", "tm", None),
            P(),
            P(None, None, "mp"),
            P("mp"),
            P("mp", None),
            P(),
            P("batch", "tm", None),
        ),
        out_specs=(
            P("batch", "tm", None),
            P("batch", "tm", None),
            P(None, ("batch", "tm")),
            P(("batch", "tm")),
        ),
        check_vma=False,
    )
```

```python
import functools
import math

import jax
import jax.numpy as jnp
from jax import lax
from jax.experimental import pallas as pl
from jax.experimental.pallas import tpu as pltpu
from jax.sharding import PartitionSpec as P


INTERPRET = False
LIMIT = 24 * 1024 * 1024
TM = 64
F32 = jnp.float32
BF16 = jnp.bfloat16


def _split(t):
    return t // 16, (t // 8) % 2, (t // 2) % 4, t % 2


def _join(z4, z2, x, yh):
    return ((z4 % 4) * 2 + z2) * 8 + (x % 4) * 2 + yh


def move_z4(a, s):
    pairs = []
    for t in range(TM):
        z4, z2, x, yh = _split(t)
        pairs.append((t, _join(z4 + s, z2, x, yh)))
    return lax.ppermute(a, "tm", pairs)


def move_x(a, s):
    pairs = []
    for t in range(TM):
        z4, z2, x, yh = _split(t)
        pairs.append((t, _join(z4, z2, x + s, yh)))
    return lax.ppermute(a, "tm", pairs)


def move_zy(a, m):
    pairs = []
    for t in range(TM):
        z4, z2, x, yh = _split(t)
        pairs.append((t, _join(z4, z2 ^ (m & 1), x, yh ^ (m >> 1))))
    return lax.ppermute(a, "tm", pairs)


def ordered(move, shifts):
    got = {s: move(s) for s in shifts}
    return [got[s] for s in (1, 2, 3)]


def vcall(kernel, out_shape, scratch=(), smem=0, n_in=0, raw=0, out_hbm=()):
    space = [pl.BlockSpec(memory_space=pltpu.SMEM)] * smem
    space += [pl.BlockSpec(memory_space=pltpu.VMEM)] * n_in
    space += [pl.BlockSpec(memory_space=pltpu.HBM if not INTERPRET else pl.ANY)] * raw
    flat, tree = jax.tree.flatten(out_shape)
    held = flat
    if not INTERPRET:
        held = [o if i in out_hbm else pltpu.VMEM(o.shape, o.dtype) for i, o in enumerate(flat)]
    call = pl.pallas_call(
        kernel,
        out_shape=jax.tree.unflatten(tree, held),
        in_specs=space,
        out_specs=jax.tree.unflatten(tree, [pl.BlockSpec(memory_space=pltpu.VMEM)] * len(flat)),
        scratch_shapes=list(scratch),
        compiler_params=pltpu.CompilerParams(vmem_limit_bytes=LIMIT),
        interpret=INTERPRET,
    )

    def run(*args):
        if not INTERPRET:
            args = [
                a if i < smem else pltpu.with_memory_space_constraint(a, pltpu.VMEM if i < smem + n_in else pltpu.HBM)
                for i, a in enumerate(args)
            ]
        return call(*args)

    return run


def dotf(a, b, ca=1, cb=0):
    if INTERPRET:
        a, b = a.astype(F32), b.astype(F32)
    return lax.dot_general(a, b, (((ca,), (cb,)), ((), ())), preferred_element_type=F32)


def front_kernel(
    factor, x_hbm, w_hbm, pay, qhat_o, khat_o, rad_o, x, w, sem, *, heads, hs
):
    x_copy = pltpu.make_async_copy(x_hbm, x, sem.at[0])
    x_copy.start()
    copies = [pltpu.make_async_copy(w_hbm.at[i], w.at[i], sem.at[1 + i]) for i in range(3)]
    for i in (1, 2, 0):
        copies[i].start()
    x_copy.wait()
    xf = x[...].astype(F32)
    centred = xf - jnp.mean(xf, axis=-1, keepdims=True)
    var = jnp.mean(centred * centred, axis=-1, keepdims=True)
    unit = centred * (1.0 / jnp.sqrt(var + 1e-05))
    normed = (unit * factor[...]).astype(BF16)
    copies[1].wait()
    kt = dotf(normed, w[1]).T
    copies[2].wait()
    vt = dotf(normed, w[2]).T
    copies[0].wait()
    qt = dotf(normed, w[0]).T
    for h in range(heads):
        lo, hi = h * hs, (h + 1) * hs
        q = qt[lo:hi]
        k = kt[lo:hi]
        qr = jnp.sqrt(jnp.mean(q * q, axis=0, keepdims=True) + 1e-06)
        kr = jnp.sqrt(jnp.mean(k * k, axis=0, keepdims=True) + 1e-06)
        qh = q / qr
        kh = k / kr
        qhat_o[lo:hi] = qh
        khat_o[lo:hi] = kh
        rad_o[h : h + 1] = qr
        rad_o[heads + h : heads + h + 1] = kr
        pay[h, 0:hs] = kh.astype(BF16)
        pay[h, hs : 2 * hs] = vt[lo:hi].astype(BF16)


def fill_pad(pad, left, own, right, place):
    reach = left.shape[0]
    rows = own.shape[0]
    pad[16 - reach : 16] = jnp.where(place > 0, left[...].astype(F32), 0.0)
    pad[16 : 16 + rows] = own[...].astype(F32)
    pad[16 + rows : 16 + rows + reach] = jnp.where(place < TM - 1, right[...].astype(F32), 0.0)


def conv_rows(pad, taps, out, rows, flip):
    count = taps.shape[0]
    reach = count // 2

    def chunk(c, _):
        lanes = pl.ds(pl.multiple_of(c * 128, 128), 128)
        acc = pad[16 : 16 + rows, lanes]
        for phase in range(8):
            shifted = pad[phase : phase + rows + 24, lanes]
            for j in range(count):
                at = 16 + reach - j if flip else 16 - reach + j
                if at % 8 == phase:
                    acc = acc + taps[j : j + 1, lanes] * shifted[at - phase : at - phase + rows]
        out[:, lanes] = acc.astype(out.dtype)
        return 0

    lax.fori_loop(0, out.shape[1] // 128, chunk, 0)


def send_kernel(idx, place, sharp, left, own, right, taps, qhat, pay, wf, o0, o1, o2, o3, gres_o, pad, g_s, gres, *, hs):
    fill_pad(pad, left, own, right, place[0])
    conv_rows(pad, taps, gres, own.shape[0], True)
    gres_o[...] = gres[...]
    gt = dotf(wf[...], gres[...].astype(BF16), 1, 1).astype(BF16)
    for h in range(4):
        g_s[h, 0:hs] = (qhat[h * hs : (h + 1) * hs] * (sharp[h] / math.sqrt(hs))).astype(BF16)
        g_s[h, hs : 2 * hs] = gt[h * hs : (h + 1) * hs]
    for s, o in enumerate((o0, o1, o2, o3)):
        at = lax.rem(idx[0] + s, 4)
        o[0 : 2 * hs] = pay[at]
        o[2 * hs : 4 * hs] = g_s[at]


def tail_kernel(
    place, part, other, x, factor, left, own, right, gres_hbm, res_o, sig_o, sums, first, last, pad, resf, gain, gres, sem,
    *, rows, taps,
):
    fetch = pltpu.make_async_copy(gres_hbm, gres, sem)
    fetch.start()
    fill_pad(pad, left, own, right, place[0])
    reach = taps // 2
    total = part[0:rows].astype(F32) + other[0:rows].astype(F32)
    xf = x[...].astype(F32)
    residual = (xf + total).astype(BF16)
    res_o[...] = residual
    first[...] = residual[:reach]
    last[...] = residual[rows - reach :]
    resf[...] = residual.astype(F32)
    centred = xf - jnp.mean(xf, axis=-1, keepdims=True)
    var = jnp.mean(centred * centred, axis=-1, keepdims=True)
    inv = 1.0 / jnp.sqrt(var + 1e-05)
    unit = centred * inv
    grad = part[rows : 2 * rows].astype(F32) + other[rows : 2 * rows].astype(F32)
    prod = grad * unit
    gain[...] = jnp.sum(prod, axis=0, keepdims=True)
    f = factor[...]
    scaled = grad * f
    m1 = jnp.mean(scaled, axis=-1, keepdims=True)
    m2 = jnp.mean(prod * f, axis=-1, keepdims=True)
    fetch.wait()
    sig_o[...] = (gres[...] + (scaled - m1 - unit * m2) * inv).astype(BF16)
    half = sums.shape[2] // 128

    for h in range(2):

        def chunk(c, _):
            lanes = pl.ds(pl.multiple_of((h * half + c) * 128, 128), 128)
            to = pl.ds(pl.multiple_of(c * 128, 128), 128)
            r = resf[:, lanes]
            for phase in range(8):
                shifted = pad[phase : phase + rows + 24, lanes]
                for j in range(taps):
                    at = 16 + reach - j
                    if at % 8 == phase:
                        moved = shifted[at - phase : at - phase + rows]
                        sums[h, j : j + 1, to] = jnp.sum(r * moved, axis=0, keepdims=True)
            sums[h, taps : taps + 1, to] = gain[:, lanes]
            return 0

        lax.fori_loop(0, half, chunk, 0)


def out_kernel(place, left, own, right, taps, out, pad):
    fill_pad(pad, left, own, right, place[0])
    conv_rows(pad, taps, out, own.shape[0], False)


def pack_kernel(p0, p1, p2, p3, kv, qg):
    half, lanes = kv.shape[0], p0.shape[1]
    for s, p in enumerate((p0, p1, p2, p3)):
        kv[:, s * lanes : (s + 1) * lanes] = p[0:half]
        qg[:, s * lanes : (s + 1) * lanes] = p[half : 2 * half]


def to_rows(a):
    return a.astype(F32).T.astype(BF16)


def rows_kernel(*refs, hs):
    kv = refs[0:4]
    qg = refs[4:8]
    te, acc = refs[8:10]
    kn, vn, qgs = refs[10:]
    span = kv[0].shape[1]
    for r in range(4):
        kn[r] = to_rows(kv[r][0:hs])
        vn[r] = to_rows(kv[r][hs : 2 * hs])
        qgs[r] = qg[r][...]

    def over_q(j, _):
        qt = qgs[j, 0:hs]
        gt = qgs[j, hs : 2 * hs]
        tot = jnp.zeros((8, span), F32)
        exp = jnp.zeros((8, span), F32)
        low = jnp.zeros((2 * hs, span), F32)
        high = jnp.zeros((hs, span), F32)
        for r in range(4):
            w = jnp.exp(dotf(kn[r], qt))
            wp = w * dotf(vn[r], gt)
            tot = tot + jnp.sum(w.reshape(span // 8, 8, span), axis=0)
            exp = exp + jnp.sum(wp.reshape(span // 8, 8, span), axis=0)
            low = low + dotf(kv[r][...], w.astype(BF16))
            high = high + dotf(kv[r][0:hs], wp.astype(BF16))
        acc[j, 0 : 2 * hs] = low
        acc[j, 2 * hs : 3 * hs] = high
        te[j, 0:1] = jnp.sum(tot, axis=0, keepdims=True)
        te[j, 1:2] = jnp.sum(exp, axis=0, keepdims=True)
        return 0

    lax.fori_loop(0, 4, over_q, 0)


def norm_kernel(te0, te1, acc, *rows, hs):
    for r in range(4):
        t = te0[r] + te1[r ^ 2]
        inv = 1.0 / t[0:1]
        delta = t[1:2] * inv
        rows[r][0:hs] = (acc[r, hs : 2 * hs] * inv).astype(BF16)
        rows[r][hs : 2 * hs] = ((acc[r, 2 * hs : 3 * hs] - delta * acc[r, 0:hs]) * inv).astype(BF16)


def cols_kernel(*refs, hs):
    te = refs[0:2]
    kv = refs[2:6]
    qg = refs[6:10]
    cols = refs[10:14]
    kn, vn, qn, gn, inv, dlt, colacc = refs[14:]
    span = kv[0].shape[1]
    for r in range(4):
        kn[r] = to_rows(kv[r][0:hs])
        vn[r] = to_rows(kv[r][hs : 2 * hs])
        qn[r] = to_rows(qg[r][0:hs])
        gn[r] = to_rows(qg[r][hs : 2 * hs])
        t = te[0][r] + te[1][r ^ 2]
        one = 1.0 / t[0:1]
        inv[r] = one
        dlt[r] = t[1:2] * one

    def over_k(b, _):
        k = kn[b]
        v = vn[b]
        gk = jnp.zeros((span, hs), F32)
        gv = jnp.zeros((span, hs), F32)
        for j in range(4):
            prob = jnp.exp(dotf(k, qg[j][0:hs])) * inv[j]
            slope = prob * (dotf(v, qg[j][hs : 2 * hs]) - dlt[j])
            gv = gv + dotf(prob.astype(BF16), gn[j])
            gk = gk + dotf(slope.astype(BF16), qn[j])
        colacc[b, 0:hs] = gk.T.astype(BF16)
        colacc[b, hs : 2 * hs] = gv.T.astype(BF16)
        return 0

    lax.fori_loop(0, 4, over_k, 0)
    for r in range(4):
        cols[r][...] = colacc[r]


def run_rows(kv, qg, hs, span):
    nat = pltpu.VMEM((4, span, hs), BF16)
    return vcall(
        functools.partial(rows_kernel, hs=hs),
        (jax.ShapeDtypeStruct((4, 2, span), F32), jax.ShapeDtypeStruct((4, 3 * hs, span), F32)),
        scratch=[nat, nat, pltpu.VMEM((4, 2 * hs, span), BF16)],
        n_in=8,
    )(*kv, *qg)


def run_cols(te, kv, qg, hs, span):
    nat = pltpu.VMEM((4, span, hs), BF16)
    row = pltpu.VMEM((4, 1, span), F32)
    return vcall(
        functools.partial(cols_kernel, hs=hs),
        tuple(jax.ShapeDtypeStruct((2 * hs, span), BF16) for _ in range(4)),
        scratch=[nat, nat, nat, nat, row, row, pltpu.VMEM((4, 2 * hs, span), BF16)],
        n_in=10,
    )(*te, *kv, *qg)


def sum_kernel(*refs, hs):
    row = refs[0][...].astype(F32)
    col = refs[4][...].astype(F32)
    for i in range(1, 4):
        row = row + refs[i][...].astype(F32)
        col = col + refs[4 + i][...].astype(F32)
    row = row.astype(BF16)
    col = col.astype(BF16)
    lanes = row.shape[1] // 4
    for s in range(4):
        refs[8 + s][0 : 2 * hs] = row[:, s * lanes : (s + 1) * lanes]
        refs[8 + s][2 * hs : 4 * hs] = col[:, s * lanes : (s + 1) * lanes]


def back_kernel(idx, sharp, b0, b1, b2, b3, qhat, khat, rad, wf, w, out, home, att, qgr, kgr, vgr, *, heads, hs):
    for s, b in enumerate((b0, b1, b2, b3)):
        home[lax.rem(idx[0] + s, 4)] = b[...]
    lanes = b0.shape[1]
    for h in range(heads):
        lo, hi = h * hs, (h + 1) * hs
        att[lo:hi] = home[h, 0:hs].astype(F32)
        gq = home[h, hs : 2 * hs].astype(F32) * (sharp[h] / math.sqrt(hs))
        gk = home[h, 2 * hs : 3 * hs].astype(F32)
        vgr[lo:hi] = home[h, 3 * hs : 4 * hs].astype(F32)
        qh = qhat[lo:hi]
        kh = khat[lo:hi]
        qgr[lo:hi] = (gq - qh * jnp.mean(gq * qh, axis=0, keepdims=True)) / rad[h : h + 1]
        kgr[lo:hi] = (gk - kh * jnp.mean(gk * kh, axis=0, keepdims=True)) / rad[heads + h : heads + h + 1]
    out[0:lanes] = dotf(att[...].T.astype(BF16), wf[...]).astype(BF16)
    normed = dotf(qgr[...].T.astype(BF16), w[0], 1, 1)
    normed = normed + dotf(kgr[...].T.astype(BF16), w[1], 1, 1)
    normed = normed + dotf(vgr[...].T.astype(BF16), w[2], 1, 1)
    out[lanes : 2 * lanes] = normed.astype(BF16)


def rims(cells, head, tail):
    left = lax.ppermute(tail, "tm", [(i, (i + 1) % TM) for i in range(TM)])
    right = lax.ppermute(head, "tm", [((i + 1) % TM, i) for i in range(TM)])
    return left, cells, right


def pieces(a, n):
    width = a.shape[1] // n
    return lambda i: lax.dynamic_slice_in_dim(a, i * width, width, axis=1)


def scatter_sum(a, batches):
    t = lax.axis_index("tm")
    z4, z2, x, yh = t // 16, (t // 8) % 2, (t // 2) % 4, t % 2
    if batches > 1:
        b = lax.axis_index("batch")
        away = lax.dynamic_index_in_dim(a, 1 - b, 0, keepdims=False)
        got = lax.ppermute(away, "batch", [(0, 1), (1, 0)])
        a = lax.dynamic_index_in_dim(a, b, 0, keepdims=False) + got
    else:
        a = jnp.concatenate([a[0], a[1]], axis=1)
    at = pieces(a, 4)
    got = ordered(lambda s: move_z4(at((z4 + s) % 4), s), (2, 1, 3))
    a = (at(z4) + got[0]) + (got[1] + got[2])
    at = pieces(a, 2)
    a = at(z2) + move_zy(at(1 - z2), 1)
    at = pieces(a, 4)
    got = ordered(lambda s: move_x(at((x + s) % 4), s), (2, 1, 3))
    a = (at(x) + got[0]) + (got[1] + got[2])
    at = pieces(a, 2)
    return at(yh) + move_zy(at(1 - yh), 2)


def step(input_signal, standardize_factor, triple_projection, score_sharpening, final_projection, filter_taps, mixture_adjoint, *, batches, mps):
    rows, width = input_signal.shape[1:]
    heads = score_sharpening.shape[0]
    hs = triple_projection.shape[2] // heads
    flat = heads * hs
    taps = filter_taps.shape[0]
    reach = taps // 2
    t = lax.axis_index("tm")
    z4 = (t // 16).astype(jnp.int32).reshape(1)
    place = t.astype(jnp.int32).reshape(1)
    x_in = input_signal[0]
    adj = mixture_adjoint[0]
    factor = standardize_factor[None]
    shape = jax.ShapeDtypeStruct
    adj_rims = rims(adj, adj[:reach], adj[rows - reach :])
    piece = shape((4 * hs, rows), BF16)
    pay, qhat, khat, rad = vcall(
        functools.partial(front_kernel, heads=heads, hs=hs),
        (shape((heads, 2 * hs, rows), BF16), shape((flat, rows), F32), shape((flat, rows), F32), shape((2 * heads, rows), F32)),
        scratch=[
            pltpu.VMEM((rows, width), BF16),
            pltpu.VMEM((3, width, flat), BF16),
            pltpu.SemaphoreType.DMA((4,)),
        ],
        n_in=1,
        raw=2,
    )(factor, x_in, triple_projection)
    pad = pltpu.VMEM((rows + 32, width), F32)
    *sent, grad_res = vcall(
        functools.partial(send_kernel, hs=hs),
        (piece,) * 4 + (shape((rows, width), F32),),
        scratch=[pad, pltpu.VMEM((4, 2 * hs, rows), BF16), pltpu.VMEM((rows, width), F32)],
        out_hbm=(4,),
        smem=3,
        n_in=7,
    )(z4, place, score_sharpening, *adj_rims, filter_taps, qhat, pay, final_projection)
    got = [sent[0]] + ordered(lambda s: move_z4(sent[s], s), (2, 1, 3))
    kv0, qg0 = vcall(pack_kernel, (shape((2 * hs, 4 * rows), BF16),) * 2, n_in=4)(*got)
    kv = [kv0] + ordered(lambda s: move_x(kv0, s), (2, 1, 3))
    qg = [qg0] + ordered(lambda m: move_zy(qg0, m), (3, 2, 1))
    span = 4 * rows
    te0, acc = run_rows(kv, qg, hs, span)
    te1 = move_zy(te0, 1)
    te1 = te0 + jnp.stack([te1[r ^ 1] for r in range(4)])
    te = [te1, move_zy(te1, 2)]
    rowp = vcall(functools.partial(norm_kernel, hs=hs), (shape((2 * hs, span), BF16),) * 4, n_in=3)(*te, acc)
    row = [rowp[0]] + ordered(lambda m: move_zy(rowp[m], m), (3, 2, 1))
    colp = run_cols(te, kv, qg, hs, span)
    col = [colp[0]] + ordered(lambda s: move_x(colp[s], -s), (2, 1, 3))
    home = vcall(
        functools.partial(sum_kernel, hs=hs),
        tuple(shape((4 * hs, rows), BF16) for _ in range(4)),
        n_in=8,
    )(*row, *col)
    back = [home[0]] + ordered(lambda s: move_z4(home[s], -s), (2, 1, 3))
    part = vcall(
        functools.partial(back_kernel, heads=heads, hs=hs),
        shape((2 * rows, width), BF16),
        scratch=[pltpu.VMEM((4, 4 * hs, rows), BF16)] + [pltpu.VMEM((flat, rows), F32)] * 4,
        smem=2,
        n_in=9,
    )(z4, score_sharpening, *back, qhat, khat, rad, final_projection, triple_projection)
    other = lax.ppermute(part, "mp", [(0, 1), (1, 0)]) if mps > 1 else jnp.zeros_like(part)
    edge = shape((reach, width), BF16)
    residual, signal_adjoint, sums, first, last = vcall(
        functools.partial(tail_kernel, rows=rows, taps=taps),
        (shape((rows, width), BF16), shape((rows, width), BF16), shape((2, taps + 1, width // 2), F32), edge, edge),
        scratch=[
            pad,
            pltpu.VMEM((rows, width), F32),
            pltpu.VMEM((1, width), F32),
            pltpu.VMEM((rows, width), F32),
            pltpu.SemaphoreType.DMA(()),
        ],
        smem=1,
        n_in=7,
        raw=1,
        out_hbm=(1,),
    )(place, part, other, x_in, factor, *adj_rims, grad_res)
    res_rims = rims(residual, first, last)
    result = vcall(out_kernel, shape((rows, width), BF16), scratch=[pad], smem=1, n_in=4)(place, *res_rims, filter_taps)
    sums = scatter_sum(sums, batches)
    return (result[None], signal_adjoint[None], sums[:taps], sums[taps])


def solution(mesh):
    call = mapped(mesh)
    return call


def mapped(mesh):
    return jax.shard_map(
        functools.partial(step, batches=mesh.shape["batch"], mps=mesh.shape["mp"]),
        mesh=mesh,
        in_specs=(
            P("batch", "tm", None),
            P(),
            P(None, None, "mp"),
            P("mp"),
            P("mp", None),
            P(),
            P("batch", "tm", None),
        ),
        out_specs=(
            P("batch", "tm", None),
            P("batch", "tm", None),
            P(None, ("batch", "tm")),
            P(("batch", "tm")),
        ),
        check_vma=False,
    )
```

```python
import functools
import math

import jax
import jax.numpy as jnp
from jax import lax
from jax.experimental import pallas as pl
from jax.experimental.pallas import tpu as pltpu
from jax.sharding import PartitionSpec as P


INTERPRET = False
LIMIT = 24 * 1024 * 1024
TM = 64
F32 = jnp.float32
BF16 = jnp.bfloat16


def _split(t):
    return t // 16, (t // 8) % 2, (t // 2) % 4, t % 2


def _join(z4, z2, x, yh):
    return ((z4 % 4) * 2 + z2) * 8 + (x % 4) * 2 + yh


def move_z4(a, s):
    pairs = []
    for t in range(TM):
        z4, z2, x, yh = _split(t)
        pairs.append((t, _join(z4 + s, z2, x, yh)))
    return lax.ppermute(a, "tm", pairs)


def move_x(a, s):
    pairs = []
    for t in range(TM):
        z4, z2, x, yh = _split(t)
        pairs.append((t, _join(z4, z2, x + s, yh)))
    return lax.ppermute(a, "tm", pairs)


def move_zy(a, m):
    pairs = []
    for t in range(TM):
        z4, z2, x, yh = _split(t)
        pairs.append((t, _join(z4, z2 ^ (m & 1), x, yh ^ (m >> 1))))
    return lax.ppermute(a, "tm", pairs)


def ordered(move, shifts):
    got = {s: move(s) for s in shifts}
    return [got[s] for s in (1, 2, 3)]


def vcall(kernel, out_shape, scratch=(), smem=0, n_in=0, raw=0, out_hbm=()):
    space = [pl.BlockSpec(memory_space=pltpu.SMEM)] * smem
    space += [pl.BlockSpec(memory_space=pltpu.VMEM)] * n_in
    space += [pl.BlockSpec(memory_space=pltpu.HBM if not INTERPRET else pl.ANY)] * raw
    flat, tree = jax.tree.flatten(out_shape)
    held = flat
    if not INTERPRET:
        held = [o if i in out_hbm else pltpu.VMEM(o.shape, o.dtype) for i, o in enumerate(flat)]
    call = pl.pallas_call(
        kernel,
        out_shape=jax.tree.unflatten(tree, held),
        in_specs=space,
        out_specs=jax.tree.unflatten(tree, [pl.BlockSpec(memory_space=pltpu.VMEM)] * len(flat)),
        scratch_shapes=list(scratch),
        compiler_params=pltpu.CompilerParams(vmem_limit_bytes=LIMIT),
        interpret=INTERPRET,
    )

    def run(*args):
        if not INTERPRET:
            args = [
                a if i < smem else pltpu.with_memory_space_constraint(a, pltpu.VMEM if i < smem + n_in else pltpu.HBM)
                for i, a in enumerate(args)
            ]
        return call(*args)

    return run


def dotf(a, b, ca=1, cb=0):
    if INTERPRET:
        a, b = a.astype(F32), b.astype(F32)
    return lax.dot_general(a, b, (((ca,), (cb,)), ((), ())), preferred_element_type=F32)


def front_kernel(
    factor, x_hbm, w_hbm, pay, qhat_o, khat_o, rad_o, x, w, sem, *, heads, hs
):
    x_copy = pltpu.make_async_copy(x_hbm, x, sem.at[0])
    x_copy.start()
    copies = [pltpu.make_async_copy(w_hbm.at[i], w.at[i], sem.at[1 + i]) for i in range(3)]
    for i in (1, 2, 0):
        copies[i].start()
    x_copy.wait()
    xf = x[...].astype(F32)
    centred = xf - jnp.mean(xf, axis=-1, keepdims=True)
    var = jnp.mean(centred * centred, axis=-1, keepdims=True)
    unit = centred * (1.0 / jnp.sqrt(var + 1e-05))
    normed = (unit * factor[...]).astype(BF16)
    copies[1].wait()
    kt = dotf(normed, w[1]).T
    copies[2].wait()
    vt = dotf(normed, w[2]).T
    copies[0].wait()
    qt = dotf(normed, w[0]).T
    for h in range(heads):
        lo, hi = h * hs, (h + 1) * hs
        q = qt[lo:hi]
        k = kt[lo:hi]
        qr = jnp.sqrt(jnp.mean(q * q, axis=0, keepdims=True) + 1e-06)
        kr = jnp.sqrt(jnp.mean(k * k, axis=0, keepdims=True) + 1e-06)
        qh = q / qr
        kh = k / kr
        qhat_o[lo:hi] = qh
        khat_o[lo:hi] = kh
        rad_o[h : h + 1] = qr
        rad_o[heads + h : heads + h + 1] = kr
        pay[h, 0:hs] = kh.astype(BF16)
        pay[h, hs : 2 * hs] = vt[lo:hi].astype(BF16)


def fill_pad(pad, left, own, right, place):
    reach = left.shape[0]
    rows = own.shape[0]
    pad[16 - reach : 16] = jnp.where(place > 0, left[...].astype(F32), 0.0)
    pad[16 : 16 + rows] = own[...].astype(F32)
    pad[16 + rows : 16 + rows + reach] = jnp.where(place < TM - 1, right[...].astype(F32), 0.0)


def conv_rows(pad, taps, out, rows, flip):
    count = taps.shape[0]
    reach = count // 2

    def chunk(c, _):
        lanes = pl.ds(pl.multiple_of(c * 128, 128), 128)
        acc = pad[16 : 16 + rows, lanes]
        for phase in range(8):
            shifted = pad[phase : phase + rows + 24, lanes]
            for j in range(count):
                at = 16 + reach - j if flip else 16 - reach + j
                if at % 8 == phase:
                    acc = acc + taps[j : j + 1, lanes] * shifted[at - phase : at - phase + rows]
        out[:, lanes] = acc.astype(out.dtype)
        return 0

    lax.fori_loop(0, out.shape[1] // 128, chunk, 0)


def send_kernel(idx, place, sharp, left, own, right, taps, qhat, pay, wf, o0, o1, o2, o3, gres_o, pad, g_s, gres, *, hs):
    fill_pad(pad, left, own, right, place[0])
    conv_rows(pad, taps, gres, own.shape[0], True)
    gres_o[...] = gres[...]
    gt = dotf(wf[...], gres[...].astype(BF16), 1, 1).astype(BF16)
    for h in range(4):
        g_s[h, 0:hs] = (qhat[h * hs : (h + 1) * hs] * (sharp[h] / math.sqrt(hs))).astype(BF16)
        g_s[h, hs : 2 * hs] = gt[h * hs : (h + 1) * hs]
    for s, o in enumerate((o0, o1, o2, o3)):
        at = lax.rem(idx[0] + s, 4)
        o[0 : 2 * hs] = pay[at]
        o[2 * hs : 4 * hs] = g_s[at]


def tail_kernel(
    place, part, other, x, factor, left, own, right, gres_hbm, res_o, sig_o, sums, first, last, pad, resf, gain, gres, sem,
    *, rows, taps,
):
    fetch = pltpu.make_async_copy(gres_hbm, gres, sem)
    fetch.start()
    fill_pad(pad, left, own, right, place[0])
    reach = taps // 2
    total = part[0:rows].astype(F32) + other[0:rows].astype(F32)
    xf = x[...].astype(F32)
    residual = (xf + total).astype(BF16)
    res_o[...] = residual
    first[...] = residual[:reach]
    last[...] = residual[rows - reach :]
    resf[...] = residual.astype(F32)
    centred = xf - jnp.mean(xf, axis=-1, keepdims=True)
    var = jnp.mean(centred * centred, axis=-1, keepdims=True)
    inv = 1.0 / jnp.sqrt(var + 1e-05)
    unit = centred * inv
    grad = part[rows : 2 * rows].astype(F32) + other[rows : 2 * rows].astype(F32)
    prod = grad * unit
    gain[...] = jnp.sum(prod, axis=0, keepdims=True)
    f = factor[...]
    scaled = grad * f
    m1 = jnp.mean(scaled, axis=-1, keepdims=True)
    m2 = jnp.mean(prod * f, axis=-1, keepdims=True)
    fetch.wait()
    sig_o[...] = (gres[...] + (scaled - m1 - unit * m2) * inv).astype(BF16)
    half = sums.shape[2] // 128

    for h in range(2):

        def chunk(c, _):
            lanes = pl.ds(pl.multiple_of((h * half + c) * 128, 128), 128)
            to = pl.ds(pl.multiple_of(c * 128, 128), 128)
            r = resf[:, lanes]
            for phase in range(8):
                shifted = pad[phase : phase + rows + 24, lanes]
                for j in range(taps):
                    at = 16 + reach - j
                    if at % 8 == phase:
                        moved = shifted[at - phase : at - phase + rows]
                        sums[h, j : j + 1, to] = jnp.sum(r * moved, axis=0, keepdims=True)
            sums[h, taps : taps + 1, to] = gain[:, lanes]
            return 0

        lax.fori_loop(0, half, chunk, 0)


def out_kernel(place, left, own, right, taps, out, pad):
    fill_pad(pad, left, own, right, place[0])
    conv_rows(pad, taps, out, own.shape[0], False)


def pack_kernel(p0, p1, p2, p3, kv, qg):
    half, lanes = kv.shape[0], p0.shape[1]
    for s, p in enumerate((p0, p1, p2, p3)):
        kv[:, s * lanes : (s + 1) * lanes] = p[0:half]
        qg[:, s * lanes : (s + 1) * lanes] = p[half : 2 * half]


def to_rows(a):
    return a.astype(F32).T.astype(BF16)


def rows_kernel(*refs, hs):
    kv = refs[0:4]
    qg = refs[4:8]
    te = refs[8]
    out = refs[9:13]
    kn, vn, qgs, acc = refs[13:]
    span = kv[0].shape[1]
    for r in range(4):
        kn[r] = to_rows(kv[r][0:hs])
        vn[r] = to_rows(kv[r][hs : 2 * hs])
        qgs[r] = qg[r][...]

    def over_q(j, _):
        qt = qgs[j, 0:hs]
        gt = qgs[j, hs : 2 * hs]
        tot = jnp.zeros((8, span), F32)
        exp = jnp.zeros((8, span), F32)
        low = jnp.zeros((2 * hs, span), F32)
        high = jnp.zeros((hs, span), F32)
        for r in range(4):
            w = jnp.exp(dotf(kn[r], qt))
            wp = w * dotf(vn[r], gt)
            tot = tot + jnp.sum(w.reshape(span // 8, 8, span), axis=0)
            exp = exp + jnp.sum(wp.reshape(span // 8, 8, span), axis=0)
            low = low + dotf(kv[r][...], w.astype(BF16))
            high = high + dotf(kv[r][0:hs], wp.astype(BF16))
        tot = jnp.sum(tot, axis=0, keepdims=True)
        exp = jnp.sum(exp, axis=0, keepdims=True)
        te[j, 0:1] = tot
        te[j, 1:2] = exp
        acc[j, 0:hs] = low[hs : 2 * hs].astype(BF16)
        acc[j, hs : 2 * hs] = (high - (exp / tot) * low[0:hs]).astype(BF16)
        acc[j, 2 * hs : 3 * hs] = low[0:hs].astype(BF16)
        return 0

    lax.fori_loop(0, 4, over_q, 0)
    for r in range(4):
        out[r][...] = acc[r]


def cols_kernel(*refs, hs):
    te = refs[0:4]
    kv = refs[4:8]
    qg = refs[8:12]
    cols = refs[12:16]
    kn, vn, qn, gn, inv, dlt, colacc = refs[16:]
    span = kv[0].shape[1]
    for r in range(4):
        kn[r] = to_rows(kv[r][0:hs])
        vn[r] = to_rows(kv[r][hs : 2 * hs])
        qn[r] = to_rows(qg[r][0:hs])
        gn[r] = to_rows(qg[r][hs : 2 * hs])
        t = (te[0][r] + te[1][r ^ 1]) + (te[2][r ^ 2] + te[3][r ^ 3])
        one = 1.0 / t[0:1]
        inv[r] = one
        dlt[r] = t[1:2] * one

    def over_k(b, _):
        k = kn[b]
        v = vn[b]
        gk = jnp.zeros((span, hs), F32)
        gv = jnp.zeros((span, hs), F32)
        for j in range(4):
            prob = jnp.exp(dotf(k, qg[j][0:hs])) * inv[j]
            slope = prob * (dotf(v, qg[j][hs : 2 * hs]) - dlt[j])
            gv = gv + dotf(prob.astype(BF16), gn[j])
            gk = gk + dotf(slope.astype(BF16), qn[j])
        colacc[b, 0:hs] = gk.T.astype(BF16)
        colacc[b, hs : 2 * hs] = gv.T.astype(BF16)
        return 0

    lax.fori_loop(0, 4, over_k, 0)
    for r in range(4):
        cols[r][...] = colacc[r]


def run_rows(kv, qg, hs, span):
    nat = pltpu.VMEM((4, span, hs), BF16)
    return vcall(
        functools.partial(rows_kernel, hs=hs),
        (jax.ShapeDtypeStruct((4, 2, span), F32),) + (jax.ShapeDtypeStruct((3 * hs, span), BF16),) * 4,
        scratch=[nat, nat, pltpu.VMEM((4, 2 * hs, span), BF16), pltpu.VMEM((4, 3 * hs, span), BF16)],
        n_in=8,
    )(*kv, *qg)


def run_cols(te, kv, qg, hs, span):
    nat = pltpu.VMEM((4, span, hs), BF16)
    row = pltpu.VMEM((4, 1, span), F32)
    return vcall(
        functools.partial(cols_kernel, hs=hs),
        tuple(jax.ShapeDtypeStruct((2 * hs, span), BF16) for _ in range(4)),
        scratch=[nat, nat, nat, nat, row, row, pltpu.VMEM((4, 2 * hs, span), BF16)],
        n_in=12,
    )(*te, *kv, *qg)


def sum_kernel(*refs, hs):
    te = refs[0:4]
    row = refs[4:8]
    out = refs[12:16]
    each = [te[m][m] for m in range(4)]
    total = (each[0] + each[1]) + (each[2] + each[3])
    inv = 1.0 / total[0:1]
    delta = total[1:2] * inv
    att = jnp.zeros((hs, inv.shape[1]), F32)
    grad = jnp.zeros((hs, inv.shape[1]), F32)
    col = jnp.zeros((2 * hs, inv.shape[1]), F32)
    for m in range(4):
        att = att + row[m][0:hs].astype(F32)
        shift = each[m][1:2] / each[m][0:1] - delta
        grad = grad + (row[m][hs : 2 * hs].astype(F32) + shift * row[m][2 * hs : 3 * hs].astype(F32))
        col = col + refs[8 + m][...].astype(F32)
    att = (att * inv).astype(BF16)
    grad = (grad * inv).astype(BF16)
    col = col.astype(BF16)
    lanes = inv.shape[1] // 4
    for s in range(4):
        part = slice(s * lanes, (s + 1) * lanes)
        out[s][0:hs] = att[:, part]
        out[s][hs : 2 * hs] = grad[:, part]
        out[s][2 * hs : 4 * hs] = col[:, part]


def back_kernel(idx, sharp, b0, b1, b2, b3, qhat, khat, rad, wf, w, out, home, att, qgr, kgr, vgr, *, heads, hs):
    for s, b in enumerate((b0, b1, b2, b3)):
        home[lax.rem(idx[0] + s, 4)] = b[...]
    lanes = b0.shape[1]
    for h in range(heads):
        lo, hi = h * hs, (h + 1) * hs
        att[lo:hi] = home[h, 0:hs].astype(F32)
        gq = home[h, hs : 2 * hs].astype(F32) * (sharp[h] / math.sqrt(hs))
        gk = home[h, 2 * hs : 3 * hs].astype(F32)
        vgr[lo:hi] = home[h, 3 * hs : 4 * hs].astype(F32)
        qh = qhat[lo:hi]
        kh = khat[lo:hi]
        qgr[lo:hi] = (gq - qh * jnp.mean(gq * qh, axis=0, keepdims=True)) / rad[h : h + 1]
        kgr[lo:hi] = (gk - kh * jnp.mean(gk * kh, axis=0, keepdims=True)) / rad[heads + h : heads + h + 1]
    out[0:lanes] = dotf(att[...].T.astype(BF16), wf[...]).astype(BF16)
    normed = dotf(qgr[...].T.astype(BF16), w[0], 1, 1)
    normed = normed + dotf(kgr[...].T.astype(BF16), w[1], 1, 1)
    normed = normed + dotf(vgr[...].T.astype(BF16), w[2], 1, 1)
    out[lanes : 2 * lanes] = normed.astype(BF16)


def rims(cells, head, tail):
    left = lax.ppermute(tail, "tm", [(i, (i + 1) % TM) for i in range(TM)])
    right = lax.ppermute(head, "tm", [((i + 1) % TM, i) for i in range(TM)])
    return left, cells, right


def pieces(a, n):
    width = a.shape[1] // n
    return lambda i: lax.dynamic_slice_in_dim(a, i * width, width, axis=1)


def scatter_sum(a, batches):
    t = lax.axis_index("tm")
    z4, z2, x, yh = t // 16, (t // 8) % 2, (t // 2) % 4, t % 2
    if batches > 1:
        b = lax.axis_index("batch")
        away = lax.dynamic_index_in_dim(a, 1 - b, 0, keepdims=False)
        got = lax.ppermute(away, "batch", [(0, 1), (1, 0)])
        a = lax.dynamic_index_in_dim(a, b, 0, keepdims=False) + got
    else:
        a = jnp.concatenate([a[0], a[1]], axis=1)
    at = pieces(a, 4)
    got = ordered(lambda s: move_z4(at((z4 + s) % 4), s), (2, 1, 3))
    a = (at(z4) + got[0]) + (got[1] + got[2])
    at = pieces(a, 2)
    a = at(z2) + move_zy(at(1 - z2), 1)
    at = pieces(a, 4)
    got = ordered(lambda s: move_x(at((x + s) % 4), s), (2, 1, 3))
    a = (at(x) + got[0]) + (got[1] + got[2])
    at = pieces(a, 2)
    return at(yh) + move_zy(at(1 - yh), 2)


def step(input_signal, standardize_factor, triple_projection, score_sharpening, final_projection, filter_taps, mixture_adjoint, *, batches, mps):
    rows, width = input_signal.shape[1:]
    heads = score_sharpening.shape[0]
    hs = triple_projection.shape[2] // heads
    flat = heads * hs
    taps = filter_taps.shape[0]
    reach = taps // 2
    t = lax.axis_index("tm")
    z4 = (t // 16).astype(jnp.int32).reshape(1)
    place = t.astype(jnp.int32).reshape(1)
    x_in = input_signal[0]
    adj = mixture_adjoint[0]
    factor = standardize_factor[None]
    shape = jax.ShapeDtypeStruct
    adj_rims = rims(adj, adj[:reach], adj[rows - reach :])
    piece = shape((4 * hs, rows), BF16)
    pay, qhat, khat, rad = vcall(
        functools.partial(front_kernel, heads=heads, hs=hs),
        (shape((heads, 2 * hs, rows), BF16), shape((flat, rows), F32), shape((flat, rows), F32), shape((2 * heads, rows), F32)),
        scratch=[
            pltpu.VMEM((rows, width), BF16),
            pltpu.VMEM((3, width, flat), BF16),
            pltpu.SemaphoreType.DMA((4,)),
        ],
        n_in=1,
        raw=2,
    )(factor, x_in, triple_projection)
    pad = pltpu.VMEM((rows + 32, width), F32)
    *sent, grad_res = vcall(
        functools.partial(send_kernel, hs=hs),
        (piece,) * 4 + (shape((rows, width), F32),),
        scratch=[pad, pltpu.VMEM((4, 2 * hs, rows), BF16), pltpu.VMEM((rows, width), F32)],
        out_hbm=(4,),
        smem=3,
        n_in=7,
    )(z4, place, score_sharpening, *adj_rims, filter_taps, qhat, pay, final_projection)
    got = [sent[0]] + ordered(lambda s: move_z4(sent[s], s), (2, 1, 3))
    kv0, qg0 = vcall(pack_kernel, (shape((2 * hs, 4 * rows), BF16),) * 2, n_in=4)(*got)
    kv = [kv0] + ordered(lambda s: move_x(kv0, s), (2, 1, 3))
    qg = [qg0] + ordered(lambda m: move_zy(qg0, m), (3, 2, 1))
    span = 4 * rows
    te0, *rowp = run_rows(kv, qg, hs, span)
    te = [te0] + ordered(lambda m: move_zy(te0, m), (3, 2, 1))
    row = [rowp[0]] + ordered(lambda m: move_zy(rowp[m], m), (3, 2, 1))
    colp = run_cols(te, kv, qg, hs, span)
    col = [colp[0]] + ordered(lambda s: move_x(colp[s], -s), (2, 1, 3))
    home = vcall(
        functools.partial(sum_kernel, hs=hs),
        tuple(shape((4 * hs, rows), BF16) for _ in range(4)),
        n_in=12,
    )(*te, *row, *col)
    back = [home[0]] + ordered(lambda s: move_z4(home[s], -s), (2, 1, 3))
    part = vcall(
        functools.partial(back_kernel, heads=heads, hs=hs),
        shape((2 * rows, width), BF16),
        scratch=[pltpu.VMEM((4, 4 * hs, rows), BF16)] + [pltpu.VMEM((flat, rows), F32)] * 4,
        smem=2,
        n_in=9,
    )(z4, score_sharpening, *back, qhat, khat, rad, final_projection, triple_projection)
    other = lax.ppermute(part, "mp", [(0, 1), (1, 0)]) if mps > 1 else jnp.zeros_like(part)
    edge = shape((reach, width), BF16)
    residual, signal_adjoint, sums, first, last = vcall(
        functools.partial(tail_kernel, rows=rows, taps=taps),
        (shape((rows, width), BF16), shape((rows, width), BF16), shape((2, taps + 1, width // 2), F32), edge, edge),
        scratch=[
            pad,
            pltpu.VMEM((rows, width), F32),
            pltpu.VMEM((1, width), F32),
            pltpu.VMEM((rows, width), F32),
            pltpu.SemaphoreType.DMA(()),
        ],
        smem=1,
        n_in=7,
        raw=1,
        out_hbm=(1,),
    )(place, part, other, x_in, factor, *adj_rims, grad_res)
    res_rims = rims(residual, first, last)
    result = vcall(out_kernel, shape((rows, width), BF16), scratch=[pad], smem=1, n_in=4)(place, *res_rims, filter_taps)
    sums = scatter_sum(sums, batches)
    return (result[None], signal_adjoint[None], sums[:taps], sums[taps])


def solution(mesh):
    call = mapped(mesh)
    return call


def mapped(mesh):
    return jax.shard_map(
        functools.partial(step, batches=mesh.shape["batch"], mps=mesh.shape["mp"]),
        mesh=mesh,
        in_specs=(
            P("batch", "tm", None),
            P(),
            P(None, None, "mp"),
            P("mp"),
            P("mp", None),
            P(),
            P("batch", "tm", None),
        ),
        out_specs=(
            P("batch", "tm", None),
            P("batch", "tm", None),
            P(None, ("batch", "tm")),
            P(("batch", "tm")),
        ),
        check_vma=False,
    )
```

```python
import functools
import math

import jax
import jax.numpy as jnp
from jax import lax
from jax.experimental import pallas as pl
from jax.experimental.pallas import tpu as pltpu
from jax.sharding import PartitionSpec as P


INTERPRET = False
LIMIT = 24 * 1024 * 1024
TM = 64
F32 = jnp.float32
BF16 = jnp.bfloat16


def _split(t):
    return t // 16, (t // 8) % 2, (t // 2) % 4, t % 2


def _join(z4, z2, x, yh):
    return ((z4 % 4) * 2 + z2) * 8 + (x % 4) * 2 + yh


def move_z4(a, s):
    pairs = []
    for t in range(TM):
        z4, z2, x, yh = _split(t)
        pairs.append((t, _join(z4 + s, z2, x, yh)))
    return lax.ppermute(a, "tm", pairs)


def move_x(a, s):
    pairs = []
    for t in range(TM):
        z4, z2, x, yh = _split(t)
        pairs.append((t, _join(z4, z2, x + s, yh)))
    return lax.ppermute(a, "tm", pairs)


def move_zy(a, m):
    pairs = []
    for t in range(TM):
        z4, z2, x, yh = _split(t)
        pairs.append((t, _join(z4, z2 ^ (m & 1), x, yh ^ (m >> 1))))
    return lax.ppermute(a, "tm", pairs)


def ordered(move, shifts):
    got = {s: move(s) for s in shifts}
    return [got[s] for s in (1, 2, 3)]


def vcall(kernel, out_shape, scratch=(), smem=0, n_in=0, raw=0, out_hbm=()):
    space = [pl.BlockSpec(memory_space=pltpu.SMEM)] * smem
    space += [pl.BlockSpec(memory_space=pltpu.VMEM)] * n_in
    space += [pl.BlockSpec(memory_space=pltpu.HBM if not INTERPRET else pl.ANY)] * raw
    flat, tree = jax.tree.flatten(out_shape)
    held = flat
    if not INTERPRET:
        held = [o if i in out_hbm else pltpu.VMEM(o.shape, o.dtype) for i, o in enumerate(flat)]
    call = pl.pallas_call(
        kernel,
        out_shape=jax.tree.unflatten(tree, held),
        in_specs=space,
        out_specs=jax.tree.unflatten(tree, [pl.BlockSpec(memory_space=pltpu.VMEM)] * len(flat)),
        scratch_shapes=list(scratch),
        compiler_params=pltpu.CompilerParams(vmem_limit_bytes=LIMIT),
        interpret=INTERPRET,
    )

    def run(*args):
        if not INTERPRET:
            args = [
                a if i < smem else pltpu.with_memory_space_constraint(a, pltpu.VMEM if i < smem + n_in else pltpu.HBM)
                for i, a in enumerate(args)
            ]
        return call(*args)

    return run


def dotf(a, b, ca=1, cb=0):
    if INTERPRET:
        a, b = a.astype(F32), b.astype(F32)
    return lax.dot_general(a, b, (((ca,), (cb,)), ((), ())), preferred_element_type=F32)


def front_kernel(
    factor, x_hbm, w_hbm, pay, qhat_o, khat_o, rad_o, x, w, sem, *, heads, hs
):
    x_copy = pltpu.make_async_copy(x_hbm, x, sem.at[0])
    x_copy.start()
    copies = [pltpu.make_async_copy(w_hbm.at[i], w.at[i], sem.at[1 + i]) for i in range(3)]
    for i in (1, 2, 0):
        copies[i].start()
    x_copy.wait()
    xf = x[...].astype(F32)
    centred = xf - jnp.mean(xf, axis=-1, keepdims=True)
    var = jnp.mean(centred * centred, axis=-1, keepdims=True)
    unit = centred * (1.0 / jnp.sqrt(var + 1e-05))
    normed = (unit * factor[...]).astype(BF16)
    copies[1].wait()
    kt = dotf(normed, w[1]).T
    copies[2].wait()
    vt = dotf(normed, w[2]).T
    copies[0].wait()
    qt = dotf(normed, w[0]).T
    for h in range(heads):
        lo, hi = h * hs, (h + 1) * hs
        q = qt[lo:hi]
        k = kt[lo:hi]
        qr = jnp.sqrt(jnp.mean(q * q, axis=0, keepdims=True) + 1e-06)
        kr = jnp.sqrt(jnp.mean(k * k, axis=0, keepdims=True) + 1e-06)
        qh = q / qr
        kh = k / kr
        qhat_o[lo:hi] = qh
        khat_o[lo:hi] = kh
        rad_o[h : h + 1] = qr
        rad_o[heads + h : heads + h + 1] = kr
        pay[h, 0:hs] = kh.astype(BF16)
        pay[h, hs : 2 * hs] = vt[lo:hi].astype(BF16)


def fill_pad(pad, left, own, right, place):
    reach = left.shape[0]
    rows = own.shape[0]
    pad[16 - reach : 16] = jnp.where(place > 0, left[...].astype(F32), 0.0)
    pad[16 : 16 + rows] = own[...].astype(F32)
    pad[16 + rows : 16 + rows + reach] = jnp.where(place < TM - 1, right[...].astype(F32), 0.0)


def conv_rows(pad, taps, out, rows, flip):
    count = taps.shape[0]
    reach = count // 2

    def chunk(c, _):
        lanes = pl.ds(pl.multiple_of(c * 128, 128), 128)
        acc = pad[16 : 16 + rows, lanes]
        for phase in range(8):
            shifted = pad[phase : phase + rows + 24, lanes]
            for j in range(count):
                at = 16 + reach - j if flip else 16 - reach + j
                if at % 8 == phase:
                    acc = acc + taps[j : j + 1, lanes] * shifted[at - phase : at - phase + rows]
        out[:, lanes] = acc.astype(out.dtype)
        return 0

    lax.fori_loop(0, out.shape[1] // 128, chunk, 0)


def send_kernel(idx, place, sharp, left, own, right, taps, qhat, pay, wf, o0, o1, o2, o3, gres_o, pad, g_s, gres, *, hs):
    fill_pad(pad, left, own, right, place[0])
    conv_rows(pad, taps, gres, own.shape[0], True)
    gres_o[...] = gres[...]
    gt = dotf(wf[...], gres[...].astype(BF16), 1, 1).astype(BF16)
    for h in range(4):
        g_s[h, 0:hs] = (qhat[h * hs : (h + 1) * hs] * (sharp[h] / math.sqrt(hs))).astype(BF16)
        g_s[h, hs : 2 * hs] = gt[h * hs : (h + 1) * hs]
    for s, o in enumerate((o0, o1, o2, o3)):
        at = lax.rem(idx[0] + s, 4)
        o[0 : 2 * hs] = pay[at]
        o[2 * hs : 4 * hs] = g_s[at]


def tail_kernel(
    place, part, other, x, factor, left, own, right, gres_hbm, res_o, sig_o, sums, first, last, pad, resf, gain, gres, sem,
    *, rows, taps,
):
    fetch = pltpu.make_async_copy(gres_hbm, gres, sem)
    fetch.start()
    fill_pad(pad, left, own, right, place[0])
    reach = taps // 2
    total = part[0:rows].astype(F32) + other[0:rows].astype(F32)
    xf = x[...].astype(F32)
    residual = (xf + total).astype(BF16)
    res_o[...] = residual
    first[...] = residual[:reach]
    last[...] = residual[rows - reach :]
    resf[...] = residual.astype(F32)
    centred = xf - jnp.mean(xf, axis=-1, keepdims=True)
    var = jnp.mean(centred * centred, axis=-1, keepdims=True)
    inv = 1.0 / jnp.sqrt(var + 1e-05)
    unit = centred * inv
    grad = part[rows : 2 * rows].astype(F32) + other[rows : 2 * rows].astype(F32)
    prod = grad * unit
    gain[...] = jnp.sum(prod, axis=0, keepdims=True)
    f = factor[...]
    scaled = grad * f
    m1 = jnp.mean(scaled, axis=-1, keepdims=True)
    m2 = jnp.mean(prod * f, axis=-1, keepdims=True)
    fetch.wait()
    sig_o[...] = (gres[...] + (scaled - m1 - unit * m2) * inv).astype(BF16)
    half = sums.shape[2] // 128

    for h in range(2):

        def chunk(c, _):
            lanes = pl.ds(pl.multiple_of((h * half + c) * 128, 128), 128)
            to = pl.ds(pl.multiple_of(c * 128, 128), 128)
            r = resf[:, lanes]
            for phase in range(8):
                shifted = pad[phase : phase + rows + 24, lanes]
                for j in range(taps):
                    at = 16 + reach - j
                    if at % 8 == phase:
                        moved = shifted[at - phase : at - phase + rows]
                        sums[h, j : j + 1, to] = jnp.sum(r * moved, axis=0, keepdims=True)
            sums[h, taps : taps + 1, to] = gain[:, lanes]
            return 0

        lax.fori_loop(0, half, chunk, 0)


def out_kernel(place, left, own, right, taps, out, pad):
    fill_pad(pad, left, own, right, place[0])
    conv_rows(pad, taps, out, own.shape[0], False)


def pack_kernel(p0, p1, p2, p3, kv, qg):
    half, lanes = kv.shape[0], p0.shape[1]
    for s, p in enumerate((p0, p1, p2, p3)):
        kv[:, s * lanes : (s + 1) * lanes] = p[0:half]
        qg[:, s * lanes : (s + 1) * lanes] = p[half : 2 * half]


def to_rows(a):
    return a.astype(F32).T.astype(BF16)


def rows_kernel(*refs, hs):
    kv = refs[0:4]
    qg = refs[4:8]
    te = refs[8]
    out = refs[9:13]
    kn, vn, qgs, acc = refs[13:]
    span = kv[0].shape[1]
    for r in range(4):
        kn[r] = to_rows(kv[r][0:hs])
        vn[r] = to_rows(kv[r][hs : 2 * hs])
        qgs[r] = qg[r][...]

    def over_q(j, _):
        qt = qgs[j, 0:hs]
        gt = qgs[j, hs : 2 * hs]
        tot = jnp.zeros((8, span), F32)
        exp = jnp.zeros((8, span), F32)
        low = jnp.zeros((2 * hs, span), F32)
        high = jnp.zeros((hs, span), F32)
        for r in range(4):
            w = jnp.exp(dotf(kn[r], qt))
            wp = w * dotf(vn[r], gt)
            tot = tot + jnp.sum(w.reshape(span // 8, 8, span), axis=0)
            exp = exp + jnp.sum(wp.reshape(span // 8, 8, span), axis=0)
            low = low + dotf(kv[r][...], w.astype(BF16))
            high = high + dotf(kv[r][0:hs], wp.astype(BF16))
        tot = jnp.sum(tot, axis=0, keepdims=True)
        exp = jnp.sum(exp, axis=0, keepdims=True)
        te[j, 0:1] = tot
        te[j, 1:2] = exp
        acc[j, 0:hs] = low[hs : 2 * hs].astype(BF16)
        acc[j, hs : 2 * hs] = (high - (exp / tot) * low[0:hs]).astype(BF16)
        acc[j, 2 * hs : 3 * hs] = low[0:hs].astype(BF16)
        return 0

    lax.fori_loop(0, 4, over_q, 0)
    for r in range(4):
        out[r][...] = acc[r]


def cols_kernel(*refs, hs):
    te = refs[0:4]
    qg = refs[4:8]
    count = (len(refs) - 15) // 2
    kv = refs[8 : 8 + count]
    cols = refs[8 + count : 8 + 2 * count]
    kn, vn, qn, gn, inv, dlt, colacc = refs[8 + 2 * count :]
    span = kv[0].shape[1]
    for r in range(count):
        kn[r] = to_rows(kv[r][0:hs])
        vn[r] = to_rows(kv[r][hs : 2 * hs])
    for r in range(4):
        qn[r] = to_rows(qg[r][0:hs])
        gn[r] = to_rows(qg[r][hs : 2 * hs])
        t = (te[0][r] + te[1][r ^ 1]) + (te[2][r ^ 2] + te[3][r ^ 3])
        one = 1.0 / t[0:1]
        inv[r] = one
        dlt[r] = t[1:2] * one

    def over_k(b, _):
        k = kn[b]
        v = vn[b]
        gk = jnp.zeros((span, hs), F32)
        gv = jnp.zeros((span, hs), F32)
        for j in range(4):
            prob = jnp.exp(dotf(k, qg[j][0:hs])) * inv[j]
            slope = prob * (dotf(v, qg[j][hs : 2 * hs]) - dlt[j])
            gv = gv + dotf(prob.astype(BF16), gn[j])
            gk = gk + dotf(slope.astype(BF16), qn[j])
        colacc[b, 0:hs] = gk.T.astype(BF16)
        colacc[b, hs : 2 * hs] = gv.T.astype(BF16)
        return 0

    lax.fori_loop(0, count, over_k, 0)
    for r in range(count):
        cols[r][...] = colacc[r]


def run_rows(kv, qg, hs, span):
    nat = pltpu.VMEM((4, span, hs), BF16)
    return vcall(
        functools.partial(rows_kernel, hs=hs),
        (jax.ShapeDtypeStruct((4, 2, span), F32),) + (jax.ShapeDtypeStruct((3 * hs, span), BF16),) * 4,
        scratch=[nat, nat, pltpu.VMEM((4, 2 * hs, span), BF16), pltpu.VMEM((4, 3 * hs, span), BF16)],
        n_in=8,
    )(*kv, *qg)


def run_cols(te, kv, qg, hs, span):
    nat = pltpu.VMEM((4, span, hs), BF16)
    row = pltpu.VMEM((4, 1, span), F32)
    return vcall(
        functools.partial(cols_kernel, hs=hs),
        tuple(jax.ShapeDtypeStruct((2 * hs, span), BF16) for _ in kv),
        scratch=[nat, nat, nat, nat, row, row, pltpu.VMEM((4, 2 * hs, span), BF16)],
        n_in=8 + len(kv),
    )(*te, *qg, *kv)


def sum_kernel(*refs, hs):
    te = refs[0:4]
    row = refs[4:8]
    out = refs[12:16]
    each = [te[m][m] for m in range(4)]
    total = (each[0] + each[1]) + (each[2] + each[3])
    inv = 1.0 / total[0:1]
    delta = total[1:2] * inv
    att = jnp.zeros((hs, inv.shape[1]), F32)
    grad = jnp.zeros((hs, inv.shape[1]), F32)
    col = jnp.zeros((2 * hs, inv.shape[1]), F32)
    for m in range(4):
        att = att + row[m][0:hs].astype(F32)
        shift = each[m][1:2] / each[m][0:1] - delta
        grad = grad + (row[m][hs : 2 * hs].astype(F32) + shift * row[m][2 * hs : 3 * hs].astype(F32))
        col = col + refs[8 + m][...].astype(F32)
    att = (att * inv).astype(BF16)
    grad = (grad * inv).astype(BF16)
    col = col.astype(BF16)
    lanes = inv.shape[1] // 4
    for s in range(4):
        part = slice(s * lanes, (s + 1) * lanes)
        out[s][0:hs] = att[:, part]
        out[s][hs : 2 * hs] = grad[:, part]
        out[s][2 * hs : 4 * hs] = col[:, part]


def back_kernel(idx, sharp, b0, b1, b2, b3, qhat, khat, rad, wf, w, out, home, att, qgr, kgr, vgr, *, heads, hs):
    for s, b in enumerate((b0, b1, b2, b3)):
        home[lax.rem(idx[0] + s, 4)] = b[...]
    lanes = b0.shape[1]
    for h in range(heads):
        lo, hi = h * hs, (h + 1) * hs
        att[lo:hi] = home[h, 0:hs].astype(F32)
        gq = home[h, hs : 2 * hs].astype(F32) * (sharp[h] / math.sqrt(hs))
        gk = home[h, 2 * hs : 3 * hs].astype(F32)
        vgr[lo:hi] = home[h, 3 * hs : 4 * hs].astype(F32)
        qh = qhat[lo:hi]
        kh = khat[lo:hi]
        qgr[lo:hi] = (gq - qh * jnp.mean(gq * qh, axis=0, keepdims=True)) / rad[h : h + 1]
        kgr[lo:hi] = (gk - kh * jnp.mean(gk * kh, axis=0, keepdims=True)) / rad[heads + h : heads + h + 1]
    out[0:lanes] = dotf(att[...].T.astype(BF16), wf[...]).astype(BF16)
    normed = dotf(qgr[...].T.astype(BF16), w[0], 1, 1)
    normed = normed + dotf(kgr[...].T.astype(BF16), w[1], 1, 1)
    normed = normed + dotf(vgr[...].T.astype(BF16), w[2], 1, 1)
    out[lanes : 2 * lanes] = normed.astype(BF16)


def rims(cells, head, tail):
    left = lax.ppermute(tail, "tm", [(i, (i + 1) % TM) for i in range(TM)])
    right = lax.ppermute(head, "tm", [((i + 1) % TM, i) for i in range(TM)])
    return left, cells, right


def pieces(a, n):
    width = a.shape[1] // n
    return lambda i: lax.dynamic_slice_in_dim(a, i * width, width, axis=1)


def scatter_sum(a, batches):
    t = lax.axis_index("tm")
    z4, z2, x, yh = t // 16, (t // 8) % 2, (t // 2) % 4, t % 2
    if batches > 1:
        b = lax.axis_index("batch")
        away = lax.dynamic_index_in_dim(a, 1 - b, 0, keepdims=False)
        got = lax.ppermute(away, "batch", [(0, 1), (1, 0)])
        a = lax.dynamic_index_in_dim(a, b, 0, keepdims=False) + got
    else:
        a = jnp.concatenate([a[0], a[1]], axis=1)
    at = pieces(a, 4)
    got = ordered(lambda s: move_z4(at((z4 + s) % 4), s), (2, 1, 3))
    a = (at(z4) + got[0]) + (got[1] + got[2])
    at = pieces(a, 2)
    a = at(z2) + move_zy(at(1 - z2), 1)
    at = pieces(a, 4)
    got = ordered(lambda s: move_x(at((x + s) % 4), s), (2, 1, 3))
    a = (at(x) + got[0]) + (got[1] + got[2])
    at = pieces(a, 2)
    return at(yh) + move_zy(at(1 - yh), 2)


def step(input_signal, standardize_factor, triple_projection, score_sharpening, final_projection, filter_taps, mixture_adjoint, *, batches, mps):
    rows, width = input_signal.shape[1:]
    heads = score_sharpening.shape[0]
    hs = triple_projection.shape[2] // heads
    flat = heads * hs
    taps = filter_taps.shape[0]
    reach = taps // 2
    t = lax.axis_index("tm")
    z4 = (t // 16).astype(jnp.int32).reshape(1)
    place = t.astype(jnp.int32).reshape(1)
    x_in = input_signal[0]
    adj = mixture_adjoint[0]
    factor = standardize_factor[None]
    shape = jax.ShapeDtypeStruct
    adj_rims = rims(adj, adj[:reach], adj[rows - reach :])
    piece = shape((4 * hs, rows), BF16)
    pay, qhat, khat, rad = vcall(
        functools.partial(front_kernel, heads=heads, hs=hs),
        (shape((heads, 2 * hs, rows), BF16), shape((flat, rows), F32), shape((flat, rows), F32), shape((2 * heads, rows), F32)),
        scratch=[
            pltpu.VMEM((rows, width), BF16),
            pltpu.VMEM((3, width, flat), BF16),
            pltpu.SemaphoreType.DMA((4,)),
        ],
        n_in=1,
        raw=2,
    )(factor, x_in, triple_projection)
    pad = pltpu.VMEM((rows + 32, width), F32)
    *sent, grad_res = vcall(
        functools.partial(send_kernel, hs=hs),
        (piece,) * 4 + (shape((rows, width), F32),),
        scratch=[pad, pltpu.VMEM((4, 2 * hs, rows), BF16), pltpu.VMEM((rows, width), F32)],
        out_hbm=(4,),
        smem=3,
        n_in=7,
    )(z4, place, score_sharpening, *adj_rims, filter_taps, qhat, pay, final_projection)
    got = [sent[0]] + ordered(lambda s: move_z4(sent[s], s), (2, 1, 3))
    kv0, qg0 = vcall(pack_kernel, (shape((2 * hs, 4 * rows), BF16),) * 2, n_in=4)(*got)
    qg = [qg0] + ordered(lambda m: move_zy(qg0, m), (3, 2, 1))
    kv = [kv0] + ordered(lambda s: move_x(kv0, s), (2, 1, 3))
    span = 4 * rows
    te0, *rowp = run_rows(kv, qg, hs, span)
    te = [te0] + ordered(lambda m: move_zy(te0, m), (3, 2, 1))
    row = [rowp[0]] + ordered(lambda m: move_zy(rowp[m], m), (3, 2, 1))
    away = run_cols(te, kv[1:], qg, hs, span)
    back = ordered(lambda s: move_x(away[s - 1], -s), (2, 1, 3))
    col = list(run_cols(te, kv[:1], qg, hs, span)) + back
    home = vcall(
        functools.partial(sum_kernel, hs=hs),
        tuple(shape((4 * hs, rows), BF16) for _ in range(4)),
        n_in=12,
    )(*te, *row, *col)
    back = [home[0]] + ordered(lambda s: move_z4(home[s], -s), (2, 1, 3))
    part = vcall(
        functools.partial(back_kernel, heads=heads, hs=hs),
        shape((2 * rows, width), BF16),
        scratch=[pltpu.VMEM((4, 4 * hs, rows), BF16)] + [pltpu.VMEM((flat, rows), F32)] * 4,
        smem=2,
        n_in=9,
    )(z4, score_sharpening, *back, qhat, khat, rad, final_projection, triple_projection)
    other = lax.ppermute(part, "mp", [(0, 1), (1, 0)]) if mps > 1 else jnp.zeros_like(part)
    edge = shape((reach, width), BF16)
    residual, signal_adjoint, sums, first, last = vcall(
        functools.partial(tail_kernel, rows=rows, taps=taps),
        (shape((rows, width), BF16), shape((rows, width), BF16), shape((2, taps + 1, width // 2), F32), edge, edge),
        scratch=[
            pad,
            pltpu.VMEM((rows, width), F32),
            pltpu.VMEM((1, width), F32),
            pltpu.VMEM((rows, width), F32),
            pltpu.SemaphoreType.DMA(()),
        ],
        smem=1,
        n_in=7,
        raw=1,
        out_hbm=(1,),
    )(place, part, other, x_in, factor, *adj_rims, grad_res)
    res_rims = rims(residual, first, last)
    result = vcall(out_kernel, shape((rows, width), BF16), scratch=[pad], smem=1, n_in=4)(place, *res_rims, filter_taps)
    sums = scatter_sum(sums, batches)
    return (result[None], signal_adjoint[None], sums[:taps], sums[taps])


def solution(mesh):
    call = mapped(mesh)
    return call


def mapped(mesh):
    return jax.shard_map(
        functools.partial(step, batches=mesh.shape["batch"], mps=mesh.shape["mp"]),
        mesh=mesh,
        in_specs=(
            P("batch", "tm", None),
            P(),
            P(None, None, "mp"),
            P("mp"),
            P("mp", None),
            P(),
            P("batch", "tm", None),
        ),
        out_specs=(
            P("batch", "tm", None),
            P("batch", "tm", None),
            P(None, ("batch", "tm")),
            P(("batch", "tm")),
        ),
        check_vma=False,
    )
```

```python
import functools
import math

import jax
import jax.numpy as jnp
from jax import lax
from jax.experimental import pallas as pl
from jax.experimental.pallas import tpu as pltpu
from jax.sharding import PartitionSpec as P


INTERPRET = False
LIMIT = 24 * 1024 * 1024
TM = 64
F32 = jnp.float32
BF16 = jnp.bfloat16


def _split(t):
    return t // 16, (t // 8) % 2, (t // 2) % 4, t % 2


def _join(z4, z2, x, yh):
    return ((z4 % 4) * 2 + z2) * 8 + (x % 4) * 2 + yh


def move_z4(a, s):
    pairs = []
    for t in range(TM):
        z4, z2, x, yh = _split(t)
        pairs.append((t, _join(z4 + s, z2, x, yh)))
    return lax.ppermute(a, "tm", pairs)


def move_x(a, s):
    pairs = []
    for t in range(TM):
        z4, z2, x, yh = _split(t)
        pairs.append((t, _join(z4, z2, x + s, yh)))
    return lax.ppermute(a, "tm", pairs)


def move_zy(a, m):
    pairs = []
    for t in range(TM):
        z4, z2, x, yh = _split(t)
        pairs.append((t, _join(z4, z2 ^ (m & 1), x, yh ^ (m >> 1))))
    return lax.ppermute(a, "tm", pairs)


def ordered(move, shifts):
    got = {s: move(s) for s in shifts}
    return [got[s] for s in (1, 2, 3)]


def vcall(kernel, out_shape, scratch=(), smem=0, n_in=0, raw=0, out_hbm=(), out_raw=()):
    space = [pl.BlockSpec(memory_space=pltpu.SMEM)] * smem
    space += [pl.BlockSpec(memory_space=pltpu.VMEM)] * n_in
    space += [pl.BlockSpec(memory_space=pltpu.HBM if not INTERPRET else pl.ANY)] * raw
    flat, tree = jax.tree.flatten(out_shape)
    held = flat
    if not INTERPRET:
        held = [o if i in out_hbm else (pltpu.HBM if i in out_raw else pltpu.VMEM)(o.shape, o.dtype) for i, o in enumerate(flat)]
    call = pl.pallas_call(
        kernel,
        out_shape=jax.tree.unflatten(tree, held),
        in_specs=space,
        out_specs=jax.tree.unflatten(
            tree,
            [
                pl.BlockSpec(memory_space=pltpu.VMEM if i not in out_raw else pl.ANY if INTERPRET else pltpu.HBM)
                for i in range(len(flat))
            ],
        ),
        scratch_shapes=list(scratch),
        compiler_params=pltpu.CompilerParams(vmem_limit_bytes=LIMIT),
        interpret=INTERPRET,
    )

    def run(*args):
        if not INTERPRET:
            args = [
                a if i < smem else pltpu.with_memory_space_constraint(a, pltpu.VMEM if i < smem + n_in else pltpu.HBM)
                for i, a in enumerate(args)
            ]
        return call(*args)

    return run


def dotf(a, b, ca=1, cb=0):
    if INTERPRET:
        a, b = a.astype(F32), b.astype(F32)
    return lax.dot_general(a, b, (((ca,), (cb,)), ((), ())), preferred_element_type=F32)


def one_row(a):
    return jnp.concatenate([a[i : i + 1] for i in range(a.shape[0])], axis=1)


def front_kernel(
    factor_hbm, x_hbm, w_hbm, pay, qhat_o, khat_o, rad_o, factor, x, w, sem, *, heads, hs
):
    x_copy = pltpu.make_async_copy(x_hbm, x, sem.at[0])
    x_copy.start()
    f_copy = pltpu.make_async_copy(factor_hbm, factor, sem.at[4])
    f_copy.start()
    copies = [pltpu.make_async_copy(w_hbm.at[i], w.at[i], sem.at[1 + i]) for i in range(3)]
    for i in (1, 2, 0):
        copies[i].start()
    x_copy.wait()
    f_copy.wait()
    xf = x[...].astype(F32)
    centred = xf - jnp.mean(xf, axis=-1, keepdims=True)
    var = jnp.mean(centred * centred, axis=-1, keepdims=True)
    unit = centred * (1.0 / jnp.sqrt(var + 1e-05))
    normed = (unit * one_row(factor)).astype(BF16)
    copies[1].wait()
    kt = dotf(normed, w[1]).T
    copies[2].wait()
    vt = dotf(normed, w[2]).T
    copies[0].wait()
    qt = dotf(normed, w[0]).T
    for h in range(heads):
        lo, hi = h * hs, (h + 1) * hs
        q = qt[lo:hi]
        k = kt[lo:hi]
        qr = jnp.sqrt(jnp.mean(q * q, axis=0, keepdims=True) + 1e-06)
        kr = jnp.sqrt(jnp.mean(k * k, axis=0, keepdims=True) + 1e-06)
        qh = q / qr
        kh = k / kr
        qhat_o[lo:hi] = qh
        khat_o[lo:hi] = kh
        rad_o[h : h + 1] = qr
        rad_o[heads + h : heads + h + 1] = kr
        pay[h, 0:hs] = kh.astype(BF16)
        pay[h, hs : 2 * hs] = vt[lo:hi].astype(BF16)


def fill_pad(pad, left, own, right, place):
    reach = left.shape[0]
    rows = own.shape[0]
    pad[16 - reach : 16] = jnp.where(place > 0, left[...].astype(F32), 0.0)
    pad[16 : 16 + rows] = own[...].astype(F32)
    pad[16 + rows : 16 + rows + reach] = jnp.where(place < TM - 1, right[...].astype(F32), 0.0)


def conv_rows(pad, taps, out, rows, flip):
    count = taps.shape[0]
    reach = count // 2

    def chunk(c, _):
        lanes = pl.ds(pl.multiple_of(c * 128, 128), 128)
        acc = pad[16 : 16 + rows, lanes]
        for phase in range(8):
            shifted = pad[phase : phase + rows + 24, lanes]
            for j in range(count):
                at = 16 + reach - j if flip else 16 - reach + j
                if at % 8 == phase:
                    acc = acc + taps[j : j + 1, lanes] * shifted[at - phase : at - phase + rows]
        out[:, lanes] = acc.astype(out.dtype)
        return 0

    lax.fori_loop(0, out.shape[1] // 128, chunk, 0)


def send_kernel(idx, place, sharp, left, own, right, taps, qhat, pay, wf, o0, o1, o2, o3, gres_o, pad, g_s, gres, sem, *, hs):
    fill_pad(pad, left, own, right, place[0])
    conv_rows(pad, taps, gres, own.shape[0], True)
    out = pltpu.make_async_copy(gres, gres_o, sem)
    out.start()
    gt = dotf(wf[...], gres[...].astype(BF16), 1, 1).astype(BF16)
    for h in range(4):
        g_s[h, 0:hs] = (qhat[h * hs : (h + 1) * hs] * (sharp[h] / math.sqrt(hs))).astype(BF16)
        g_s[h, hs : 2 * hs] = gt[h * hs : (h + 1) * hs]
    for s, o in enumerate((o0, o1, o2, o3)):
        at = lax.rem(idx[0] + s, 4)
        o[0 : 2 * hs] = pay[at]
        o[2 * hs : 4 * hs] = g_s[at]
    out.wait()


def tail_kernel(
    place, part, other, x, factor, left, own, right, gres_hbm, res_o, sig_o, sums, first, last, pad, resf, gain, gres, sem,
    *, rows, taps,
):
    fetch = pltpu.make_async_copy(gres_hbm, gres, sem)
    fetch.start()
    fill_pad(pad, left, own, right, place[0])
    reach = taps // 2
    total = part[0:rows].astype(F32) + other[0:rows].astype(F32)
    xf = x[...].astype(F32)
    residual = (xf + total).astype(BF16)
    res_o[...] = residual
    first[...] = residual[:reach]
    last[...] = residual[rows - reach :]
    resf[...] = residual.astype(F32)
    centred = xf - jnp.mean(xf, axis=-1, keepdims=True)
    var = jnp.mean(centred * centred, axis=-1, keepdims=True)
    inv = 1.0 / jnp.sqrt(var + 1e-05)
    unit = centred * inv
    grad = part[rows : 2 * rows].astype(F32) + other[rows : 2 * rows].astype(F32)
    prod = grad * unit
    gain[...] = jnp.sum(prod, axis=0, keepdims=True)
    f = one_row(factor)
    scaled = grad * f
    m1 = jnp.mean(scaled, axis=-1, keepdims=True)
    m2 = jnp.mean(prod * f, axis=-1, keepdims=True)
    fetch.wait()
    sig_o[...] = (gres[...] + (scaled - m1 - unit * m2) * inv).astype(BF16)
    half = sums.shape[2] // 128

    for h in range(2):

        def chunk(c, _):
            lanes = pl.ds(pl.multiple_of((h * half + c) * 128, 128), 128)
            to = pl.ds(pl.multiple_of(c * 128, 128), 128)
            r = resf[:, lanes]
            for phase in range(8):
                shifted = pad[phase : phase + rows + 24, lanes]
                for j in range(taps):
                    at = 16 + reach - j
                    if at % 8 == phase:
                        moved = shifted[at - phase : at - phase + rows]
                        sums[h, j : j + 1, to] = jnp.sum(r * moved, axis=0, keepdims=True)
            sums[h, taps : taps + 1, to] = gain[:, lanes]
            return 0

        lax.fori_loop(0, half, chunk, 0)


def out_kernel(place, left, own, right, taps, out, pad):
    fill_pad(pad, left, own, right, place[0])
    conv_rows(pad, taps, out, own.shape[0], False)


def pack_kernel(p0, p1, p2, p3, kv, qg):
    half, lanes = kv.shape[0], p0.shape[1]
    for s, p in enumerate((p0, p1, p2, p3)):
        kv[:, s * lanes : (s + 1) * lanes] = p[0:half]
        qg[:, s * lanes : (s + 1) * lanes] = p[half : 2 * half]


def to_rows(a):
    return a.astype(F32).T.astype(BF16)


def rows_kernel(*refs, hs):
    kv = refs[0:4]
    qg = refs[4:8]
    te = refs[8]
    out = refs[9:13]
    kn, vn, qgs, acc = refs[13:]
    span = kv[0].shape[1]
    for r in range(4):
        kn[r] = to_rows(kv[r][0:hs])
        vn[r] = to_rows(kv[r][hs : 2 * hs])
        qgs[r] = qg[r][...]

    def over_q(j, _):
        qt = qgs[j, 0:hs]
        gt = qgs[j, hs : 2 * hs]
        tot = jnp.zeros((8, span), F32)
        exp = jnp.zeros((8, span), F32)
        low = jnp.zeros((2 * hs, span), F32)
        high = jnp.zeros((hs, span), F32)
        for r in range(4):
            w = jnp.exp(dotf(kn[r], qt))
            wp = w * dotf(vn[r], gt)
            tot = tot + jnp.sum(w.reshape(span // 8, 8, span), axis=0)
            exp = exp + jnp.sum(wp.reshape(span // 8, 8, span), axis=0)
            low = low + dotf(kv[r][...], w.astype(BF16))
            high = high + dotf(kv[r][0:hs], wp.astype(BF16))
        tot = jnp.sum(tot, axis=0, keepdims=True)
        exp = jnp.sum(exp, axis=0, keepdims=True)
        te[j, 0:1] = tot
        te[j, 1:2] = exp
        acc[j, 0:hs] = low[hs : 2 * hs].astype(BF16)
        acc[j, hs : 2 * hs] = (high - (exp / tot) * low[0:hs]).astype(BF16)
        acc[j, 2 * hs : 3 * hs] = low[0:hs].astype(BF16)
        return 0

    lax.fori_loop(0, 4, over_q, 0)
    for r in range(4):
        out[r][...] = acc[r]


def cols_kernel(*refs, hs):
    te = refs[0:4]
    kv = refs[4:8]
    qg = refs[8:12]
    cols = refs[12:16]
    kn, vn, qn, gn, inv, dlt, colacc = refs[16:]
    span = kv[0].shape[1]
    for r in range(4):
        kn[r] = to_rows(kv[r][0:hs])
        vn[r] = to_rows(kv[r][hs : 2 * hs])
        qn[r] = to_rows(qg[r][0:hs])
        gn[r] = to_rows(qg[r][hs : 2 * hs])
        t = (te[0][r] + te[1][r ^ 1]) + (te[2][r ^ 2] + te[3][r ^ 3])
        one = 1.0 / t[0:1]
        inv[r] = one
        dlt[r] = t[1:2] * one

    def over_k(b, _):
        k = kn[b]
        v = vn[b]
        gk = jnp.zeros((span, hs), F32)
        gv = jnp.zeros((span, hs), F32)
        for j in range(4):
            prob = jnp.exp(dotf(k, qg[j][0:hs])) * inv[j]
            slope = prob * (dotf(v, qg[j][hs : 2 * hs]) - dlt[j])
            gv = gv + dotf(prob.astype(BF16), gn[j])
            gk = gk + dotf(slope.astype(BF16), qn[j])
        colacc[b, 0:hs] = gk.T.astype(BF16)
        colacc[b, hs : 2 * hs] = gv.T.astype(BF16)
        return 0

    lax.fori_loop(0, 4, over_k, 0)
    for r in range(4):
        cols[r][...] = colacc[r]


def run_rows(kv, qg, hs, span):
    nat = pltpu.VMEM((4, span, hs), BF16)
    return vcall(
        functools.partial(rows_kernel, hs=hs),
        (jax.ShapeDtypeStruct((4, 2, span), F32),) + (jax.ShapeDtypeStruct((3 * hs, span), BF16),) * 4,
        scratch=[nat, nat, pltpu.VMEM((4, 2 * hs, span), BF16), pltpu.VMEM((4, 3 * hs, span), BF16)],
        n_in=8,
    )(*kv, *qg)


def run_cols(te, kv, qg, hs, span):
    nat = pltpu.VMEM((4, span, hs), BF16)
    row = pltpu.VMEM((4, 1, span), F32)
    return vcall(
        functools.partial(cols_kernel, hs=hs),
        tuple(jax.ShapeDtypeStruct((2 * hs, span), BF16) for _ in range(4)),
        scratch=[nat, nat, nat, nat, row, row, pltpu.VMEM((4, 2 * hs, span), BF16)],
        n_in=12,
    )(*te, *kv, *qg)


def sum_kernel(*refs, hs):
    te = refs[0:4]
    row = refs[4:8]
    out = refs[12:16]
    each = [te[m][m] for m in range(4)]
    total = (each[0] + each[1]) + (each[2] + each[3])
    inv = 1.0 / total[0:1]
    delta = total[1:2] * inv
    att = jnp.zeros((hs, inv.shape[1]), F32)
    grad = jnp.zeros((hs, inv.shape[1]), F32)
    col = jnp.zeros((2 * hs, inv.shape[1]), F32)
    for m in range(4):
        att = att + row[m][0:hs].astype(F32)
        shift = each[m][1:2] / each[m][0:1] - delta
        grad = grad + (row[m][hs : 2 * hs].astype(F32) + shift * row[m][2 * hs : 3 * hs].astype(F32))
        col = col + refs[8 + m][...].astype(F32)
    att = (att * inv).astype(BF16)
    grad = (grad * inv).astype(BF16)
    col = col.astype(BF16)
    lanes = inv.shape[1] // 4
    for s in range(4):
        part = slice(s * lanes, (s + 1) * lanes)
        out[s][0:hs] = att[:, part]
        out[s][hs : 2 * hs] = grad[:, part]
        out[s][2 * hs : 4 * hs] = col[:, part]


def back_kernel(idx, sharp, b0, b1, b2, b3, qhat, khat, rad, wf, w, out, home, att, qgr, kgr, vgr, *, heads, hs):
    for s, b in enumerate((b0, b1, b2, b3)):
        home[lax.rem(idx[0] + s, 4)] = b[...]
    lanes = b0.shape[1]
    for h in range(heads):
        lo, hi = h * hs, (h + 1) * hs
        att[lo:hi] = home[h, 0:hs].astype(F32)
        gq = home[h, hs : 2 * hs].astype(F32) * (sharp[h] / math.sqrt(hs))
        gk = home[h, 2 * hs : 3 * hs].astype(F32)
        vgr[lo:hi] = home[h, 3 * hs : 4 * hs].astype(F32)
        qh = qhat[lo:hi]
        kh = khat[lo:hi]
        qgr[lo:hi] = (gq - qh * jnp.mean(gq * qh, axis=0, keepdims=True)) / rad[h : h + 1]
        kgr[lo:hi] = (gk - kh * jnp.mean(gk * kh, axis=0, keepdims=True)) / rad[heads + h : heads + h + 1]
    out[0:lanes] = dotf(att[...].T.astype(BF16), wf[...]).astype(BF16)
    normed = dotf(qgr[...].T.astype(BF16), w[0], 1, 1)
    normed = normed + dotf(kgr[...].T.astype(BF16), w[1], 1, 1)
    normed = normed + dotf(vgr[...].T.astype(BF16), w[2], 1, 1)
    out[lanes : 2 * lanes] = normed.astype(BF16)


def rims(cells, head, tail):
    left = lax.ppermute(tail, "tm", [(i, (i + 1) % TM) for i in range(TM)])
    right = lax.ppermute(head, "tm", [((i + 1) % TM, i) for i in range(TM)])
    return left, cells, right


def pieces(a, n):
    width = a.shape[1] // n
    return lambda i: lax.dynamic_slice_in_dim(a, i * width, width, axis=1)


def scatter_sum(a, batches):
    t = lax.axis_index("tm")
    z4, z2, x, yh = t // 16, (t // 8) % 2, (t // 2) % 4, t % 2
    if batches > 1:
        b = lax.axis_index("batch")
        away = lax.dynamic_index_in_dim(a, 1 - b, 0, keepdims=False)
        got = lax.ppermute(away, "batch", [(0, 1), (1, 0)])
        a = lax.dynamic_index_in_dim(a, b, 0, keepdims=False) + got
    else:
        a = jnp.concatenate([a[0], a[1]], axis=1)
    at = pieces(a, 4)
    got = ordered(lambda s: move_z4(at((z4 + s) % 4), s), (2, 1, 3))
    a = (at(z4) + got[0]) + (got[1] + got[2])
    at = pieces(a, 2)
    a = at(z2) + move_zy(at(1 - z2), 1)
    at = pieces(a, 4)
    got = ordered(lambda s: move_x(at((x + s) % 4), s), (2, 1, 3))
    a = (at(x) + got[0]) + (got[1] + got[2])
    at = pieces(a, 2)
    return at(yh) + move_zy(at(1 - yh), 2)


def step(input_signal, standardize_factor, triple_projection, score_sharpening, final_projection, filter_taps, mixture_adjoint, *, batches, mps):
    rows, width = input_signal.shape[1:]
    heads = score_sharpening.shape[0]
    hs = triple_projection.shape[2] // heads
    flat = heads * hs
    taps = filter_taps.shape[0]
    reach = taps // 2
    t = lax.axis_index("tm")
    z4 = (t // 16).astype(jnp.int32).reshape(1)
    place = t.astype(jnp.int32).reshape(1)
    x_in = input_signal[0]
    adj = mixture_adjoint[0]
    factor = standardize_factor.reshape(-1, 128)
    shape = jax.ShapeDtypeStruct
    adj_rims = rims(adj, adj[:reach], adj[rows - reach :])
    piece = shape((4 * hs, rows), BF16)
    pay, qhat, khat, rad = vcall(
        functools.partial(front_kernel, heads=heads, hs=hs),
        (shape((heads, 2 * hs, rows), BF16), shape((flat, rows), F32), shape((flat, rows), F32), shape((2 * heads, rows), F32)),
        scratch=[
            pltpu.VMEM(factor.shape, F32),
            pltpu.VMEM((rows, width), BF16),
            pltpu.VMEM((3, width, flat), BF16),
            pltpu.SemaphoreType.DMA((5,)),
        ],
        raw=3,
    )(factor, x_in, triple_projection)
    pad = pltpu.VMEM((rows + 32, width), F32)
    *sent, grad_res = vcall(
        functools.partial(send_kernel, hs=hs),
        (piece,) * 4 + (shape((rows, width), F32),),
        scratch=[pad, pltpu.VMEM((4, 2 * hs, rows), BF16), pltpu.VMEM((rows, width), F32), pltpu.SemaphoreType.DMA(())],
        out_raw=(4,),
        smem=3,
        n_in=7,
    )(z4, place, score_sharpening, *adj_rims, filter_taps, qhat, pay, final_projection)
    got = [sent[0]] + ordered(lambda s: move_z4(sent[s], s), (2, 1, 3))
    kv0, qg0 = vcall(pack_kernel, (shape((2 * hs, 4 * rows), BF16),) * 2, n_in=4)(*got)
    qg = [qg0] + ordered(lambda m: move_zy(qg0, m), (3, 2, 1))
    kv = [kv0] + ordered(lambda s: move_x(kv0, s), (2, 1, 3))
    span = 4 * rows
    te0, *rowp = run_rows(kv, qg, hs, span)
    te = [te0] + ordered(lambda m: move_zy(te0, m), (3, 2, 1))
    row = [rowp[0]] + ordered(lambda m: move_zy(rowp[m], m), (3, 2, 1))
    colp = run_cols(te, kv, qg, hs, span)
    col = [colp[0]] + ordered(lambda s: move_x(colp[s], -s), (2, 1, 3))
    home = vcall(
        functools.partial(sum_kernel, hs=hs),
        tuple(shape((4 * hs, rows), BF16) for _ in range(4)),
        n_in=12,
    )(*te, *row, *col)
    back = [home[0]] + ordered(lambda s: move_z4(home[s], -s), (2, 1, 3))
    part = vcall(
        functools.partial(back_kernel, heads=heads, hs=hs),
        shape((2 * rows, width), BF16),
        scratch=[pltpu.VMEM((4, 4 * hs, rows), BF16)] + [pltpu.VMEM((flat, rows), F32)] * 4,
        smem=2,
        n_in=9,
    )(z4, score_sharpening, *back, qhat, khat, rad, final_projection, triple_projection)
    other = lax.ppermute(part, "mp", [(0, 1), (1, 0)]) if mps > 1 else jnp.zeros_like(part)
    edge = shape((reach, width), BF16)
    residual, signal_adjoint, sums, first, last = vcall(
        functools.partial(tail_kernel, rows=rows, taps=taps),
        (shape((rows, width), BF16), shape((rows, width), BF16), shape((2, taps + 1, width // 2), F32), edge, edge),
        scratch=[
            pad,
            pltpu.VMEM((rows, width), F32),
            pltpu.VMEM((1, width), F32),
            pltpu.VMEM((rows, width), F32),
            pltpu.SemaphoreType.DMA(()),
        ],
        smem=1,
        n_in=7,
        raw=1,
        out_hbm=(1,),
    )(place, part, other, x_in, factor, *adj_rims, grad_res)
    res_rims = rims(residual, first, last)
    result = vcall(out_kernel, shape((rows, width), BF16), scratch=[pad], smem=1, n_in=4)(place, *res_rims, filter_taps)
    sums = scatter_sum(sums, batches)
    return (result[None], signal_adjoint[None], sums[:taps], sums[taps])


def solution(mesh):
    call = mapped(mesh)
    return call


def mapped(mesh):
    return jax.shard_map(
        functools.partial(step, batches=mesh.shape["batch"], mps=mesh.shape["mp"]),
        mesh=mesh,
        in_specs=(
            P("batch", "tm", None),
            P(),
            P(None, None, "mp"),
            P("mp"),
            P("mp", None),
            P(),
            P("batch", "tm", None),
        ),
        out_specs=(
            P("batch", "tm", None),
            P("batch", "tm", None),
            P(None, ("batch", "tm")),
            P(("batch", "tm")),
        ),
        check_vma=False,
    )
```
